32 devices in a mesh: dp: 8 (over z, x), tensor: 4 (over y, core).
Axes of the slice: x: 2, y: 2, z: 4, core: 2. Of those that a mesh axis runs over, the one named last changes fastest.
Arguments:
- frames: bfloat16 [16, 800, 768], P('dp', 'tensor'), may hold values from -6 to 6
- cotangent: float32 [16, 800, 768], P('dp', 'tensor'), may hold values from -6 to 6
- lengths: int32 [16], P('dp'), may hold values from 100 to 780
- query_weight: bfloat16 [768, 768], P(None, 'tensor'), may hold values from -0.21875 to 0.21875
- query_bias: float32 [768], P('tensor'), may hold values from -3 to 3
- key_weight: bfloat16 [768, 768], P(None, 'tensor'), may hold values from -0.21875 to 0.21875
- value_weight: bfloat16 [768, 768], P(None, 'tensor'), may hold values from -0.21875 to 0.21875
- value_bias: float32 [768], P('tensor'), may hold values from -3 to 3
- out_weight: bfloat16 [768, 768], P('tensor'), may hold values from -1.75 to 1.75
- out_bias: float32 [768], replicated, may hold values from -3 to 3
- first_gain: float32 [768], replicated, may hold values from 0.5 to 1.5
- first_shift: float32 [768], replicated, may hold values from -3 to 3
- up_weight: bfloat16 [768, 3072], P(None, 'tensor'), may hold values from -0.21875 to 0.21875
- up_bias: float32 [3072], P('tensor'), may hold values from -3 to 3
- down_weight: bfloat16 [3072, 768], P('tensor'), may hold values from -0.109375 to 0.109375
- down_bias: float32 [768], replicated, may hold values from -3 to 3
- second_gain: float32 [768], replicated, may hold values from 0.5 to 1.5
- second_shift: float32 [768], replicated, may hold values from -3 to 3
Outputs:
- layer_output: bfloat16 [16, 800, 768], P('dp', 'tensor')
- input_gradient: float32 [16, 800, 768], P('dp', 'tensor')
- query_weight_gradient: float32 [768, 768], P(None, 'tensor')
- query_bias_gradient: float32 [768], P('tensor')
- key_weight_gradient: float32 [768, 768], P(None, 'tensor')
- value_weight_gradient: float32 [768, 768], P(None, 'tensor')
- value_bias_gradient: float32 [768], P('tensor')
- out_weight_gradient: float32 [768, 768], P('tensor')
- out_bias_gradient: float32 [768], replicated
- first_gain_gradient: float32 [768], replicated
- first_shift_gradient: float32 [768], replicated
- up_weight_gradient: float32 [768, 3072], P(None, 'tensor')
- up_bias_gradient: float32 [3072], P('tensor')
- down_weight_gradient: float32 [3072, 768], P('tensor')
- down_bias_gradient: float32 [768], replicated
- second_gain_gradient: float32 [768], replicated
- second_shift_gradient: float32 [768], replicated
The draws below stay inside these ranges and needn't reach their ends.
All inputs are finite; a program needn't handle non-finite values.
Results may differ from the reference program's by a relative error of at most 0.019.
Values may be sent and summed in bfloat16 or wider, within the bound.
A program may use at most 192 MiB of HBM per device.

```python
import jax
import jax.numpy as jnp
from jax import lax

D = 768
HEADS = 12
HEAD_DIM = 64
FF = 3072
LEN = 800
SEQS = 16


def with_ends(drawn, stream_key, low, high):
    shape = drawn.shape
    spot = [jax.random.randint(jax.random.fold_in(stream_key, axis), (), 0, shape[axis]) for axis in range(len(shape))]
    drawn = drawn.at[tuple(spot)].set(low)
    longest = shape.index(max(shape))
    spot[longest] = (spot[longest] + 1) % shape[longest]
    return drawn.at[tuple(spot)].set(high)


def level_of(stream_key, shape, shards, least, largest):
    level, own = 1.0, jax.random.fold_in(stream_key, 6)
    for position, blocks in shards:
        steps = jnp.exp(jax.random.uniform(jax.random.fold_in(own, position), (blocks,), jnp.float32, least / len(shards), largest / len(shards)))
        level = level * jnp.repeat(steps, shape[position] // blocks).reshape([-1 if axis == position else 1 for axis in range(len(shape))])
    return level


def gaussian(own_key, dims, deviation, bound, pieces=(), dtype=jnp.bfloat16):
    entries = deviation * jax.random.normal(own_key, dims, jnp.float32)
    if pieces:
        entries = entries * level_of(own_key, dims, pieces, -0.22, 0.18)
    return jnp.clip(entries, -bound, bound).astype(dtype)


def setup_inputs(seed: int = 0) -> dict:
    keys = jax.random.split(jax.random.key(seed), 19)
    return {
        "frames": gaussian(keys[0], (SEQS, LEN, D), 1.0, 6.0, ((0, 8), (1, 4))),
        "cotangent": gaussian(keys[1], (SEQS, LEN, D), 1.0, 6.0, ((0, 8), (1, 4)), jnp.float32),
        "lengths": with_ends(jax.random.randint(keys[2], (SEQS,), LEN // 8, LEN - LEN // 40 + 1), jax.random.fold_in(keys[2], 1), LEN // 8, (LEN - LEN // 40 + 1) - 1).astype(jnp.int32),
        "query_weight": gaussian(keys[3], (D, D), D ** -0.5, 0.21875, ((1, 4),)),
        "query_bias": gaussian(keys[4], (D,), 0.5, 3.0, ((0, 4),), jnp.float32),
        "key_weight": gaussian(keys[5], (D, D), D ** -0.5, 0.21875, ((1, 4),)),
        "value_weight": gaussian(keys[6], (D, D), D ** -0.5, 0.21875, ((1, 4),)),
        "value_bias": gaussian(keys[7], (D,), 0.5, 3.0, ((0, 4),), jnp.float32),
        "out_weight": gaussian(keys[8], (D, D), (D // 64) ** -0.5, 1.75, ((0, 4),)),
        "out_bias": gaussian(keys[9], (D,), 0.5, 3.0, (), jnp.float32),
        "first_gain": jnp.clip(1.0 + 0.1 * jax.random.normal(keys[10], (D,), jnp.float32), 0.5, 1.5),
        "first_shift": gaussian(keys[11], (D,), 0.5, 3.0, (), jnp.float32),
        "up_weight": gaussian(keys[12], (D, FF), D ** -0.5, 0.21875, ((1, 4),)),
        "up_bias": gaussian(keys[13], (FF,), 0.5, 3.0, ((0, 4),), jnp.float32),
        "down_weight": gaussian(keys[14], (FF, D), FF ** -0.5, 0.109375, ((0, 4),)),
        "down_bias": gaussian(keys[15], (D,), 0.5, 3.0, (), jnp.float32),
        "second_gain": jnp.clip(1.0 + 0.1 * jax.random.normal(keys[16], (D,), jnp.float32), 0.5, 1.5),
        "second_shift": gaussian(keys[17], (D,), 0.5, 3.0, (), jnp.float32),
    }


@jax.custom_vjp
def low(v):
    return lax.optimization_barrier(v.astype(jnp.bfloat16)).astype(jnp.float32)

@jax.custom_vjp
def low_back(v):
    return v

def low_keep(v):
    return (low(v), None)

def low_pass(kept, grad):
    return (grad,)

def back_keep(v):
    return (v, None)

def back_low(kept, grad):
    return (low(grad),)
low.defvjp(low_keep, low_pass)
low_back.defvjp(back_keep, back_low)
EPSILON = 1e-05
HIGH = lax.Precision.HIGHEST

def matmul(left, right):
    return jnp.dot(left, right, precision=HIGH, preferred_element_type=jnp.float32)

def layer_norm(rows, gain, shift):
    centred = rows - lax.optimization_barrier(jnp.mean(rows, axis=-1, keepdims=True))
    spread = lax.optimization_barrier(jnp.mean(centred * centred, axis=-1, keepdims=True))
    return centred * lax.rsqrt(spread + EPSILON) * gain + shift

def layer_forward(params, frames, key_count):
    query_weight, query_bias, key_weight, value_weight, value_bias, out_weight, out_bias, first_gain, first_shift, up_weight, up_bias, down_weight, down_bias, second_gain, second_shift = params
    factor = HEAD_DIM ** (-0.5)
    queries = low(low_back(matmul(frames, query_weight) + query_bias)).reshape(LEN, HEADS, HEAD_DIM)
    key_rows = low(low_back(matmul(frames, key_weight))).reshape(LEN, HEADS, HEAD_DIM)
    values = low(low_back(matmul(frames, value_weight) + value_bias)).reshape(LEN, HEADS, HEAD_DIM)
    scores = low_back(jnp.einsum('qhd,khd->hqk', queries, key_rows, precision=HIGH) * factor)
    key_mask = jnp.arange(LEN) < key_count
    scores = jnp.where(key_mask[None, None, :], scores, -1e+30)
    attention = low(jax.nn.softmax(scores, axis=-1))
    context = low(low_back(jnp.einsum('hqk,khd->qhd', attention, values, precision=HIGH))).reshape(LEN, D)
    attended = low_back(matmul(context, out_weight)) + out_bias
    first = layer_norm(frames + attended, first_gain, first_shift)
    hidden = low_back(matmul(low(first), up_weight) + up_bias)
    activated = low(jax.nn.gelu(hidden, approximate=False))
    second = first + low_back(matmul(activated, down_weight)) + down_bias
    return layer_norm(second, second_gain, second_shift)

def reference(frames, cotangent, lengths, query_weight, query_bias, key_weight, value_weight, value_bias, out_weight, out_bias, first_gain, first_shift, up_weight, up_bias, down_weight, down_bias, second_gain, second_shift):
    params = tuple((item.astype(jnp.float32) for item in (query_weight, query_bias, key_weight, value_weight, value_bias, out_weight, out_bias, first_gain, first_shift, up_weight, up_bias, down_weight, down_bias, second_gain, second_shift)))

    def one_utterance(running, item):
        seq_frames, seq_cotangent, key_count = item
        live = (jnp.arange(LEN) < key_count).astype(jnp.float32)[:, None]

        def forward_only(weights, inputs):
            return layer_forward(weights, inputs, key_count)
        output, pullback = jax.vjp(forward_only, params, seq_frames)
        param_grads, frame_grad = pullback(seq_cotangent * live)
        running = tuple((left + right for left, right in zip(running, param_grads)))
        return (running, (output.astype(jnp.bfloat16), frame_grad))
    zeros = tuple((jnp.zeros_like(item) for item in params))
    totals, (outputs, frame_grads) = lax.scan(one_utterance, zeros, (frames.astype(jnp.float32), cotangent.astype(jnp.float32), lengths))
    return (outputs, frame_grads, totals[0], totals[1], totals[2], totals[3], totals[4], totals[5], totals[6], totals[7], totals[8], totals[9], totals[10], totals[11], totals[12], totals[13], totals[14])
```

```python
import functools

import jax
import jax.numpy as jnp
from jax import lax
from jax.experimental import pallas as pl
from jax.experimental.pallas import tpu as pltpu
from jax.sharding import PartitionSpec as P

MESH = pl.DeviceIdType.MESH


def ring_place(index, count):
    return jnp.where(index % 2 == 0, index // 2, count - 1 - index // 2)


def ring_index(place, count):
    return jnp.where(place < count // 2, 2 * place, 2 * (count - 1 - place) + 1)


def grad_ring(count, parts, *refs):
    own = refs[:parts]
    full = refs[parts : 2 * parts]
    first = refs[2 * parts : 3 * parts]
    landed = refs[3 * parts : 4 * parts]
    add_send, add_recv, share_send, share_recv, out_sem = refs[4 * parts : 4 * parts + 5]
    shared = refs[4 * parts + 5 :]
    tensor = lax.axis_index("tensor")
    place = ring_place(lax.axis_index("dp"), count)
    right = ring_index((place + 1) % count, count)
    left = ring_index((place + count - 1) % count, count)
    barrier = pltpu.get_barrier_semaphore()
    for peer in (left, right):
        pl.semaphore_signal(barrier, inc=1, device_id=(peer, tensor), device_id_type=MESH)
    pl.semaphore_wait(barrier, 2)
    steps = count - 1

    def chunk(way, step):
        shift = count - 1 - step if way == 0 else 1 + step
        return (place + shift) % count

    def add_copy(part, way, step):
        source = first[part].at[way] if step == 0 else landed[part].at[way, step - 1]
        return pltpu.make_async_remote_copy(
            src_ref=source,
            dst_ref=landed[part].at[way, step],
            send_sem=add_send.at[part, way, step],
            recv_sem=add_recv.at[part, way, step],
            device_id=(right if way == 0 else left, tensor),
            device_id_type=MESH,
        )

    def share_copy(part, way, step):
        shift = count - step if way == 0 else step
        slot = shared[part].at[(place + shift) % count, way]
        return pltpu.make_async_remote_copy(
            src_ref=slot,
            dst_ref=slot,
            send_sem=share_send.at[part, way, step],
            recv_sem=share_recv.at[part, way, step],
            device_id=(right if way == 0 else left, tensor),
            device_id_type=MESH,
        )

    for part in range(parts):
        for way in range(2):
            first[part][way] = own[part][chunk(way, 0), way].astype(jnp.bfloat16)
            add_copy(part, way, 0).start()
    for step in range(steps):
        for part in range(parts):
            for way in range(2):
                add_copy(part, way, step).wait_recv()
                total = landed[part][way, step].astype(jnp.float32) + own[part][
                    chunk(way, step + 1), way
                ].astype(jnp.float32)
                if step < steps - 1:
                    landed[part][way, step] = total.astype(jnp.bfloat16)
                    add_copy(part, way, step + 1).start()
                else:
                    shared[part][place, way] = total.astype(jnp.bfloat16)
                    share_copy(part, way, 0).start()
    for step in range(steps):
        for part in range(parts):
            for way in range(2):
                share_copy(part, way, step).wait_recv()
                if step < steps - 1:
                    share_copy(part, way, step + 1).start()
    for part in range(parts):
        for way in range(2):
            for step in range(steps):
                add_copy(part, way, step).wait_send()
                share_copy(part, way, step).wait_send()
    outs = [pltpu.make_async_copy(shared[part], full[part], out_sem.at[part]) for part in range(parts)]
    for copy in outs:
        copy.start()
    for copy in outs:
        copy.wait()


def ring_sum(grads, count):
    rows = [grad.shape[0] // (2 * count) for grad in grads]
    blocks = [
        grad.reshape(count, 2, size, grad.shape[1]) for grad, size in zip(grads, rows)
    ]
    parts = len(blocks)
    half = [jax.ShapeDtypeStruct(block.shape, jnp.bfloat16) for block in blocks]
    summed = pl.pallas_call(
        functools.partial(grad_ring, count, parts),
        out_shape=half,
        in_specs=[pl.BlockSpec(memory_space=pltpu.VMEM)] * parts,
        out_specs=[pl.BlockSpec(memory_space=pl.ANY)] * parts,
        scratch_shapes=[pltpu.VMEM(block.shape[1:], jnp.bfloat16) for block in blocks]
        + [
            pltpu.VMEM((2, count - 1) + block.shape[2:], jnp.bfloat16) for block in blocks
        ]
        + [pltpu.SemaphoreType.DMA((parts, 2, count - 1))] * 4
        + [pltpu.SemaphoreType.DMA((parts,))]
        + [pltpu.VMEM(block.shape, jnp.bfloat16) for block in blocks],
        compiler_params=pltpu.CompilerParams(
            collective_id=0, has_side_effects=True, vmem_limit_bytes=60 << 20
        ),
        name="grad_ring",
    )(*blocks)
    return [
        block.reshape(grad.shape).astype(jnp.float32) for block, grad in zip(summed, grads)
    ]


HEAD_DIM = 64


EPSILON = 1e-05
ROOT_HALF = 0.7071067811865476
INVERSE_ROOT_TAU = 0.3989422804014327


def norm_rows(rows, gain, shift):
    centred = rows - jnp.mean(rows, axis=-1, keepdims=True)
    inverse = lax.rsqrt(jnp.mean(centred * centred, axis=-1, keepdims=True) + EPSILON)
    normed = centred * inverse
    return (normed * gain + shift, normed, inverse)


def norm_back(grad_out, normed, inverse, gain):
    scaled = grad_out * gain
    grad_in = inverse * (
        scaled
        - jnp.mean(scaled, axis=-1, keepdims=True)
        - normed * jnp.mean(scaled * normed, axis=-1, keepdims=True)
    )
    return (grad_in, jnp.sum(grad_out * normed, axis=0), jnp.sum(grad_out, axis=0))


def add_terms(running, terms):
    if running is None:
        return terms
    return tuple((left + right for left, right in zip(running, terms)))


def head_split(matrix):
    return matrix.reshape(matrix.shape[0], matrix.shape[1] // HEAD_DIM, HEAD_DIM)


def masked_scores(queries, key_rows, key_mask):
    scores = jnp.einsum(
        "qhd,khd->hqk",
        head_split(queries),
        head_split(key_rows),
        preferred_element_type=jnp.float32,
    ) * HEAD_DIM ** (-0.5)
    return jnp.where(key_mask[None, None, :], scores, -1e30)


def layer_forward(local_frames, key_count, weights):
    (
        query_weight,
        query_bias,
        key_weight,
        value_weight,
        value_bias,
        out_weight,
        out_bias,
        first_gain,
        first_shift,
        up_weight,
        up_bias,
        down_weight,
        down_bias,
        second_gain,
        second_shift,
    ) = weights
    full_frames = lax.all_gather(local_frames, "tensor", axis=0, tiled=True)
    length = full_frames.shape[0]
    queries = (
        jnp.dot(full_frames, query_weight, preferred_element_type=jnp.float32) + query_bias
    ).astype(jnp.bfloat16)
    key_rows = jnp.dot(full_frames, key_weight, preferred_element_type=jnp.float32).astype(
        jnp.bfloat16
    )
    values = (
        jnp.dot(full_frames, value_weight, preferred_element_type=jnp.float32) + value_bias
    ).astype(jnp.bfloat16)
    key_mask = jnp.arange(length) < key_count
    scores = masked_scores(queries, key_rows, key_mask)
    row_top = jnp.max(scores, axis=-1, keepdims=True)
    exponent = jnp.exp(scores - row_top)
    row_total = jnp.sum(exponent, axis=-1, keepdims=True)
    attention = (exponent / row_total).astype(jnp.bfloat16)
    log_total = row_top + jnp.log(row_total)
    context = (
        jnp.einsum(
            "hqk,khd->qhd", attention, head_split(values), preferred_element_type=jnp.float32
        )
        .reshape(length, -1)
        .astype(jnp.bfloat16)
    )
    attended = lax.psum_scatter(
        jnp.dot(context, out_weight, preferred_element_type=jnp.float32).astype(jnp.bfloat16),
        "tensor",
        scatter_dimension=0,
        tiled=True,
    ).astype(jnp.float32)
    first, first_normed, first_inverse = norm_rows(
        local_frames.astype(jnp.float32) + attended + out_bias, first_gain, first_shift
    )
    first_full = lax.all_gather(first.astype(jnp.bfloat16), "tensor", axis=0, tiled=True)
    hidden = jnp.dot(first_full, up_weight, preferred_element_type=jnp.float32) + up_bias
    activated = jax.nn.gelu(hidden, approximate=False).astype(jnp.bfloat16)
    mixed = lax.psum_scatter(
        jnp.dot(activated, down_weight, preferred_element_type=jnp.float32).astype(jnp.bfloat16),
        "tensor",
        scatter_dimension=0,
        tiled=True,
    ).astype(jnp.float32)
    output, second_normed, second_inverse = norm_rows(
        first + mixed + down_bias, second_gain, second_shift
    )
    stored = (
        full_frames,
        queries,
        key_rows,
        values,
        key_mask,
        log_total,
        context,
        first_normed,
        first_inverse,
        first_full,
        hidden,
        activated,
        second_normed,
        second_inverse,
    )
    return (output, stored)


def ffn_backward(stored, grad_output, weights):
    (
        full_frames,
        queries,
        key_rows,
        values,
        key_mask,
        log_total,
        context,
        first_normed,
        first_inverse,
        first_full,
        hidden,
        activated,
        second_normed,
        second_inverse,
    ) = stored
    up_weight, down_weight, second_gain = (weights[9], weights[11], weights[13])
    grad_second, second_gain_term, second_shift_term = norm_back(
        grad_output, second_normed, second_inverse, second_gain
    )
    down_bias_term = jnp.sum(grad_second, axis=0)
    grad_mixed = lax.all_gather(grad_second.astype(jnp.bfloat16), "tensor", axis=0, tiled=True)
    grad_active = jnp.einsum(
        "rd,fd->rf", grad_mixed, down_weight, preferred_element_type=jnp.float32
    )
    gelu_slope = (
        0.5 * (1.0 + lax.erf(hidden * ROOT_HALF))
        + hidden * jnp.exp(-0.5 * hidden * hidden) * INVERSE_ROOT_TAU
    )
    grad_hidden = (grad_active * gelu_slope).astype(jnp.bfloat16)
    down_weight_term = jnp.einsum(
        "rf,rd->fd", activated, grad_mixed, preferred_element_type=jnp.float32
    )
    up_weight_term = jnp.einsum(
        "rd,rf->df", first_full, grad_hidden, preferred_element_type=jnp.float32
    )
    up_bias_term = jnp.sum(grad_hidden, axis=0, dtype=jnp.float32)
    grad_first = (
        lax.psum_scatter(
            jnp.einsum(
                "rf,df->rd", grad_hidden, up_weight, preferred_element_type=jnp.float32
            ).astype(jnp.bfloat16),
            "tensor",
            scatter_dimension=0,
            tiled=True,
        ).astype(jnp.float32)
        + grad_second
    )
    return (
        grad_first,
        (up_weight_term, up_bias_term, down_weight_term),
        (second_gain_term, second_shift_term, down_bias_term),
    )


def attention_backward(stored, grad_first, weights):
    (
        full_frames,
        queries,
        key_rows,
        values,
        key_mask,
        log_total,
        context,
        first_normed,
        first_inverse,
        first_full,
        hidden,
        activated,
        second_normed,
        second_inverse,
    ) = stored
    query_weight, key_weight, value_weight, out_weight, first_gain = (
        weights[0],
        weights[2],
        weights[3],
        weights[5],
        weights[7],
    )
    length = full_frames.shape[0]
    factor = HEAD_DIM ** (-0.5)
    grad_attn_in, first_gain_term, first_shift_term = norm_back(
        grad_first, first_normed, first_inverse, first_gain
    )
    out_bias_term = jnp.sum(grad_attn_in, axis=0)
    grad_attended = lax.all_gather(grad_attn_in.astype(jnp.bfloat16), "tensor", axis=0, tiled=True)
    grad_context = jnp.einsum(
        "rd,cd->rc", grad_attended, out_weight, preferred_element_type=jnp.float32
    ).astype(jnp.bfloat16)
    out_weight_term = jnp.einsum(
        "rc,rd->cd", context, grad_attended, preferred_element_type=jnp.float32
    )
    scores = masked_scores(queries, key_rows, key_mask)
    attention = jnp.exp(scores - log_total)
    context_heads = head_split(grad_context)
    grad_values = (
        jnp.einsum(
            "hqk,qhd->khd",
            attention.astype(jnp.bfloat16),
            context_heads,
            preferred_element_type=jnp.float32,
        )
        .reshape(length, -1)
        .astype(jnp.bfloat16)
    )
    grad_attention = jnp.einsum(
        "qhd,khd->hqk", context_heads, head_split(values), preferred_element_type=jnp.float32
    )
    grad_scores = (
        attention * (grad_attention - jnp.sum(attention * grad_attention, axis=-1, keepdims=True))
    ).astype(jnp.bfloat16)
    grad_queries = (
        (
            jnp.einsum(
                "hqk,khd->qhd",
                grad_scores,
                head_split(key_rows),
                preferred_element_type=jnp.float32,
            )
            * factor
        )
        .reshape(length, -1)
        .astype(jnp.bfloat16)
    )
    grad_keys = (
        (
            jnp.einsum(
                "hqk,qhd->khd", grad_scores, head_split(queries), preferred_element_type=jnp.float32
            )
            * factor
        )
        .reshape(length, -1)
        .astype(jnp.bfloat16)
    )
    query_weight_term = jnp.einsum(
        "rd,rc->dc", full_frames, grad_queries, preferred_element_type=jnp.float32
    )
    key_weight_term = jnp.einsum(
        "rd,rc->dc", full_frames, grad_keys, preferred_element_type=jnp.float32
    )
    value_weight_term = jnp.einsum(
        "rd,rc->dc", full_frames, grad_values, preferred_element_type=jnp.float32
    )
    query_bias_term = jnp.sum(grad_queries, axis=0, dtype=jnp.float32)
    value_bias_term = jnp.sum(grad_values, axis=0, dtype=jnp.float32)
    total = jnp.einsum("rc,dc->rd", grad_queries, query_weight, preferred_element_type=jnp.float32)
    total = total + jnp.einsum(
        "rc,dc->rd", grad_keys, key_weight, preferred_element_type=jnp.float32
    )
    grad_input = (
        lax.psum_scatter(
            (
                total
                + jnp.einsum(
                    "rc,dc->rd", grad_values, value_weight, preferred_element_type=jnp.float32
                )
            ).astype(jnp.bfloat16),
            "tensor",
            scatter_dimension=0,
            tiled=True,
        ).astype(jnp.float32)
        + grad_attn_in
    )
    return (
        grad_input,
        (
            query_weight_term,
            query_bias_term,
            key_weight_term,
            value_weight_term,
            value_bias_term,
            out_weight_term,
        ),
        (first_gain_term, first_shift_term, out_bias_term),
    )


def shards(
    frames,
    cotangent,
    lengths,
    query_weight,
    query_bias,
    key_weight,
    value_weight,
    value_bias,
    out_weight,
    out_bias,
    first_gain,
    first_shift,
    up_weight,
    up_bias,
    down_weight,
    down_bias,
    second_gain,
    second_shift,
):
    weights = (
        query_weight,
        query_bias,
        key_weight,
        value_weight,
        value_bias,
        out_weight,
        out_bias,
        first_gain,
        first_shift,
        up_weight,
        up_bias,
        down_weight,
        down_bias,
        second_gain,
        second_shift,
    )
    micro_count = frames.shape[0]
    share_rows = frames.shape[1]
    share_start = lax.axis_index("tensor") * share_rows
    outputs = []
    stored_list = []
    for micro_index in range(micro_count):
        output, stored = layer_forward(frames[micro_index], lengths[micro_index], weights)
        outputs.append(output.astype(jnp.bfloat16))
        stored_list.append(stored)
    attention_total = None
    ffn_total = None
    first_total = None
    second_total = None
    input_grads = []
    for micro_index in range(micro_count):
        stored = layer_forward(frames[micro_index], lengths[micro_index], weights)[1]
        live_rows = (jnp.arange(share_rows) + share_start < lengths[micro_index]).astype(
            jnp.float32
        )[:, None]
        grad_first, ffn_terms, second_terms = ffn_backward(
            stored, cotangent[micro_index] * live_rows, weights
        )
        ffn_total = add_terms(ffn_total, ffn_terms)
        second_total = add_terms(second_total, second_terms)
        grad_input, attention_terms, first_terms = attention_backward(stored, grad_first, weights)
        attention_total = add_terms(attention_total, attention_terms)
        first_total = add_terms(first_total, first_terms)
        input_grads.append(grad_input)
    (
        query_weight_sum,
        query_bias_sum,
        key_weight_sum,
        value_weight_sum,
        value_bias_sum,
        out_weight_sum,
    ) = attention_total
    up_weight_sum, up_bias_sum, down_weight_sum = ffn_total
    count = lax.axis_size("dp")
    large = (query_weight_sum, key_weight_sum, value_weight_sum, out_weight_sum, up_weight_sum, down_weight_sum)
    if count % 2 == 0 and all(grad.shape[0] % (16 * count) == 0 for grad in large[:3]):
        out_pad = jnp.pad(out_weight_sum, ((0, 256 - out_weight_sum.shape[0]), (0, 0)))
        large = ring_sum(large[:3] + (out_pad,) + large[4:], count)
        large[3] = large[3][: out_weight_sum.shape[0]]
    else:
        large = lax.psum(large, "dp")
    query_bias_sum, value_bias_sum, up_bias_sum = lax.psum(
        (query_bias_sum, value_bias_sum, up_bias_sum), "dp"
    )
    summed = (large[0], query_bias_sum, large[1], large[2], value_bias_sum, large[3], large[4], up_bias_sum, large[5])
    attention_total = summed[:6]
    ffn_total = summed[6:]
    first_gain_sum, first_shift_sum, out_bias_sum = first_total
    second_gain_sum, second_shift_sum, down_bias_sum = second_total
    small_sums = lax.psum(
        (
            first_gain_sum,
            first_shift_sum,
            out_bias_sum,
            second_gain_sum,
            second_shift_sum,
            down_bias_sum,
        ),
        ("dp", "tensor"),
    )
    return (
        jnp.stack(outputs),
        jnp.stack(input_grads),
        attention_total[0],
        attention_total[1],
        attention_total[2],
        attention_total[3],
        attention_total[4],
        attention_total[5],
        small_sums[2],
        small_sums[0],
        small_sums[1],
        ffn_total[0],
        ffn_total[1],
        ffn_total[2],
        small_sums[5],
        small_sums[3],
        small_sums[4],
    )


def solution(mesh):
    return jax.shard_map(
        shards,
        mesh=mesh,
        in_specs=(
            P("dp", "tensor", None),
            P("dp", "tensor", None),
            P("dp"),
            P(None, "tensor"),
            P("tensor"),
            P(None, "tensor"),
            P(None, "tensor"),
            P("tensor"),
            P("tensor", None),
            P(),
            P(),
            P(),
            P(None, "tensor"),
            P("tensor"),
            P("tensor", None),
            P(),
            P(),
            P(),
        ),
        out_specs=(
            P("dp", "tensor", None),
            P("dp", "tensor", None),
            P(None, "tensor"),
            P("tensor"),
            P(None, "tensor"),
            P(None, "tensor"),
            P("tensor"),
            P("tensor", None),
            P(),
            P(),
            P(),
            P(None, "tensor"),
            P("tensor"),
            P("tensor", None),
            P(),
            P(),
            P(),
        ),
        check_vma=False,
    )
```

```python
import functools

import jax
import jax.numpy as jnp
from jax import lax
from jax.experimental import pallas as pl
from jax.experimental.pallas import tpu as pltpu
from jax.sharding import PartitionSpec as P

MESH = pl.DeviceIdType.MESH
HEAD_DIM = 64
EPSILON = 1e-05
ROOT_HALF = 0.7071067811865476
INVERSE_ROOT_TAU = 0.3989422804014327
MASKED = -1e30
VMEM_BYTES = 62 << 20
BF = jnp.bfloat16
F32 = jnp.float32


def up_to(size, unit):
    return (size + unit - 1) // unit * unit


def dot(left, right):
    return jnp.dot(left, right, preferred_element_type=F32)


def dot_nt(left, right):
    return lax.dot_general(left, right, (((1,), (1,)), ((), ())), preferred_element_type=F32)


def dot_tn(left, right):
    return lax.dot_general(left, right, (((0,), (0,)), ((), ())), preferred_element_type=F32)


def pad_rows(rows, size):
    extra = size - rows.shape[0]
    if extra == 0:
        return rows
    return jnp.concatenate([rows, jnp.zeros((extra, rows.shape[1]), rows.dtype)], axis=0)


class Group:
    def __init__(self):
        self.dp = lax.axis_index("dp")
        self.own = lax.axis_index("tensor")
        self.y = self.own // 2
        self.core = self.own % 2
        self.mate = self.y * 2 + (1 - self.core)
        self.far = (1 - self.y) * 2 + self.core

    def greet(self):
        barrier = pltpu.get_barrier_semaphore()
        for peer in (self.mate, self.far):
            pl.semaphore_signal(barrier, inc=1, device_id=(self.dp, peer), device_id_type=MESH)
        pl.semaphore_wait(barrier, 2)

    def share(self, turn):
        late = turn // 2
        other = ((turn + 1) // 2) % 2
        ybit = (1 - self.y) * (1 - late) + self.y * late
        core = self.core * (1 - other) + (1 - self.core) * other
        return ybit * 2 + core

    def copy(self, source, target, send, recv, peer):
        return pltpu.make_async_remote_copy(
            src_ref=source,
            dst_ref=target,
            send_sem=send,
            recv_sem=recv,
            device_id=(self.dp, peer),
            device_id_type=MESH,
        )


class Gather:
    def __init__(self, group, full, send, recv):
        self.group, self.full, self.send, self.recv = group, full, send, recv

    def _copy(self, seq, kind):
        group = self.group
        share = group.far if kind == 2 else group.own
        slot = self.full.at[seq, share]
        peer = group.far if kind == 0 else group.mate
        return group.copy(slot, slot, self.send.at[seq, kind], self.recv.at[seq, kind], peer)

    def start(self, seq):
        self._copy(seq, 0).start()
        self._copy(seq, 1).start()

    def wait(self, seq, turn):
        @pl.when(turn == 0)
        def _():
            self._copy(seq, 0).wait_recv()
            self._copy(seq, 2).start()

        @pl.when(turn == 1)
        def _():
            self._copy(seq, 2).wait_recv()

        @pl.when(turn == 2)
        def _():
            self._copy(seq, 1).wait_recv()

    def close(self, seq):
        for kind in range(3):
            self._copy(seq, kind).wait_send()


class Scatter:
    def __init__(self, group, buffers, send, recv):
        self.group = group
        self.outgoing, self.keep, self.near, self.cross, self.landed = buffers
        self.send, self.recv = send, recv

    def _near(self, seq, index):
        return self.group.copy(
            self.outgoing.at[seq, index],
            self.near.at[seq, index],
            self.send.at[seq, index],
            self.recv.at[seq, index],
            self.group.mate,
        )

    def _cross(self, seq):
        return self.group.copy(
            self.cross.at[seq],
            self.landed.at[seq],
            self.send.at[seq, 2],
            self.recv.at[seq, 2],
            self.group.far,
        )

    def put(self, seq, turn, terms):
        @pl.when((turn == 0) | (turn == 3))
        def _():
            self.keep[seq, turn // 3] = terms

        @pl.when((turn == 1) | (turn == 2))
        def _():
            self.outgoing[seq, turn - 1] = terms.astype(BF)
            self._near(seq, turn - 1).start()

        @pl.when(turn == 2)
        def _():
            self._near(seq, 0).wait_recv()
            total = self.keep[seq, 0] + self.near[seq, 0].astype(F32)
            self.cross[seq] = total.astype(BF)
            self._cross(seq).start()

    def take(self, seq):
        self._near(seq, 1).wait_recv()
        self._cross(seq).wait_recv()
        for index in range(2):
            self._near(seq, index).wait_send()
        self._cross(seq).wait_send()
        return (
            self.keep[seq, 1]
            + self.near[seq, 1].astype(F32)
            + self.landed[seq].astype(F32)
        )


def norm(rows):
    centred = rows - jnp.mean(rows, axis=-1, keepdims=True)
    inverse = lax.rsqrt(jnp.mean(centred * centred, axis=-1, keepdims=True) + EPSILON)
    return centred * inverse, inverse


def norm_back(grad, normed, inverse, gain):
    scaled = grad * gain
    return inverse * (
        scaled
        - jnp.mean(scaled, axis=-1, keepdims=True)
        - normed * jnp.mean(scaled * normed, axis=-1, keepdims=True)
    )


def sum_rows(rows):
    return jnp.sum(rows, axis=0, keepdims=True)


def lane_index(rows, lanes):
    return lax.broadcasted_iota(jnp.int32, (rows, lanes), 1)


def front(
    lengths, frames, cotangent, query_weight, key_weight, value_weight, projection_bias,
    out_weight, up_weight, down_weight, vectors,
    layer_output, full_frames, projected, context, grad_attended, up_grad, down_grad, sums,
    wide_weight, wide_out, first_normed, first_inverse, first_full, hidden, activated,
    grad_second, grad_mixed, grad_hidden,
    outgoing, keep, near, cross, landed,
    gather_send, gather_recv, scatter_send, scatter_recv,
):
    seqs, share_rows, width = frames.shape
    rows = full_frames.shape[2]
    heads_width = query_weight.shape[1]
    lanes = wide_weight.shape[1] // 3
    heads = heads_width // HEAD_DIM
    length = 4 * rows
    group = Group()
    out_bias, first_gain, first_shift, down_bias, second_gain, second_shift, up_bias = (
        vectors[index : index + 1] for index in range(7)
    )
    buffers = (outgoing, keep, near, cross, landed)
    gathers = [
        Gather(group, full, gather_send.at[index], gather_recv.at[index])
        for index, full in enumerate((full_frames, first_full, grad_mixed))
    ]
    scatters = [
        Scatter(group, buffers, scatter_send.at[index], scatter_recv.at[index]) for index in range(3)
    ]

    group.greet()

    def each(stage):
        def body(seq, carry):
            stage(seq)
            return carry

        lax.fori_loop(0, seqs, body, 0)

    def turns(step):
        def body(turn, carry):
            step(turn)
            return carry

        lax.fori_loop(0, 4, body, 0)

    def send_frames(seq):
        full_frames[seq, group.own] = pad_rows(frames[seq].astype(F32), rows).astype(BF)
        gathers[0].start(seq)

    each(send_frames)
    wide_weight[...] = jnp.zeros_like(wide_weight)
    for index, weight in enumerate((query_weight, key_weight, value_weight)):
        wide_weight[:, index * lanes : index * lanes + heads_width] = weight[...]
    wide_out[...] = jnp.zeros_like(wide_out)
    wide_out[:heads_width] = out_weight[...]
    sums[...] = jnp.zeros_like(sums)
    up_grad[...] = jnp.zeros_like(up_grad)
    down_grad[...] = jnp.zeros_like(down_grad)

    def attention(seq):
        def project(step):
            turn = (1 - step // 2) * (3 - step) + (step // 2) * (step - 2)
            gathers[0].wait(seq, turn)
            share = group.share(turn)
            result = dot(full_frames[seq, share], wide_weight[...]) + projection_bias[...]
            place = lax.broadcasted_iota(jnp.int32, (rows, lanes), 0)
            dead = (place >= share_rows) | (place + share * share_rows >= lengths[seq])
            flag = jnp.where(dead & (lane_index(rows, lanes) == heads_width), MASKED, 0.0)
            start = pl.multiple_of(share * rows, 16)
            projected[seq, pl.ds(start, rows), 0:lanes] = (
                result[:, :lanes].astype(BF) * HEAD_DIM ** (-0.5)
            ).astype(BF)
            projected[seq, pl.ds(start, rows), lanes : 2 * lanes] = (
                result[:, lanes : 2 * lanes] + flag
            ).astype(BF)
            projected[seq, pl.ds(start, rows), 2 * lanes : 3 * lanes] = result[:, 2 * lanes :].astype(BF)

        turns(project)

        def attend(turn):
            share = group.share(turn)
            start = pl.multiple_of(share * rows, 16)
            queries = projected[seq, pl.ds(start, rows), 0:lanes]
            lane = lane_index(rows, lanes)
            mixed = jnp.zeros((rows, lanes), F32)
            for head in range(heads):
                inside = lane // HEAD_DIM == head
                picked = jnp.where(inside | (lane == heads_width), queries, jnp.zeros_like(queries))
                scores = dot_nt(picked, projected[seq, :, lanes : 2 * lanes])
                exponent = jnp.exp(scores - jnp.max(scores, axis=-1, keepdims=True))
                weights = exponent * (1.0 / jnp.sum(exponent, axis=-1, keepdims=True))
                part = dot(weights.astype(BF), projected[seq, :, 2 * lanes : 3 * lanes])
                mixed = jnp.where(inside, part, mixed)
            mixed = mixed.astype(BF)
            context[seq, pl.ds(start, rows)] = mixed
            scatters[0].put(seq, turn, dot(mixed, wide_out[...]))

        turns(attend)

    each(attention)

    def first_norm(seq):
        attended = scatters[0].take(seq)
        normed, inverse = norm(full_frames[seq, group.own].astype(F32) + attended + out_bias)
        first_normed[seq] = normed
        first_inverse[seq] = inverse
        first_full[seq, group.own] = (normed * first_gain + first_shift).astype(BF)
        gathers[1].start(seq)

    each(first_norm)

    def feed(seq):
        def step(turn):
            gathers[1].wait(seq, turn)
            share = group.share(turn)
            start = pl.multiple_of(share * rows, 16)
            inner = dot(first_full[seq, share], up_weight[...]) + up_bias
            hidden[seq, pl.ds(start, rows)] = inner
            active = (0.5 * inner * (1.0 + lax.erf(inner * ROOT_HALF))).astype(BF)
            activated[seq, pl.ds(start, rows)] = active
            scatters[1].put(seq, turn, dot(active, down_weight[...]))

        turns(step)

    each(feed)

    def second_norm(seq):
        mixed = scatters[1].take(seq)
        first = first_normed[seq] * first_gain + first_shift
        normed, inverse = norm(first + mixed + down_bias)
        layer_output[seq] = (normed * second_gain + second_shift)[:share_rows].astype(BF)
        place = lax.broadcasted_iota(jnp.int32, (rows, width), 0)
        live = (place < share_rows) & (place + group.own * share_rows < lengths[seq])
        grad = jnp.where(live, pad_rows(cotangent[seq], rows), 0.0)
        back = norm_back(grad, normed, inverse, second_gain)
        sums[0:1] += sum_rows(grad * normed)
        sums[1:2] += sum_rows(grad)
        sums[2:3] += sum_rows(back)
        grad_second[seq] = back
        grad_mixed[seq, group.own] = back.astype(BF)
        gathers[2].start(seq)

    each(second_norm)

    def feed_back(seq):
        def step(turn):
            gathers[2].wait(seq, turn)
            share = group.share(turn)
            start = pl.multiple_of(share * rows, 16)
            grad_active = dot_nt(grad_mixed[seq, share], down_weight[...])
            inner = hidden[seq, pl.ds(start, rows)]
            slope = (
                0.5 * (1.0 + lax.erf(inner * ROOT_HALF))
                + inner * jnp.exp(-0.5 * inner * inner) * INVERSE_ROOT_TAU
            )
            grad = (grad_active * slope).astype(BF)
            grad_hidden[seq, pl.ds(start, rows)] = grad
            sums[6:7] += sum_rows(grad.astype(F32))
            scatters[2].put(seq, turn, dot_nt(grad, up_weight[...]))

        turns(step)

        def weights(step, carry):
            share = step
            start = pl.multiple_of(share * rows, 16)
            down_grad[...] += dot_tn(activated[seq, pl.ds(start, rows)], grad_mixed[seq, share])
            up_grad[...] += dot_tn(first_full[seq, share], grad_hidden[seq, pl.ds(start, rows)])
            return carry

        lax.fori_loop(0, 4, weights, 0)

    each(feed_back)

    def first_back(seq):
        grad = grad_second[seq] + scatters[2].take(seq)
        back = norm_back(grad, first_normed[seq], first_inverse[seq], first_gain)
        sums[3:4] += sum_rows(grad * first_normed[seq])
        sums[4:5] += sum_rows(grad)
        sums[5:6] += sum_rows(back)
        grad_attended[seq] = back

    each(first_back)

    def close(seq):
        for gather in gathers:
            gather.close(seq)

    each(close)


def rear(
    attended_in, full_frames, projected, context, query_weight, key_weight, value_weight, out_weight,
    input_grad, wide_grad, out_grad, sums,
    wide_weight, wide_out, grad_full, grad_context, grad_projected, total,
    outgoing, keep, near, cross, landed,
    gather_send, gather_recv, scatter_send, scatter_recv,
):
    seqs, rows, width = attended_in.shape
    share_rows = input_grad.shape[1]
    heads_width = query_weight.shape[1]
    lanes = wide_weight.shape[1] // 3
    heads = heads_width // HEAD_DIM
    length = 4 * rows
    group = Group()
    gather = Gather(group, grad_full, gather_send, gather_recv)
    scatter = Scatter(group, (outgoing, keep, near, cross, landed), scatter_send, scatter_recv)
    group.greet()

    def each(stage):
        def body(seq, carry):
            stage(seq)
            return carry

        lax.fori_loop(0, seqs, body, 0)

    def turns(step):
        def body(turn, carry):
            step(turn)
            return carry

        lax.fori_loop(0, 4, body, 0)

    def send(seq):
        grad_full[seq, group.own] = attended_in[seq].astype(BF)
        gather.start(seq)

    each(send)
    wide_weight[...] = jnp.zeros_like(wide_weight)
    for index, weight in enumerate((query_weight, key_weight, value_weight)):
        wide_weight[:, index * lanes : index * lanes + heads_width] = weight[...]
    wide_out[...] = jnp.zeros_like(wide_out)
    wide_out[:heads_width] = out_weight[...]
    wide_grad[...] = jnp.zeros_like(wide_grad)
    out_grad[...] = jnp.zeros_like(out_grad)
    sums[...] = jnp.zeros_like(sums)

    def back(seq):
        def step(turn):
            gather.wait(seq, turn)
            share = group.share(turn)
            start = pl.multiple_of(share * rows, 16)
            grad_context[pl.ds(start, rows)] = dot_nt(grad_full[seq, share], wide_out[...]).astype(BF)
            out_grad[...] += dot_tn(context[seq, pl.ds(start, rows)], grad_full[seq, share])

        turns(step)
        total[...] = jnp.zeros_like(total)

        def head_step(head, carry):
            lane = lane_index(length, lanes)
            inside = lane // HEAD_DIM == head
            queries = projected[seq, :, 0:lanes]
            keys = projected[seq, :, lanes : 2 * lanes]
            values = projected[seq, :, 2 * lanes : 3 * lanes]
            picked = jnp.where(inside | (lane == heads_width), queries, jnp.zeros_like(queries))
            scores = dot_nt(keys, picked)
            exponent = jnp.exp(scores - jnp.max(scores, axis=0, keepdims=True))
            weights = exponent * (1.0 / jnp.sum(exponent, axis=0, keepdims=True))
            grads = grad_context[...]
            part = dot(weights.astype(BF), grads)
            total[:, 2 * lanes : 3 * lanes] = jnp.where(inside, part, total[:, 2 * lanes : 3 * lanes])
            slopes = weights * dot_nt(values, jnp.where(inside, grads, jnp.zeros_like(grads)))
            slopes = (slopes - weights * jnp.sum(slopes, axis=0, keepdims=True)).astype(BF)
            part = dot(slopes, queries)
            total[:, lanes : 2 * lanes] = jnp.where(inside, part, total[:, lanes : 2 * lanes])
            part = dot_tn(slopes, keys) * HEAD_DIM ** (-0.5)
            total[:, 0:lanes] = jnp.where(inside, part, total[:, 0:lanes])
            return carry

        lax.fori_loop(0, heads, head_step, 0)

        def finish(turn):
            share = group.share(turn)
            start = pl.multiple_of(share * rows, 16)
            grads = total[pl.ds(start, rows)].astype(BF)
            grad_projected[seq, pl.ds(start, rows)] = grads
            sums[...] += sum_rows(grads.astype(F32))
            scatter.put(seq, turn, dot_nt(grads, wide_weight[...]))

        turns(finish)

        def weights(share, carry):
            start = pl.multiple_of(share * rows, 16)
            wide_grad[...] += dot_tn(full_frames[seq, share], grad_projected[seq, pl.ds(start, rows)])
            return carry

        lax.fori_loop(0, 4, weights, 0)

    each(back)

    def last(seq):
        input_grad[seq] = (scatter.take(seq) + attended_in[seq])[:share_rows]
        gather.close(seq)

    each(last)


def ring_place(index, count):
    return jnp.where(index % 2 == 0, index // 2, count - 1 - index // 2)


def ring_index(place, count):
    return jnp.where(place < count // 2, 2 * place, 2 * (count - 1 - place) + 1)


def grad_ring(count, parts, *refs):
    own = refs[:parts]
    full = refs[parts : 2 * parts]
    first = refs[2 * parts : 3 * parts]
    landed = refs[3 * parts : 4 * parts]
    add_send, add_recv, share_send, share_recv, out_sem = refs[4 * parts : 4 * parts + 5]
    shared = refs[4 * parts + 5 :]
    tensor = lax.axis_index("tensor")
    place = ring_place(lax.axis_index("dp"), count)
    right = ring_index((place + 1) % count, count)
    left = ring_index((place + count - 1) % count, count)
    barrier = pltpu.get_barrier_semaphore()
    for peer in (left, right):
        pl.semaphore_signal(barrier, inc=1, device_id=(peer, tensor), device_id_type=MESH)
    pl.semaphore_wait(barrier, 2)
    steps = count - 1

    def chunk(way, step):
        shift = count - 1 - step if way == 0 else 1 + step
        return (place + shift) % count

    def add_copy(part, way, step):
        source = first[part].at[way] if step == 0 else landed[part].at[way, step - 1]
        return pltpu.make_async_remote_copy(
            src_ref=source,
            dst_ref=landed[part].at[way, step],
            send_sem=add_send.at[part, way, step],
            recv_sem=add_recv.at[part, way, step],
            device_id=(right if way == 0 else left, tensor),
            device_id_type=MESH,
        )

    def share_copy(part, way, step):
        shift = count - step if way == 0 else step
        slot = shared[part].at[(place + shift) % count, way]
        return pltpu.make_async_remote_copy(
            src_ref=slot,
            dst_ref=slot,
            send_sem=share_send.at[part, way, step],
            recv_sem=share_recv.at[part, way, step],
            device_id=(right if way == 0 else left, tensor),
            device_id_type=MESH,
        )

    for part in range(parts):
        for way in range(2):
            first[part][way] = own[part][chunk(way, 0), way].astype(jnp.bfloat16)
            add_copy(part, way, 0).start()
    for step in range(steps):
        for part in range(parts):
            for way in range(2):
                add_copy(part, way, step).wait_recv()
                total = landed[part][way, step].astype(jnp.float32) + own[part][
                    chunk(way, step + 1), way
                ].astype(jnp.float32)
                if step < steps - 1:
                    landed[part][way, step] = total.astype(jnp.bfloat16)
                    add_copy(part, way, step + 1).start()
                else:
                    shared[part][place, way] = total.astype(jnp.bfloat16)
                    share_copy(part, way, 0).start()
    for step in range(steps):
        for part in range(parts):
            for way in range(2):
                share_copy(part, way, step).wait_recv()
                if step < steps - 1:
                    share_copy(part, way, step + 1).start()
    for part in range(parts):
        for way in range(2):
            for step in range(steps):
                add_copy(part, way, step).wait_send()
                share_copy(part, way, step).wait_send()
    outs = [pltpu.make_async_copy(shared[part], full[part], out_sem.at[part]) for part in range(parts)]
    for copy in outs:
        copy.start()
    for copy in outs:
        copy.wait()


def ring_sum(grads, count):
    rows = [grad.shape[0] // (2 * count) for grad in grads]
    blocks = [
        grad.reshape(count, 2, size, grad.shape[1]) for grad, size in zip(grads, rows)
    ]
    parts = len(blocks)
    half = [jax.ShapeDtypeStruct(block.shape, jnp.bfloat16) for block in blocks]
    summed = pl.pallas_call(
        functools.partial(grad_ring, count, parts),
        out_shape=half,
        in_specs=[pl.BlockSpec(memory_space=pltpu.VMEM)] * parts,
        out_specs=[pl.BlockSpec(memory_space=pl.ANY)] * parts,
        scratch_shapes=[pltpu.VMEM(block.shape[1:], jnp.bfloat16) for block in blocks]
        + [
            pltpu.VMEM((2, count - 1) + block.shape[2:], jnp.bfloat16) for block in blocks
        ]
        + [pltpu.SemaphoreType.DMA((parts, 2, count - 1))] * 4
        + [pltpu.SemaphoreType.DMA((parts,))]
        + [pltpu.VMEM(block.shape, jnp.bfloat16) for block in blocks],
        compiler_params=pltpu.CompilerParams(
            collective_id=0, has_side_effects=True, vmem_limit_bytes=60 << 20
        ),
        name="grad_ring",
    )(*blocks)
    return [
        block.reshape(grad.shape).astype(jnp.float32) for block, grad in zip(summed, grads)
    ]


VMEM_SPEC = pl.BlockSpec(memory_space=pltpu.VMEM)


def group_scratch(seqs, rows, width):
    return [
        pltpu.VMEM((seqs, 2, rows, width), BF),
        pltpu.VMEM((seqs, 2, rows, width), F32),
        pltpu.VMEM((seqs, 2, rows, width), BF),
        pltpu.VMEM((seqs, rows, width), BF),
        pltpu.VMEM((seqs, rows, width), BF),
    ]


def shards(
    frames,
    cotangent,
    lengths,
    query_weight,
    query_bias,
    key_weight,
    value_weight,
    value_bias,
    out_weight,
    out_bias,
    first_gain,
    first_shift,
    up_weight,
    up_bias,
    down_weight,
    down_bias,
    second_gain,
    second_shift,
):
    seqs, share_rows, width = frames.shape
    rows = up_to(share_rows, 16)
    length = 4 * rows
    heads_width = query_weight.shape[1]
    inner = up_weight.shape[1]
    lanes = up_to(heads_width + 1, 128)
    pad = lanes - heads_width
    projection_bias = jnp.concatenate(
        [
            query_bias,
            jnp.full((1,), HEAD_DIM**0.5, F32),
            jnp.zeros((pad - 1 + lanes,), F32),
            value_bias,
            jnp.zeros((pad,), F32),
        ]
    )[None]
    vectors = jnp.stack(
        [out_bias, first_gain, first_shift, down_bias, second_gain, second_shift, up_bias]
    )
    shape = jax.ShapeDtypeStruct
    (
        layer_output, full_frames, projected, context, grad_attended, up_grad, down_grad, sums,
    ) = pl.pallas_call(
        front,
        out_shape=[
            shape(frames.shape, BF),
            shape((seqs, 4, rows, width), BF),
            shape((seqs, length, 3 * lanes), BF),
            shape((seqs, length, lanes), BF),
            shape((seqs, rows, width), F32),
            shape(up_weight.shape, F32),
            shape(down_weight.shape, F32),
            shape((8, width), F32),
        ],
        in_specs=[pl.BlockSpec(memory_space=pltpu.SMEM)] + [VMEM_SPEC] * 10,
        out_specs=[VMEM_SPEC] * 8,
        scratch_shapes=[
            pltpu.VMEM((width, 3 * lanes), BF),
            pltpu.VMEM((lanes, width), BF),
            pltpu.VMEM((seqs, rows, width), F32),
            pltpu.VMEM((seqs, rows, 1), F32),
            pltpu.VMEM((seqs, 4, rows, width), BF),
            pltpu.VMEM((seqs, length, inner), F32),
            pltpu.VMEM((seqs, length, inner), BF),
            pltpu.VMEM((seqs, rows, width), F32),
            pltpu.VMEM((seqs, 4, rows, width), BF),
            pltpu.VMEM((seqs, length, inner), BF),
        ]
        + group_scratch(seqs, rows, width)
        + [pltpu.SemaphoreType.DMA((3, seqs, 3))] * 4,
        compiler_params=pltpu.CompilerParams(
            collective_id=1, has_side_effects=True, vmem_limit_bytes=VMEM_BYTES
        ),
        name="front",
    )(
        lengths, frames, cotangent, query_weight, key_weight, value_weight, projection_bias,
        out_weight, up_weight, down_weight, vectors,
    )
    input_grad, wide_grad, out_grad, rear_sums = pl.pallas_call(
        rear,
        out_shape=[
            shape(frames.shape, F32),
            shape((width, 3 * lanes), F32),
            shape((lanes, width), F32),
            shape((1, 3 * lanes), F32),
        ],
        in_specs=[VMEM_SPEC] * 8,
        out_specs=[VMEM_SPEC] * 4,
        scratch_shapes=[
            pltpu.VMEM((width, 3 * lanes), BF),
            pltpu.VMEM((lanes, width), BF),
            pltpu.VMEM((seqs, 4, rows, width), BF),
            pltpu.VMEM((length, lanes), BF),
            pltpu.VMEM((seqs, length, 3 * lanes), BF),
            pltpu.VMEM((length, 3 * lanes), F32),
        ]
        + group_scratch(seqs, rows, width)
        + [pltpu.SemaphoreType.DMA((seqs, 3))] * 4,
        compiler_params=pltpu.CompilerParams(
            collective_id=2, has_side_effects=True, vmem_limit_bytes=VMEM_BYTES
        ),
        name="rear",
    )(
        grad_attended, full_frames, projected, context, query_weight, key_weight, value_weight, out_weight,
    )
    count = lax.axis_size("dp")
    large = [wide_grad, out_grad, up_grad, down_grad]
    if count % 2 == 0 and all(grad.shape[0] % (16 * count) == 0 for grad in large):
        large = ring_sum(large, count)
    else:
        large = lax.psum(large, "dp")
    wide_grad, out_grad, up_grad, down_grad = large
    rear_sums, up_bias_grad = lax.psum((rear_sums[0], sums[6]), "dp")
    small = lax.psum(sums[:6], ("dp", "tensor"))
    return (
        layer_output,
        input_grad,
        wide_grad[:, :heads_width],
        rear_sums[:heads_width],
        wide_grad[:, lanes : lanes + heads_width],
        wide_grad[:, 2 * lanes : 2 * lanes + heads_width],
        rear_sums[2 * lanes : 2 * lanes + heads_width],
        out_grad[:heads_width],
        small[5],
        small[3],
        small[4],
        up_grad,
        up_bias_grad,
        down_grad,
        small[2],
        small[0],
        small[1],
    )


def solution(mesh):
    return jax.shard_map(
        shards,
        mesh=mesh,
        in_specs=(
            P("dp", "tensor", None),
            P("dp", "tensor", None),
            P("dp"),
            P(None, "tensor"),
            P("tensor"),
            P(None, "tensor"),
            P(None, "tensor"),
            P("tensor"),
            P("tensor", None),
            P(),
            P(),
            P(),
            P(None, "tensor"),
            P("tensor"),
            P("tensor", None),
            P(),
            P(),
            P(),
        ),
        out_specs=(
            P("dp", "tensor", None),
            P("dp", "tensor", None),
            P(None, "tensor"),
            P("tensor"),
            P(None, "tensor"),
            P(None, "tensor"),
            P("tensor"),
            P("tensor", None),
            P(),
            P(),
            P(),
            P(None, "tensor"),
            P("tensor"),
            P("tensor", None),
            P(),
            P(),
            P(),
        ),
        check_vma=False,
    )
```

```python
import functools

import jax
import jax.numpy as jnp
from jax import lax
from jax.experimental import pallas as pl
from jax.experimental.pallas import tpu as pltpu
from jax.sharding import PartitionSpec as P

MESH = pl.DeviceIdType.MESH
HEAD_DIM = 64
EPSILON = 1e-05
ROOT_HALF = 0.7071067811865476
INVERSE_ROOT_TAU = 0.3989422804014327
MASKED = -1e30
VMEM_BYTES = 62 << 20
BF = jnp.bfloat16
F32 = jnp.float32


def up_to(size, unit):
    return (size + unit - 1) // unit * unit


def dot(left, right):
    return jnp.dot(left, right, preferred_element_type=F32)


def dot_nt(left, right):
    return lax.dot_general(left, right, (((1,), (1,)), ((), ())), preferred_element_type=F32)


def dot_tn(left, right):
    return lax.dot_general(left, right, (((0,), (0,)), ((), ())), preferred_element_type=F32)


def pad_rows(rows, size):
    extra = size - rows.shape[0]
    if extra == 0:
        return rows
    return jnp.concatenate([rows, jnp.zeros((extra, rows.shape[1]), rows.dtype)], axis=0)


class Group:
    def __init__(self):
        self.dp = lax.axis_index("dp")
        self.own = lax.axis_index("tensor")
        self.y = self.own // 2
        self.core = self.own % 2
        self.mate = self.y * 2 + (1 - self.core)
        self.far = (1 - self.y) * 2 + self.core

    def greet(self, dp_peers=()):
        barrier = pltpu.get_barrier_semaphore()
        peers = [(self.dp, self.mate), (self.dp, self.far)] + [(peer, self.own) for peer in dp_peers]
        for peer in peers:
            pl.semaphore_signal(barrier, inc=1, device_id=peer, device_id_type=MESH)
        pl.semaphore_wait(barrier, len(peers))

    def share(self, turn):
        late = turn // 2
        other = ((turn + 1) // 2) % 2
        ybit = (1 - self.y) * (1 - late) + self.y * late
        core = self.core * (1 - other) + (1 - self.core) * other
        return ybit * 2 + core

    def copy(self, source, target, send, recv, peer):
        return pltpu.make_async_remote_copy(
            src_ref=source,
            dst_ref=target,
            send_sem=send,
            recv_sem=recv,
            device_id=(self.dp, peer),
            device_id_type=MESH,
        )


class Gather:
    def __init__(self, group, full, send, recv):
        self.group, self.full, self.send, self.recv = group, full, send, recv

    def _copy(self, seq, kind):
        group = self.group
        share = group.far if kind == 2 else group.own
        slot = self.full.at[seq, share]
        peer = group.far if kind == 0 else group.mate
        return group.copy(slot, slot, self.send.at[seq, kind], self.recv.at[seq, kind], peer)

    def start(self, seq):
        self._copy(seq, 0).start()
        self._copy(seq, 1).start()

    def wait(self, seq, turn):
        @pl.when(turn == 0)
        def _():
            self._copy(seq, 0).wait_recv()
            self._copy(seq, 2).start()

        @pl.when(turn == 1)
        def _():
            self._copy(seq, 2).wait_recv()

        @pl.when(turn == 2)
        def _():
            self._copy(seq, 1).wait_recv()

    def close(self, seq):
        for kind in range(3):
            self._copy(seq, kind).wait_send()


class Scatter:
    def __init__(self, group, buffers, send, recv):
        self.group = group
        self.outgoing, self.keep, self.near, self.cross, self.landed = buffers
        self.send, self.recv = send, recv

    def _near(self, seq, index):
        return self.group.copy(
            self.outgoing.at[seq, index],
            self.near.at[seq, index],
            self.send.at[seq, index],
            self.recv.at[seq, index],
            self.group.mate,
        )

    def _cross(self, seq):
        return self.group.copy(
            self.cross.at[seq],
            self.landed.at[seq],
            self.send.at[seq, 2],
            self.recv.at[seq, 2],
            self.group.far,
        )

    def put(self, seq, turn, terms):
        @pl.when((turn == 0) | (turn == 3))
        def _():
            self.keep[seq, turn // 3] = terms

        @pl.when((turn == 1) | (turn == 2))
        def _():
            self.outgoing[seq, turn - 1] = terms.astype(BF)
            self._near(seq, turn - 1).start()

        @pl.when(turn == 2)
        def _():
            self._near(seq, 0).wait_recv()
            total = self.keep[seq, 0] + self.near[seq, 0].astype(F32)
            self.cross[seq] = total.astype(BF)
            self._cross(seq).start()

    def take(self, seq):
        self._near(seq, 1).wait_recv()
        self._cross(seq).wait_recv()
        for index in range(2):
            self._near(seq, index).wait_send()
        self._cross(seq).wait_send()
        return (
            self.keep[seq, 1]
            + self.near[seq, 1].astype(F32)
            + self.landed[seq].astype(F32)
        )


def norm(rows):
    centred = rows - jnp.mean(rows, axis=-1, keepdims=True)
    inverse = lax.rsqrt(jnp.mean(centred * centred, axis=-1, keepdims=True) + EPSILON)
    return centred * inverse, inverse


def norm_back(grad, normed, inverse, gain):
    scaled = grad * gain
    return inverse * (
        scaled
        - jnp.mean(scaled, axis=-1, keepdims=True)
        - normed * jnp.mean(scaled * normed, axis=-1, keepdims=True)
    )


def sum_rows(rows):
    return jnp.sum(rows, axis=0, keepdims=True)


def lane_index(rows, lanes):
    return lax.broadcasted_iota(jnp.int32, (rows, lanes), 1)


def front(
    lengths, frames, cotangent, query_weight, key_weight, value_weight, query_bias, value_bias,
    out_weight, out_bias_row, first_gain_row, first_shift_row, up_weight, up_bias_row,
    down_weight, down_bias_row, second_gain_row, second_shift_row,
    layer_output, full_frames, projected, context, grad_attended, up_grad, down_grad, sums,
    wide_weight, wide_out, projection_bias, first_normed, first_inverse, first_full, hidden, activated,
    grad_second, grad_mixed, grad_hidden,
    outgoing, keep, near, cross, landed,
    gather_send, gather_recv, scatter_send, scatter_recv,
):
    seqs, share_rows, width = frames.shape
    rows = full_frames.shape[2]
    heads_width = query_weight.shape[0]
    lanes = wide_weight.shape[0] // 3
    heads = heads_width // HEAD_DIM
    length = 4 * rows
    group = Group()
    out_bias, first_gain, first_shift, down_bias, second_gain, second_shift, up_bias = (
        row[...].reshape(1, row.shape[0])
        for row in (
            out_bias_row, first_gain_row, first_shift_row, down_bias_row, second_gain_row,
            second_shift_row, up_bias_row,
        )
    )
    buffers = (outgoing, keep, near, cross, landed)
    gathers = [
        Gather(group, full, gather_send.at[index], gather_recv.at[index])
        for index, full in enumerate((full_frames, first_full, grad_mixed))
    ]
    scatters = [
        Scatter(group, buffers, scatter_send.at[index], scatter_recv.at[index]) for index in range(3)
    ]

    group.greet()

    def each(stage):
        def body(seq, carry):
            stage(seq)
            return carry

        lax.fori_loop(0, seqs, body, 0)

    def turns(step):
        def body(turn, carry):
            step(turn)
            return carry

        lax.fori_loop(0, 4, body, 0)

    def send_frames(seq):
        full_frames[seq, group.own] = pad_rows(frames[seq].astype(F32), rows).astype(BF)
        gathers[0].start(seq)

    each(send_frames)
    wide_weight[...] = jnp.zeros_like(wide_weight)
    for index, weight in enumerate((query_weight, key_weight, value_weight)):
        wide_weight[index * lanes : index * lanes + heads_width] = weight[...]
    wide_out[...] = jnp.zeros_like(wide_out)
    wide_out[:heads_width] = out_weight[...]
    projection_bias[...] = jnp.where(
        lane_index(1, 3 * lanes) == heads_width, HEAD_DIM**0.5, 0.0
    )
    projection_bias[:, :heads_width] = query_bias[...].reshape(1, heads_width)
    projection_bias[:, 2 * lanes : 2 * lanes + heads_width] = value_bias[...].reshape(1, heads_width)
    sums[...] = jnp.zeros_like(sums)
    up_grad[...] = jnp.zeros_like(up_grad)
    down_grad[...] = jnp.zeros_like(down_grad)

    def attention(seq):
        def project(step):
            turn = (1 - step // 2) * (3 - step) + (step // 2) * (step - 2)
            gathers[0].wait(seq, turn)
            share = group.share(turn)
            result = dot_nt(full_frames[seq, share], wide_weight[...]) + projection_bias[...]
            place = lax.broadcasted_iota(jnp.int32, (rows, lanes), 0)
            dead = (place >= share_rows) | (place + share * share_rows >= lengths[seq])
            flag = jnp.where(dead & (lane_index(rows, lanes) == heads_width), MASKED, 0.0)
            start = pl.multiple_of(share * rows, 16)
            projected[seq, pl.ds(start, rows), 0:lanes] = (
                result[:, :lanes].astype(BF) * HEAD_DIM ** (-0.5)
            ).astype(BF)
            projected[seq, pl.ds(start, rows), lanes : 2 * lanes] = (
                result[:, lanes : 2 * lanes] + flag
            ).astype(BF)
            projected[seq, pl.ds(start, rows), 2 * lanes : 3 * lanes] = result[:, 2 * lanes :].astype(BF)

        turns(project)

        def attend(turn):
            share = group.share(turn)
            start = pl.multiple_of(share * rows, 16)
            queries = projected[seq, pl.ds(start, rows), 0:lanes]
            lane = lane_index(rows, lanes)
            mixed = jnp.zeros((rows, lanes), F32)
            for head in range(heads):
                inside = lane // HEAD_DIM == head
                picked = jnp.where(inside | (lane == heads_width), queries, jnp.zeros_like(queries))
                scores = dot_nt(picked, projected[seq, :, lanes : 2 * lanes])
                exponent = jnp.exp(scores - jnp.max(scores, axis=-1, keepdims=True))
                weights = exponent * (1.0 / jnp.sum(exponent, axis=-1, keepdims=True))
                part = dot(weights.astype(BF), projected[seq, :, 2 * lanes : 3 * lanes])
                mixed = jnp.where(inside, part, mixed)
            mixed = mixed.astype(BF)
            context[seq, pl.ds(start, rows)] = mixed
            scatters[0].put(seq, turn, dot(mixed, wide_out[...]))

        turns(attend)

    each(attention)

    def first_norm(seq):
        attended = scatters[0].take(seq)
        normed, inverse = norm(full_frames[seq, group.own].astype(F32) + attended + out_bias)
        first_normed[seq] = normed
        first_inverse[seq] = inverse
        first_full[seq, group.own] = (normed * first_gain + first_shift).astype(BF)
        gathers[1].start(seq)

    each(first_norm)

    def feed(seq):
        def step(turn):
            gathers[1].wait(seq, turn)
            share = group.share(turn)
            start = pl.multiple_of(share * rows, 16)
            inner = dot(first_full[seq, share], up_weight[...]) + up_bias
            hidden[seq, pl.ds(start, rows)] = inner
            active = (0.5 * inner * (1.0 + lax.erf(inner * ROOT_HALF))).astype(BF)
            activated[seq, pl.ds(start, rows)] = active
            scatters[1].put(seq, turn, dot(active, down_weight[...]))

        turns(step)

    each(feed)

    def second_norm(seq):
        mixed = scatters[1].take(seq)
        first = first_normed[seq] * first_gain + first_shift
        normed, inverse = norm(first + mixed + down_bias)
        layer_output[seq] = (normed * second_gain + second_shift)[:share_rows].astype(BF)
        place = lax.broadcasted_iota(jnp.int32, (rows, width), 0)
        live = (place < share_rows) & (place + group.own * share_rows < lengths[seq])
        grad = jnp.where(live, pad_rows(cotangent[seq], rows), 0.0)
        back = norm_back(grad, normed, inverse, second_gain)
        sums[0:1] += sum_rows(grad * normed)
        sums[1:2] += sum_rows(grad)
        sums[2:3] += sum_rows(back)
        grad_second[seq] = back
        grad_mixed[seq, group.own] = back.astype(BF)
        gathers[2].start(seq)

    each(second_norm)

    def feed_back(seq):
        def step(turn):
            gathers[2].wait(seq, turn)
            share = group.share(turn)
            start = pl.multiple_of(share * rows, 16)
            grad_active = dot_nt(grad_mixed[seq, share], down_weight[...])
            inner = hidden[seq, pl.ds(start, rows)]
            slope = (
                0.5 * (1.0 + lax.erf(inner * ROOT_HALF))
                + inner * jnp.exp(-0.5 * inner * inner) * INVERSE_ROOT_TAU
            )
            grad = (grad_active * slope).astype(BF)
            grad_hidden[seq, pl.ds(start, rows)] = grad
            sums[6:7] += sum_rows(grad.astype(F32))
            scatters[2].put(seq, turn, dot_nt(grad, up_weight[...]))

        turns(step)

        def weights(step, carry):
            share = step
            start = pl.multiple_of(share * rows, 16)
            down_grad[...] += dot_tn(activated[seq, pl.ds(start, rows)], grad_mixed[seq, share])
            up_grad[...] += dot_tn(first_full[seq, share], grad_hidden[seq, pl.ds(start, rows)])
            return carry

        lax.fori_loop(0, 4, weights, 0)

    each(feed_back)

    def first_back(seq):
        grad = grad_second[seq] + scatters[2].take(seq)
        back = norm_back(grad, first_normed[seq], first_inverse[seq], first_gain)
        sums[3:4] += sum_rows(grad * first_normed[seq])
        sums[4:5] += sum_rows(grad)
        sums[5:6] += sum_rows(back)
        grad_attended[seq] = back

    each(first_back)

    def close(seq):
        for gather in gathers:
            gather.close(seq)

    each(close)


class Ring:
    def __init__(self, group, count, own, opening, landed, shared, sems):
        self.group, self.count, self.steps = group, count, count - 1
        self.own, self.opening, self.landed, self.shared = own, opening, landed, shared
        self.add_send, self.add_recv, self.share_send, self.share_recv = sems
        self.rows = own.shape[0] // (2 * count)
        self.place, self.right, self.left = ring_peers(group.dp, count)

    def _own(self, way, step):
        shift = self.count - 1 - step if way == 0 else 1 + step
        chunk = (self.place + shift) % self.count
        start = pl.multiple_of((2 * chunk + way) * self.rows, 16)
        return self.own[pl.ds(start, self.rows)]

    def _copy(self, source, target, send, recv, way):
        return pltpu.make_async_remote_copy(
            src_ref=source,
            dst_ref=target,
            send_sem=send,
            recv_sem=recv,
            device_id=(self.right if way == 0 else self.left, self.group.own),
            device_id_type=MESH,
        )

    def _add(self, way, step, source=None):
        target = self.landed.at[way, step]
        return self._copy(
            target if source is None else source,
            target,
            self.add_send.at[way, step],
            self.add_recv.at[way, step],
            way,
        )

    def _share(self, way, step):
        shift = self.count - step if way == 0 else step
        slot = self.shared.at[(self.place + shift) % self.count, way]
        return self._copy(
            slot, slot, self.share_send.at[way, step], self.share_recv.at[way, step], way
        )

    def open(self):
        for way in range(2):
            self.opening[way] = self._own(way, 0).astype(BF)
            self._add(way, 0, self.opening.at[way]).start()

    def advance(self, step):
        last = self.steps - 1
        for way in range(2):
            if step < self.steps:
                self._add(way, step).wait_recv()
                total = self.landed[way, step].astype(F32) + self._own(way, step + 1)
                if step < last:
                    self.landed[way, step] = total.astype(BF)
                    self._add(way, step + 1, self.landed.at[way, step]).start()
                else:
                    self.shared[self.place, way] = total.astype(BF)
                    self._share(way, 0).start()
            else:
                turn = step - self.steps
                self._share(way, turn).wait_recv()
                if turn < last:
                    self._share(way, turn + 1).start()

    def close(self):
        for way in range(2):
            for step in range(self.steps):
                self._add(way, step).wait_send()
                self._share(way, step).wait_send()


def ring_peers(index, count):
    odd = index % 2
    place = (1 - odd) * (index // 2) + odd * (count - 1 - index // 2)

    def at(spot):
        late = spot // (count // 2)
        return (1 - late) * 2 * spot + late * (2 * (count - 1 - spot) + 1)

    return place, at((place + 1) % count), at((place + count - 1) % count)


def halving_peers(index, count):
    peers = []
    bit = 1
    while bit < count:
        peers.append(index + bit * (1 - 2 * ((index // bit) % 2)))
        bit *= 2
    return peers


class Totals:
    def __init__(self, group, peers, outgoing, arriving, send, recv, shared):
        self.group, self.shared = group, shared
        self.outgoing, self.arriving, self.send, self.recv = outgoing, arriving, send, recv
        own = group.own
        self.peers = [(group.dp, group.mate), (group.dp, group.far)] + [(peer, own) for peer in peers]

    def _copy(self, level):
        return pltpu.make_async_remote_copy(
            src_ref=self.outgoing.at[level],
            dst_ref=self.arriving.at[level],
            send_sem=self.send.at[level],
            recv_sem=self.recv.at[level],
            device_id=self.peers[level],
            device_id_type=MESH,
        )

    def begin(self, level, rows):
        self.outgoing[level] = rows
        self._copy(level).start()

    def end(self, level):
        self._copy(level).wait()
        other = self.arriving[level]
        if level < 2:
            place = lax.broadcasted_iota(jnp.int32, other.shape, 0)
            other = jnp.where(place < self.shared, other, 0.0)
        return self.outgoing[level] + other


def rear(
    count,
    attended_in, full_frames, projected, context, query_weight, key_weight, value_weight, out_weight,
    up_grad, down_grad, front_sums,
    input_grad, *refs,
):
    outs, refs = refs[: 4 if count else 2], refs[4 if count else 2 :]
    (
        wide_weight, wide_out, grad_full, grad_context, grad_projected, total,
        outgoing, keep, near, cross, landed,
        gather_send, gather_recv, scatter_send, scatter_recv,
    ), refs = refs[:15], refs[15:]
    seqs, rows, width = attended_in.shape
    share_rows = input_grad.shape[1]
    heads_width = query_weight.shape[0]
    lanes = wide_weight.shape[0] // 3
    heads = heads_width // HEAD_DIM
    length = 4 * rows
    group = Group()
    gather = Gather(group, grad_full, gather_send, gather_recv)
    scatter = Scatter(group, (outgoing, keep, near, cross, landed), scatter_send, scatter_recv)
    if count:
        sums = outs[3]
        heads_grad, opening, ring_landed, ring_shared = refs[:4]
        add_send, add_recv, share_send, share_recv, out_sem = refs[4:9]
        small_out, small_in, small_send, small_recv = refs[9:13]
        _, right, left = ring_peers(group.dp, count)
        pairs = halving_peers(group.dp, count)
        group.greet([right, left] + pairs)
        rings = [
            Ring(
                group,
                count,
                own,
                opening.at[index],
                ring_landed.at[index],
                ring_shared.at[index],
                [sem.at[index] for sem in (add_send, add_recv, share_send, share_recv)],
            )
            for index, own in enumerate((up_grad, down_grad, heads_grad))
        ]
        totals = Totals(group, pairs, small_out, small_in, small_send, small_recv, 6)
    else:
        heads_grad, sums = outs
        group.greet()
    ahead = [0]

    def poll():
        if count and ahead[0] < 2 * (count - 1):
            for ring in rings[:2]:
                ring.advance(ahead[0])
            ahead[0] += 1

    def turns(step):
        def body(turn, carry):
            step(turn)
            return carry

        lax.fori_loop(0, 4, body, 0)

    for seq in range(seqs):
        grad_full[seq, group.own] = attended_in[seq].astype(BF)
        gather.start(seq)
    if count:
        for ring in rings[:2]:
            ring.open()
        totals.begin(0, front_sums[...])
    wide_weight[...] = jnp.zeros_like(wide_weight)
    for index, weight in enumerate((query_weight, key_weight, value_weight)):
        wide_weight[index * lanes : index * lanes + heads_width] = weight[...]
    wide_out[...] = jnp.zeros_like(wide_out)
    wide_out[:heads_width] = out_weight[...]
    heads_grad[...] = jnp.zeros_like(heads_grad)
    sums[...] = jnp.zeros_like(sums)

    for seq in range(seqs):

        def step(turn):
            gather.wait(seq, turn)
            share = group.share(turn)
            start = pl.multiple_of(share * rows, 16)
            grad_context[pl.ds(start, rows)] = dot_nt(grad_full[seq, share], wide_out[...]).astype(BF)
            heads_grad[3 * heads_width :] += dot_tn(
                context[seq, pl.ds(start, rows)], grad_full[seq, share]
            )[:heads_width]

        turns(step)
        poll()
        total[...] = jnp.zeros_like(total)

        def head_step(head):
            lane = lane_index(length, lanes)
            inside = lane // HEAD_DIM == head
            queries = projected[seq, :, 0:lanes]
            keys = projected[seq, :, lanes : 2 * lanes]
            values = projected[seq, :, 2 * lanes : 3 * lanes]
            picked = jnp.where(inside | (lane == heads_width), queries, jnp.zeros_like(queries))
            scores = dot_nt(keys, picked)
            exponent = jnp.exp(scores - jnp.max(scores, axis=0, keepdims=True))
            weights = exponent * (1.0 / jnp.sum(exponent, axis=0, keepdims=True))
            grads = grad_context[...]
            part = dot(weights.astype(BF), grads)
            total[:, 2 * lanes : 3 * lanes] = jnp.where(inside, part, total[:, 2 * lanes : 3 * lanes])
            slopes = weights * dot_nt(values, jnp.where(inside, grads, jnp.zeros_like(grads)))
            slopes = (slopes - weights * jnp.sum(slopes, axis=0, keepdims=True)).astype(BF)
            part = dot(slopes, queries)
            total[:, lanes : 2 * lanes] = jnp.where(inside, part, total[:, lanes : 2 * lanes])
            part = dot_tn(slopes, keys) * HEAD_DIM ** (-0.5)
            total[:, 0:lanes] = jnp.where(inside, part, total[:, 0:lanes])

        for head in range(heads):
            head_step(head)
            poll()

        def finish(turn):
            share = group.share(turn)
            start = pl.multiple_of(share * rows, 16)
            grads = total[pl.ds(start, rows)].astype(BF)
            grad_projected[pl.ds(start, rows)] = grads
            sums[7:8] += sum_rows(grads.astype(F32))
            scatter.put(seq, turn, dot(grads, wide_weight[...]))

        turns(finish)
        poll()

        def weights(share, carry):
            start = pl.multiple_of(share * rows, 16)
            for index in range(3):
                heads_grad[index * heads_width : (index + 1) * heads_width] += dot_tn(
                    grad_projected[pl.ds(start, rows), index * lanes : (index + 1) * lanes],
                    full_frames[seq, share],
                )[:heads_width]
            return carry

        lax.fori_loop(0, 4, weights, 0)
        poll()
        if count and seq == 0:
            totals.begin(1, totals.end(0))

    if count:
        rings[2].open()
        place = lax.broadcasted_iota(jnp.int32, front_sums.shape, 0)
        rows_sum = totals.end(1)
        totals.begin(2, jnp.where(place == 7, sums[...], rows_sum))
    else:
        sums[:7] = front_sums[:7]

    for seq in range(seqs):
        input_grad[seq] = (scatter.take(seq) + attended_in[seq])[:share_rows]
        gather.close(seq)

    if count:
        level = 2
        last = len(pairs) + 1
        for step in range(2 * (count - 1)):
            poll()
            rings[2].advance(step)
            if step % 3 == 2 and level <= last:
                rows_sum = totals.end(level)
                level += 1
                if level <= last:
                    totals.begin(level, rows_sum)
                else:
                    sums[...] = rows_sum
        while ahead[0] < 2 * (count - 1):
            poll()
        copies = [
            pltpu.make_async_copy(ring_shared.at[index], outs[index], out_sem.at[index])
            for index in range(3)
        ]
        for copy in copies:
            copy.start()
        for ring in rings:
            ring.close()
        for copy in copies:
            copy.wait()


VMEM_SPEC = pl.BlockSpec(memory_space=pltpu.VMEM)
ANY_SPEC = pl.BlockSpec(memory_space=pl.ANY)


def group_scratch(seqs, rows, width):
    return [
        pltpu.VMEM((seqs, 2, rows, width), BF),
        pltpu.VMEM((seqs, 2, rows, width), F32),
        pltpu.VMEM((seqs, 2, rows, width), BF),
        pltpu.VMEM((seqs, rows, width), BF),
        pltpu.VMEM((seqs, rows, width), BF),
    ]


def shards(
    frames,
    cotangent,
    lengths,
    query_weight,
    query_bias,
    key_weight,
    value_weight,
    value_bias,
    out_weight,
    out_bias,
    first_gain,
    first_shift,
    up_weight,
    up_bias,
    down_weight,
    down_bias,
    second_gain,
    second_shift,
):
    seqs, share_rows, width = frames.shape
    rows = up_to(share_rows, 16)
    length = 4 * rows
    heads_width = query_weight.shape[1]
    inner = up_weight.shape[1]
    lanes = up_to(heads_width + 1, 128)
    query_rows, key_rows, value_rows = query_weight.T, key_weight.T, value_weight.T
    shape = jax.ShapeDtypeStruct
    (
        layer_output, full_frames, projected, context, grad_attended, up_grad, down_grad, sums,
    ) = pl.pallas_call(
        front,
        out_shape=[
            shape(frames.shape, BF),
            shape((seqs, 4, rows, width), BF),
            shape((seqs, length, 3 * lanes), BF),
            shape((seqs, length, lanes), BF),
            shape((seqs, rows, width), F32),
            shape(up_weight.shape, F32),
            shape(down_weight.shape, F32),
            shape((8, width), F32),
        ],
        in_specs=[pl.BlockSpec(memory_space=pltpu.SMEM)] + [VMEM_SPEC] * 17,
        out_specs=[VMEM_SPEC] * 8,
        scratch_shapes=[
            pltpu.VMEM((3 * lanes, width), BF),
            pltpu.VMEM((lanes, width), BF),
            pltpu.VMEM((1, 3 * lanes), F32),
            pltpu.VMEM((seqs, rows, width), F32),
            pltpu.VMEM((seqs, rows, 1), F32),
            pltpu.VMEM((seqs, 4, rows, width), BF),
            pltpu.VMEM((seqs, length, inner), F32),
            pltpu.VMEM((seqs, length, inner), BF),
            pltpu.VMEM((seqs, rows, width), F32),
            pltpu.VMEM((seqs, 4, rows, width), BF),
            pltpu.VMEM((seqs, length, inner), BF),
        ]
        + group_scratch(seqs, rows, width)
        + [pltpu.SemaphoreType.DMA((3, seqs, 3))] * 4,
        compiler_params=pltpu.CompilerParams(
            collective_id=0, has_side_effects=True, vmem_limit_bytes=VMEM_BYTES
        ),
        name="front",
    )(
        lengths, frames, cotangent, query_rows, key_rows, value_rows, query_bias, value_bias,
        out_weight, out_bias, first_gain, first_shift, up_weight, up_bias,
        down_weight, down_bias, second_gain, second_shift,
    )
    count = lax.axis_size("dp")
    ringed = count % 2 == 0 and count & (count - 1) == 0 and width % (32 * count) == 0
    half = width // (2 * count)
    levels = 2 + count.bit_length() - 1
    grads = [shape((count, 2, half, width), BF)] * 3 if ringed else [shape((4 * heads_width, width), F32)]
    outs = pl.pallas_call(
        functools.partial(rear, count if ringed else 0),
        out_shape=[shape(frames.shape, F32)] + grads + [shape((8, width), F32)],
        in_specs=[VMEM_SPEC] * 8 + [VMEM_SPEC if ringed else ANY_SPEC] * 2 + [VMEM_SPEC],
        out_specs=[VMEM_SPEC] + [ANY_SPEC if ringed else VMEM_SPEC] * len(grads) + [VMEM_SPEC],
        scratch_shapes=[
            pltpu.VMEM((3 * lanes, width), BF),
            pltpu.VMEM((lanes, width), BF),
            pltpu.VMEM((seqs, 4, rows, width), BF),
            pltpu.VMEM((length, lanes), BF),
            pltpu.VMEM((length, 3 * lanes), BF),
            pltpu.VMEM((length, 3 * lanes), F32),
        ]
        + group_scratch(seqs, rows, width)
        + [pltpu.SemaphoreType.DMA((seqs, 3))] * 4
        + (
            [
                pltpu.VMEM((4 * heads_width, width), F32),
                pltpu.VMEM((3, 2, half, width), BF),
                pltpu.VMEM((3, 2, count - 1, half, width), BF),
                pltpu.VMEM((3, count, 2, half, width), BF),
            ]
            + [pltpu.SemaphoreType.DMA((3, 2, count - 1))] * 4
            + [pltpu.SemaphoreType.DMA((3,))]
            + [pltpu.VMEM((levels, 8, width), F32)] * 2
            + [pltpu.SemaphoreType.DMA((levels,))] * 2
            if ringed
            else []
        ),
        compiler_params=pltpu.CompilerParams(
            collective_id=1, has_side_effects=True, vmem_limit_bytes=VMEM_BYTES
        ),
        name="rear",
    )(
        grad_attended, full_frames, projected, context, query_rows, key_rows, value_rows, out_weight,
        up_grad, down_grad, sums,
    )
    input_grad, sums = outs[0], outs[-1]
    if ringed:
        up_grad, down_grad, heads_grad = (
            grad.reshape(width, width).astype(F32) for grad in outs[1:4]
        )
    else:
        up_grad, down_grad, heads_grad = lax.psum((up_grad, down_grad, outs[1]), "dp")
        sums = lax.psum(sums, "dp")
        sums = jnp.concatenate([lax.psum(sums[:6], "tensor"), sums[6:]])
    query_grad, key_grad, value_grad, out_grad = (
        heads_grad[index * heads_width : (index + 1) * heads_width] for index in range(4)
    )
    return (
        layer_output,
        input_grad,
        query_grad.T,
        sums[7, :heads_width],
        key_grad.T,
        value_grad.T,
        sums[7, 2 * lanes : 2 * lanes + heads_width],
        out_grad,
        sums[5],
        sums[3],
        sums[4],
        up_grad,
        sums[6],
        down_grad,
        sums[2],
        sums[0],
        sums[1],
    )


def solution(mesh):
    return jax.shard_map(
        shards,
        mesh=mesh,
        in_specs=(
            P("dp", "tensor", None),
            P("dp", "tensor", None),
            P("dp"),
            P(None, "tensor"),
            P("tensor"),
            P(None, "tensor"),
            P(None, "tensor"),
            P("tensor"),
            P("tensor", None),
            P(),
            P(),
            P(),
            P(None, "tensor"),
            P("tensor"),
            P("tensor", None),
            P(),
            P(),
            P(),
        ),
        out_specs=(
            P("dp", "tensor", None),
            P("dp", "tensor", None),
            P(None, "tensor"),
            P("tensor"),
            P(None, "tensor"),
            P(None, "tensor"),
            P("tensor"),
            P("tensor", None),
            P(),
            P(),
            P(),
            P(None, "tensor"),
            P("tensor"),
            P("tensor", None),
            P(),
            P(),
            P(),
        ),
        check_vma=False,
    )
```

```python
import functools
import types

import jax
import jax.numpy as jnp
from jax import lax
from jax.experimental import pallas as pl
from jax.experimental.pallas import tpu as pltpu
from jax.sharding import PartitionSpec as P

MESH = pl.DeviceIdType.MESH
HEAD_DIM = 64
EPSILON = 1e-05
ROOT_HALF = 0.7071067811865476
INVERSE_ROOT_TAU = 0.3989422804014327
MASKED = -1e30
VMEM_BYTES = 62 << 20
BF = jnp.bfloat16
F32 = jnp.float32


def up_to(size, unit):
    return (size + unit - 1) // unit * unit


def dot(left, right):
    return jnp.dot(left, right, preferred_element_type=F32)


def dot_nt(left, right):
    return lax.dot_general(left, right, (((1,), (1,)), ((), ())), preferred_element_type=F32)


def dot_tn(left, right):
    return lax.dot_general(left, right, (((0,), (0,)), ((), ())), preferred_element_type=F32)


def pad_rows(rows, size):
    extra = size - rows.shape[0]
    if extra == 0:
        return rows
    return jnp.concatenate([rows, jnp.zeros((extra, rows.shape[1]), rows.dtype)], axis=0)


class Group:
    def __init__(self):
        self.dp = lax.axis_index("dp")
        self.own = lax.axis_index("tensor")
        self.y = self.own // 2
        self.core = self.own % 2
        self.mate = self.y * 2 + (1 - self.core)
        self.far = (1 - self.y) * 2 + self.core

    def greet(self, dp_peers):
        barrier = pltpu.get_barrier_semaphore()
        peers = [(self.dp, self.mate), (self.dp, self.far)] + [(peer, self.own) for peer in dp_peers]
        for peer in peers:
            pl.semaphore_signal(barrier, inc=1, device_id=peer, device_id_type=MESH)
        return lambda: pl.semaphore_wait(barrier, len(peers))

    def share(self, turn):
        late = turn // 2
        other = ((turn + 1) // 2) % 2
        ybit = (1 - self.y) * (1 - late) + self.y * late
        core = self.core * (1 - other) + (1 - self.core) * other
        return ybit * 2 + core

    def copy(self, source, target, send, recv, peer):
        return pltpu.make_async_remote_copy(
            src_ref=source,
            dst_ref=target,
            send_sem=send,
            recv_sem=recv,
            device_id=(self.dp, peer),
            device_id_type=MESH,
        )


class Gather:
    def __init__(self, group, full, send, recv):
        self.group, self.full, self.send, self.recv = group, full, send, recv

    def _copy(self, seq, kind):
        group = self.group
        share = group.far if kind == 2 else group.own
        slot = self.full.at[seq, share]
        peer = group.far if kind == 0 else group.mate
        return group.copy(slot, slot, self.send.at[seq, kind], self.recv.at[seq, kind], peer)

    def start(self, seq):
        self._copy(seq, 0).start()
        self._copy(seq, 1).start()

    def wait(self, seq, turn):
        @pl.when(turn == 0)
        def _():
            self._copy(seq, 0).wait_recv()
            self._copy(seq, 2).start()

        @pl.when(turn == 1)
        def _():
            self._copy(seq, 2).wait_recv()

        @pl.when(turn == 2)
        def _():
            self._copy(seq, 1).wait_recv()

    def close(self, seq):
        for kind in range(3):
            self._copy(seq, kind).wait_send()


class Scatter:
    def __init__(self, group, buffers, send, recv):
        self.group = group
        self.outgoing, self.keep, self.near, self.cross, self.landed = buffers
        self.send, self.recv = send, recv

    def _near(self, seq, index):
        return self.group.copy(
            self.outgoing.at[seq, index],
            self.near.at[seq, index],
            self.send.at[seq, index],
            self.recv.at[seq, index],
            self.group.mate,
        )

    def _cross(self, seq):
        return self.group.copy(
            self.cross.at[seq],
            self.landed.at[seq],
            self.send.at[seq, 2],
            self.recv.at[seq, 2],
            self.group.far,
        )

    def put(self, seq, turn, terms):
        @pl.when((turn == 0) | (turn == 3))
        def _():
            self.keep[seq, turn // 3] = terms

        @pl.when((turn == 1) | (turn == 2))
        def _():
            self.outgoing[seq, turn - 1] = terms.astype(BF)
            self._near(seq, turn - 1).start()

        @pl.when(turn == 2)
        def _():
            self._near(seq, 0).wait_recv()
            total = self.keep[seq, 0] + self.near[seq, 0].astype(F32)
            self.cross[seq] = total.astype(BF)
            self._cross(seq).start()

    def take(self, seq):
        self._near(seq, 1).wait_recv()
        self._cross(seq).wait_recv()
        for index in range(2):
            self._near(seq, index).wait_send()
        self._cross(seq).wait_send()
        return (
            self.keep[seq, 1]
            + self.near[seq, 1].astype(F32)
            + self.landed[seq].astype(F32)
        )


def norm(rows):
    centred = rows - jnp.mean(rows, axis=-1, keepdims=True)
    inverse = lax.rsqrt(jnp.mean(centred * centred, axis=-1, keepdims=True) + EPSILON)
    return centred * inverse, inverse


def norm_back(grad, normed, inverse, gain):
    scaled = grad * gain
    return inverse * (
        scaled
        - jnp.mean(scaled, axis=-1, keepdims=True)
        - normed * jnp.mean(scaled * normed, axis=-1, keepdims=True)
    )


def sum_rows(rows):
    return jnp.sum(rows, axis=0, keepdims=True)


def lane_index(rows, lanes):
    return lax.broadcasted_iota(jnp.int32, (rows, lanes), 1)


class Ring:
    def __init__(self, group, count, own, opening, landed, shared, sems, first, rows):
        self.group, self.count, self.steps = group, count, count - 1
        self.own, self.opening, self.landed, self.shared = own, opening, landed, shared
        self.add_send, self.add_recv, self.share_send, self.share_recv = sems
        self.half = own.shape[0] // (2 * count)
        self.first, self.rows = first, rows
        self.span = pl.ds(first, rows)
        self.place, self.right, self.left = ring_peers(group.dp, count)

    def _own(self, way, step):
        shift = self.count - 1 - step if way == 0 else 1 + step
        chunk = (self.place + shift) % self.count
        start = pl.multiple_of((2 * chunk + way) * self.half + self.first, 16)
        return self.own[pl.ds(start, self.rows)]

    def _copy(self, source, target, send, recv, way):
        return pltpu.make_async_remote_copy(
            src_ref=source,
            dst_ref=target,
            send_sem=send,
            recv_sem=recv,
            device_id=(self.right if way == 0 else self.left, self.group.own),
            device_id_type=MESH,
        )

    def _add(self, way, step, source=None):
        target = self.landed.at[way, step, self.span]
        return self._copy(
            target if source is None else source,
            target,
            self.add_send.at[way, step],
            self.add_recv.at[way, step],
            way,
        )

    def _share(self, way, step):
        shift = self.count - step if way == 0 else step
        slot = self.shared.at[(self.place + shift) % self.count, way, self.span]
        return self._copy(
            slot, slot, self.share_send.at[way, step], self.share_recv.at[way, step], way
        )

    def open(self):
        for way in range(2):
            self.opening[way, self.span] = self._own(way, 0).astype(BF)
            self._add(way, 0, self.opening.at[way, self.span]).start()

    def advance(self, step):
        last = self.steps - 1
        for way in range(2):
            if step < self.steps:
                self._add(way, step).wait_recv()
                total = self.landed[way, step, self.span].astype(F32) + self._own(way, step + 1)
                if step < last:
                    self.landed[way, step, self.span] = total.astype(BF)
                    self._add(way, step + 1, self.landed.at[way, step, self.span]).start()
                else:
                    self.shared[self.place, way, self.span] = total.astype(BF)
                    self._share(way, 0).start()
            else:
                turn = step - self.steps
                self._share(way, turn).wait_recv()
                if turn < last:
                    self._share(way, turn + 1).start()

    def close(self):
        for way in range(2):
            for step in range(self.steps):
                self._add(way, step).wait_send()
                self._share(way, step).wait_send()


def ring_peers(index, count):
    odd = index % 2
    place = (1 - odd) * (index // 2) + odd * (count - 1 - index // 2)

    def at(spot):
        late = spot // (count // 2)
        return (1 - late) * 2 * spot + late * (2 * (count - 1 - spot) + 1)

    return place, at((place + 1) % count), at((place + count - 1) % count)


def halving_peers(index, count):
    peers = []
    bit = 1
    while bit < count:
        peers.append(index + bit * (1 - 2 * ((index // bit) % 2)))
        bit *= 2
    return peers


class Totals:
    def __init__(self, group, peers, outgoing, arriving, send, recv, shared):
        self.group, self.shared = group, shared
        self.outgoing, self.arriving, self.send, self.recv = outgoing, arriving, send, recv
        own = group.own
        self.peers = [(group.dp, group.mate), (group.dp, group.far)] + [(peer, own) for peer in peers]

    def _copy(self, level):
        return pltpu.make_async_remote_copy(
            src_ref=self.outgoing.at[level],
            dst_ref=self.arriving.at[level],
            send_sem=self.send.at[level],
            recv_sem=self.recv.at[level],
            device_id=self.peers[level],
            device_id_type=MESH,
        )

    def begin(self, level, rows):
        self.outgoing[level] = rows
        self._copy(level).start()

    def end(self, level):
        self._copy(level).wait()
        other = self.arriving[level]
        if level < 2:
            place = lax.broadcasted_iota(jnp.int32, other.shape, 0)
            other = jnp.where(place < self.shared, other, 0.0)
        return self.outgoing[level] + other


def layer(count, names, *refs):
    r = types.SimpleNamespace(**dict(zip(names, refs)))
    seqs, share_rows, width = r.frames.shape
    rows = r.full_frames.shape[2]
    length = 4 * rows
    heads_width = r.query_weight.shape[0]
    lanes = r.wide_weight.shape[0] // 3
    heads = heads_width // HEAD_DIM
    group = Group()
    pairs = []
    ring_sides = []
    if count:
        pairs = halving_peers(group.dp, count)
        ring_sides = list(ring_peers(group.dp, count)[1:])
    met = group.greet(ring_sides + pairs)

    out_bias, first_gain, first_shift, down_bias, second_gain, second_shift, up_bias = (
        row[...].reshape(1, row.shape[0])
        for row in (
            r.out_bias, r.first_gain, r.first_shift, r.down_bias, r.second_gain, r.second_shift, r.up_bias,
        )
    )
    buffers = (r.outgoing, r.keep, r.near, r.cross, r.landed)
    gathers = [
        Gather(group, full, r.gather_send.at[index], r.gather_recv.at[index])
        for index, full in enumerate((r.full_frames, r.first_full, r.grad_mixed, r.grad_full))
    ]
    scatters = [
        Scatter(group, buffers, r.scatter_send.at[index], r.scatter_recv.at[index])
        for index in range(4)
    ]
    grad_total = r.hidden.at[0]
    heads_grad = r.hidden.at[1, pl.ds(0, 4 * heads_width)]
    grad_projected = r.activated.at[0]

    def each(stage):
        def body(seq, carry):
            stage(seq)
            return carry

        lax.fori_loop(0, seqs, body, 0)

    def turns(step):
        def body(turn, carry):
            step(turn)
            return carry

        lax.fori_loop(0, 4, body, 0)

    def at_share(share):
        return pl.ds(pl.multiple_of(share * rows, 16), rows)

    def place_frames(seq):
        r.full_frames[seq, group.own] = pad_rows(r.frames[seq].astype(F32), rows).astype(BF)

    each(place_frames)
    met()
    each(gathers[0].start)
    r.wide_weight[...] = jnp.zeros_like(r.wide_weight)
    for index, weight in enumerate((r.query_weight, r.key_weight, r.value_weight)):
        r.wide_weight[index * lanes : index * lanes + heads_width] = weight[...]
    r.wide_out[...] = jnp.zeros_like(r.wide_out)
    r.wide_out[:heads_width] = r.out_weight[...]
    r.projection_bias[...] = jnp.where(
        lane_index(1, 3 * lanes) == heads_width, HEAD_DIM**0.5, 0.0
    )
    r.projection_bias[:, :heads_width] = r.query_bias[...].reshape(1, heads_width)
    r.projection_bias[:, 2 * lanes : 2 * lanes + heads_width] = r.value_bias[...].reshape(1, heads_width)
    r.rows_sum[...] = jnp.zeros_like(r.rows_sum)

    def attention(seq):
        def project(step):
            turn = (1 - step // 2) * (3 - step) + (step // 2) * (step - 2)
            gathers[0].wait(seq, turn)
            share = group.share(turn)
            result = dot_nt(r.full_frames[seq, share], r.wide_weight[...]) + r.projection_bias[...]
            place = lax.broadcasted_iota(jnp.int32, (rows, lanes), 0)
            dead = (place >= share_rows) | (place + share * share_rows >= r.lengths[seq])
            flag = jnp.where(dead & (lane_index(rows, lanes) == heads_width), MASKED, 0.0)
            r.projected[seq, at_share(share), 0:lanes] = (
                result[:, :lanes].astype(BF) * HEAD_DIM ** (-0.5)
            ).astype(BF)
            r.projected[seq, at_share(share), lanes : 2 * lanes] = (
                result[:, lanes : 2 * lanes] + flag
            ).astype(BF)
            r.projected[seq, at_share(share), 2 * lanes : 3 * lanes] = result[:, 2 * lanes :].astype(BF)

        turns(project)

        def attend(turn):
            share = group.share(turn)
            queries = r.projected[seq, at_share(share), 0:lanes]
            lane = lane_index(rows, lanes)
            mixed = jnp.zeros((rows, lanes), F32)
            for head in range(heads):
                inside = lane // HEAD_DIM == head
                picked = jnp.where(inside | (lane == heads_width), queries, jnp.zeros_like(queries))
                scores = dot_nt(picked, r.projected[seq, :, lanes : 2 * lanes])
                exponent = jnp.exp(scores - jnp.max(scores, axis=-1, keepdims=True))
                weights = exponent * (1.0 / jnp.sum(exponent, axis=-1, keepdims=True))
                part = dot(weights.astype(BF), r.projected[seq, :, 2 * lanes : 3 * lanes])
                mixed = jnp.where(inside, part, mixed)
            mixed = mixed.astype(BF)
            r.context[seq, at_share(share)] = mixed
            scatters[0].put(seq, turn, dot(mixed, r.wide_out[...]))

        turns(attend)

    each(attention)

    def first_norm(seq):
        attended = scatters[0].take(seq)
        normed, inverse = norm(r.full_frames[seq, group.own].astype(F32) + attended + out_bias)
        r.first_normed[seq] = normed
        r.first_inverse[seq] = inverse
        r.first_full[seq, group.own] = (normed * first_gain + first_shift).astype(BF)
        gathers[1].start(seq)

    each(first_norm)

    def feed(seq):
        def step(turn):
            gathers[1].wait(seq, turn)
            share = group.share(turn)
            inner = dot(r.first_full[seq, share], r.up_weight[...]) + up_bias
            r.hidden[seq, at_share(share)] = inner
            active = (0.5 * inner * (1.0 + lax.erf(inner * ROOT_HALF))).astype(BF)
            r.activated[seq, at_share(share)] = active
            scatters[1].put(seq, turn, dot(active, r.down_weight[...]))

        turns(step)

    each(feed)

    def second_norm(seq):
        mixed = scatters[1].take(seq)
        first = r.first_normed[seq] * first_gain + first_shift
        normed, inverse = norm(first + mixed + down_bias)
        place = lax.broadcasted_iota(jnp.int32, (rows, width), 0)
        live = (place < share_rows) & (place + group.own * share_rows < r.lengths[seq])
        grad = jnp.where(live, pad_rows(r.cotangent[seq], rows), 0.0)
        back = norm_back(grad, normed, inverse, second_gain)
        r.grad_mixed[seq, group.own] = back.astype(BF)
        gathers[2].start(seq)
        r.grad_rows[seq] = back
        r.layer_output[seq] = (normed * second_gain + second_shift)[:share_rows].astype(BF)
        r.rows_sum[0:1] += sum_rows(grad * normed)
        r.rows_sum[1:2] += sum_rows(grad)
        r.rows_sum[2:3] += sum_rows(back)

    each(second_norm)

    def feed_back(seq):
        def step(turn):
            gathers[2].wait(seq, turn)
            share = group.share(turn)
            grad_active = dot_nt(r.grad_mixed[seq, share], r.down_weight[...])
            inner = r.hidden[seq, at_share(share)]
            slope = (
                0.5 * (1.0 + lax.erf(inner * ROOT_HALF))
                + inner * jnp.exp(-0.5 * inner * inner) * INVERSE_ROOT_TAU
            )
            grad = (grad_active * slope).astype(BF)
            r.grad_hidden[seq, at_share(share)] = grad
            r.rows_sum[6:7] += sum_rows(grad.astype(F32))
            scatters[2].put(seq, turn, dot_nt(grad, r.up_weight[...]))

        turns(step)

    each(feed_back)

    def feed_weights(seq):
        down = dot_tn(r.activated[seq], r.grad_mixed[seq].reshape(length, width))
        r.down_grad[...] = down if seq == 0 else r.down_grad[...] + down
        up = dot_tn(r.first_full[seq].reshape(length, width), r.grad_hidden[seq])
        r.up_grad[...] = up if seq == 0 else r.up_grad[...] + up

    def first_back(seq):
        grad = r.grad_rows[seq] + scatters[2].take(seq)
        normed = r.first_normed[seq]
        back = norm_back(grad, normed, r.first_inverse[seq], first_gain)
        r.grad_full[seq, group.own] = back.astype(BF)
        gathers[3].start(seq)
        r.grad_rows[seq] = back
        r.rows_sum[3:4] += sum_rows(grad * normed)
        r.rows_sum[4:5] += sum_rows(grad)
        r.rows_sum[5:6] += sum_rows(back)

    queue = []

    def poll(times=1):
        for _ in range(times):
            if queue:
                queue.pop(0)()

    for seq in range(seqs):
        feed_weights(seq)
        if seq == seqs - 1 and count:
            half = width // (2 * count)

            def make_ring(index, own, first, size):
                return Ring(
                    group,
                    count,
                    own,
                    r.opening.at[index],
                    r.ring_landed.at[index],
                    r.ring_shared.at[index],
                    [
                        sem.at[index, first // 16]
                        for sem in (r.add_send, r.add_recv, r.share_send, r.share_recv)
                    ],
                    first,
                    size,
                )

            rings = [make_ring(0, r.up_grad, 0, half), make_ring(1, r.down_grad, 0, half)]
            late_rings = [make_ring(2, heads_grad, first, 16) for first in range(0, half, 16)]
            for ring in rings:
                ring.open()
            for step in range(2 * (count - 1)):
                for ring in rings:
                    queue.append(functools.partial(ring.advance, step))
        first_back(seq)
    poll()
    if count:
        totals = Totals(
            group, pairs, r.small_out, r.small_in, r.small_send, r.small_recv, 6
        )
        totals.begin(0, r.rows_sum[...])
    heads_grad[...] = jnp.zeros_like(heads_grad)

    for seq in range(seqs):

        def step(turn):
            gathers[3].wait(seq, turn)
            share = group.share(turn)
            r.grad_context[at_share(share)] = dot_nt(r.grad_full[seq, share], r.wide_out[...]).astype(BF)
            heads_grad[3 * heads_width :] += dot_tn(
                r.context[seq, at_share(share)], r.grad_full[seq, share]
            )[:heads_width]

        turns(step)
        poll(2)
        grad_total[...] = jnp.zeros_like(grad_total)
        keys = r.projected[seq, :, lanes : 2 * lanes]
        values = r.projected[seq, :, 2 * lanes : 3 * lanes]
        inside_rows = lane_index(length, lanes) // HEAD_DIM
        for head in range(heads):
            for start in range(0, length, 512):
                size = min(512, length - start)
                span = slice(start, start + size)
                lane = lane_index(size, lanes)
                inside = lane // HEAD_DIM == head
                queries = r.projected[seq, span, 0:lanes]
                picked = jnp.where(inside | (lane == heads_width), queries, jnp.zeros_like(queries))
                scores = dot_nt(keys, picked)
                exponent = jnp.exp(scores - jnp.max(scores, axis=0, keepdims=True))
                weights = exponent * (1.0 / jnp.sum(exponent, axis=0, keepdims=True))
                grads = r.grad_context[span]
                part = dot(weights.astype(BF), grads)
                grad_total[:, 2 * lanes : 3 * lanes] += jnp.where(inside_rows == head, part, 0.0)
                slopes = weights * dot_nt(values, jnp.where(inside, grads, jnp.zeros_like(grads)))
                slopes = (slopes - weights * jnp.sum(slopes, axis=0, keepdims=True)).astype(BF)
                part = dot(slopes, queries)
                grad_total[:, lanes : 2 * lanes] += jnp.where(inside_rows == head, part, 0.0)
                part = dot_tn(slopes, keys) * HEAD_DIM ** (-0.5)
                grad_total[span, 0:lanes] = jnp.where(inside, part, grad_total[span, 0:lanes])
                poll()

        def finish(turn):
            share = group.share(turn)
            grads = grad_total[at_share(share)].astype(BF)
            grad_projected[at_share(share)] = grads
            r.rows_sum[7:8] += sum_rows(grads.astype(F32))
            scatters[3].put(seq, turn, dot(grads, r.wide_weight[...]))

        turns(finish)
        poll(2)
        for index in range(3):
            heads_grad[index * heads_width : (index + 1) * heads_width] += dot_tn(
                grad_projected[:, index * lanes : (index + 1) * lanes],
                r.full_frames[seq].reshape(length, width),
            )[:heads_width]
        poll()
        if count and seq == 0:
            totals.begin(1, totals.end(0))

    if count:
        for ring in late_rings:
            ring.open()
        poll()
        place = lax.broadcasted_iota(jnp.int32, r.rows_sum.shape, 0)
        totals.begin(2, jnp.where(place == 7, r.rows_sum[...], totals.end(1)))

    for seq in range(seqs):
        if seq:
            poll(4)
        r.input_grad[seq] = (scatters[3].take(seq) + r.grad_rows[seq])[:share_rows]

    if count:
        poll(len(queue))
        copies = [
            pltpu.make_async_copy(r.ring_shared.at[index], out, r.out_sem.at[index])
            for index, out in enumerate((r.up_sum, r.down_sum, r.heads_sum))
        ]
        copies[0].start()
        copies[1].start()
        level = 2
        last = len(pairs) + 1
        for step in range(2 * (count - 1)):
            for ring in late_rings:
                ring.advance(step)
            if step % 3 == 2 and level <= last:
                rows_total = totals.end(level)
                level += 1
                if level <= last:
                    totals.begin(level, rows_total)
                else:
                    r.sums[...] = rows_total
        copies[2].start()
        for ring in rings + late_rings:
            ring.close()
    else:
        r.sums[...] = r.rows_sum[...]
        copies = [
            pltpu.make_async_copy(own, out, r.out_sem.at[index])
            for index, (own, out) in enumerate(
                ((r.up_grad, r.up_sum), (r.down_grad, r.down_sum), (heads_grad, r.heads_sum))
            )
        ]
        for copy in copies:
            copy.start()
    for seq in range(seqs):
        for gather in gathers:
            gather.close(seq)
    for copy in copies:
        copy.wait()


VMEM_SPEC = pl.BlockSpec(memory_space=pltpu.VMEM)
ANY_SPEC = pl.BlockSpec(memory_space=pl.ANY)


def shards(
    frames,
    cotangent,
    lengths,
    query_weight,
    query_bias,
    key_weight,
    value_weight,
    value_bias,
    out_weight,
    out_bias,
    first_gain,
    first_shift,
    up_weight,
    up_bias,
    down_weight,
    down_bias,
    second_gain,
    second_shift,
):
    seqs, share_rows, width = frames.shape
    rows = up_to(share_rows, 16)
    length = 4 * rows
    heads_width = query_weight.shape[1]
    inner = up_weight.shape[1]
    lanes = up_to(heads_width + 1, 128)
    shape = jax.ShapeDtypeStruct
    count = lax.axis_size("dp")
    ringed = count & (count - 1) == 0 and width % (32 * count) == 0
    half = width // (2 * count)
    levels = 2 + count.bit_length() - 1
    full = pltpu.VMEM((seqs, 4, rows, width), BF)
    part = pltpu.VMEM((seqs, rows, width), BF)
    stream = pltpu.VMEM((seqs, rows, width), F32)
    inputs = dict(
        lengths=lengths,
        frames=frames,
        cotangent=cotangent,
        query_weight=query_weight.T,
        query_bias=query_bias,
        key_weight=key_weight.T,
        value_weight=value_weight.T,
        value_bias=value_bias,
        out_weight=out_weight,
        out_bias=out_bias,
        first_gain=first_gain,
        first_shift=first_shift,
        up_weight=up_weight,
        up_bias=up_bias,
        down_weight=down_weight,
        down_bias=down_bias,
        second_gain=second_gain,
        second_shift=second_shift,
    )
    summed = (
        shape((count, 2, half, width), BF) if ringed else shape((width, width), F32)
    )
    outputs = dict(
        layer_output=shape(frames.shape, BF),
        input_grad=shape(frames.shape, F32),
        sums=shape((8, width), F32),
        up_sum=summed,
        down_sum=summed,
        heads_sum=summed,
    )
    scratch = dict(
        wide_weight=pltpu.VMEM((3 * lanes, width), BF),
        wide_out=pltpu.VMEM((lanes, width), BF),
        projection_bias=pltpu.VMEM((1, 3 * lanes), F32),
        rows_sum=pltpu.VMEM((8, width), F32),
        full_frames=full,
        first_full=full,
        grad_mixed=full,
        grad_full=full,
        projected=pltpu.VMEM((seqs, length, 3 * lanes), BF),
        context=pltpu.VMEM((seqs, length, lanes), BF),
        first_normed=stream,
        first_inverse=pltpu.VMEM((seqs, rows, 1), F32),
        grad_rows=stream,
        hidden=pltpu.VMEM((seqs, length, inner), F32),
        activated=pltpu.VMEM((seqs, length, inner), BF),
        grad_hidden=pltpu.VMEM((seqs, length, inner), BF),
        grad_context=pltpu.VMEM((length, lanes), BF),
        up_grad=pltpu.VMEM(up_weight.shape, F32),
        down_grad=pltpu.VMEM(down_weight.shape, F32),
        outgoing=pltpu.VMEM((seqs, 2, rows, width), BF),
        keep=pltpu.VMEM((seqs, 2, rows, width), F32),
        near=pltpu.VMEM((seqs, 2, rows, width), BF),
        cross=part,
        landed=part,
        gather_send=pltpu.SemaphoreType.DMA((4, seqs, 3)),
        gather_recv=pltpu.SemaphoreType.DMA((4, seqs, 3)),
        scatter_send=pltpu.SemaphoreType.DMA((4, seqs, 3)),
        scatter_recv=pltpu.SemaphoreType.DMA((4, seqs, 3)),
        out_sem=pltpu.SemaphoreType.DMA((3,)),
    )
    if ringed:
        ring_sem = pltpu.SemaphoreType.DMA((3, half // 16, 2, count - 1))
        scratch.update(
            opening=pltpu.VMEM((3, 2, half, width), BF),
            ring_landed=pltpu.VMEM((3, 2, count - 1, half, width), BF),
            ring_shared=pltpu.VMEM((3, count, 2, half, width), BF),
            add_send=ring_sem,
            add_recv=ring_sem,
            share_send=ring_sem,
            share_recv=ring_sem,
            small_out=pltpu.VMEM((levels, 8, width), F32),
            small_in=pltpu.VMEM((levels, 8, width), F32),
            small_send=pltpu.SemaphoreType.DMA((levels,)),
            small_recv=pltpu.SemaphoreType.DMA((levels,)),
        )
    outs = pl.pallas_call(
        functools.partial(layer, count if ringed else 0, [*inputs, *outputs, *scratch]),
        out_shape=list(outputs.values()),
        in_specs=[pl.BlockSpec(memory_space=pltpu.SMEM)] + [VMEM_SPEC] * (len(inputs) - 1),
        out_specs=[VMEM_SPEC] * 3 + [ANY_SPEC] * 3,
        scratch_shapes=list(scratch.values()),
        compiler_params=pltpu.CompilerParams(
            collective_id=0, has_side_effects=True, vmem_limit_bytes=VMEM_BYTES
        ),
        name="layer",
    )(*inputs.values())
    layer_output, input_grad, sums = outs[:3]
    if ringed:
        up_grad, down_grad, heads_grad = (
            grad.reshape(width, width).astype(F32) for grad in outs[3:]
        )
    else:
        up_grad, down_grad, heads_grad = lax.psum(tuple(outs[3:]), "dp")
        sums = lax.psum(sums, "dp")
        sums = jnp.concatenate([lax.psum(sums[:6], "tensor"), sums[6:]])
    query_grad, key_grad, value_grad, out_grad = (
        heads_grad[index * heads_width : (index + 1) * heads_width] for index in range(4)
    )
    return (
        layer_output,
        input_grad,
        query_grad.T,
        sums[7, :heads_width],
        key_grad.T,
        value_grad.T,
        sums[7, 2 * lanes : 2 * lanes + heads_width],
        out_grad,
        sums[5],
        sums[3],
        sums[4],
        up_grad,
        sums[6],
        down_grad,
        sums[2],
        sums[0],
        sums[1],
    )


def solution(mesh):
    return jax.shard_map(
        shards,
        mesh=mesh,
        in_specs=(
            P("dp", "tensor", None),
            P("dp", "tensor", None),
            P("dp"),
            P(None, "tensor"),
            P("tensor"),
            P(None, "tensor"),
            P(None, "tensor"),
            P("tensor"),
            P("tensor", None),
            P(),
            P(),
            P(),
            P(None, "tensor"),
            P("tensor"),
            P("tensor", None),
            P(),
            P(),
            P(),
        ),
        out_specs=(
            P("dp", "tensor", None),
            P("dp", "tensor", None),
            P(None, "tensor"),
            P("tensor"),
            P(None, "tensor"),
            P(None, "tensor"),
            P("tensor"),
            P("tensor", None),
            P(),
            P(),
            P(),
            P(None, "tensor"),
            P("tensor"),
            P("tensor", None),
            P(),
            P(),
            P(),
        ),
        check_vma=False,
    )
```

```python
import functools
import types

import jax
import jax.numpy as jnp
from jax import lax
from jax.experimental import pallas as pl
from jax.experimental.pallas import tpu as pltpu
from jax.sharding import PartitionSpec as P

MESH = pl.DeviceIdType.MESH
HEAD_DIM = 64
EPSILON = 1e-05
ROOT_HALF = 0.7071067811865476
INVERSE_ROOT_TAU = 0.3989422804014327
MASKED = -1e30
VMEM_BYTES = 62 << 20
POLLS = (4, 2, 1, 2, 2, 1)
BF = jnp.bfloat16
F32 = jnp.float32


def up_to(size, unit):
    return (size + unit - 1) // unit * unit


def dot(left, right):
    return jnp.dot(left, right, preferred_element_type=F32)


def dot_nt(left, right):
    return lax.dot_general(left, right, (((1,), (1,)), ((), ())), preferred_element_type=F32)


def dot_tn(left, right):
    return lax.dot_general(left, right, (((0,), (0,)), ((), ())), preferred_element_type=F32)


def pad_rows(rows, size):
    extra = size - rows.shape[0]
    if extra == 0:
        return rows
    return jnp.concatenate([rows, jnp.zeros((extra, rows.shape[1]), rows.dtype)], axis=0)


class Group:
    def __init__(self):
        self.dp = lax.axis_index("dp")
        self.own = lax.axis_index("tensor")
        self.y = self.own // 2
        self.core = self.own % 2
        self.mate = self.y * 2 + (1 - self.core)
        self.far = (1 - self.y) * 2 + self.core

    def greet(self, dp_peers):
        barrier = pltpu.get_barrier_semaphore()
        peers = [(self.dp, self.mate), (self.dp, self.far)] + [(peer, self.own) for peer in dp_peers]
        for peer in peers:
            pl.semaphore_signal(barrier, inc=1, device_id=peer, device_id_type=MESH)
        return lambda: pl.semaphore_wait(barrier, len(peers))

    def share(self, turn):
        late = turn // 2
        other = ((turn + 1) // 2) % 2
        ybit = (1 - self.y) * (1 - late) + self.y * late
        core = self.core * (1 - other) + (1 - self.core) * other
        return ybit * 2 + core

    def copy(self, source, target, send, recv, peer):
        return pltpu.make_async_remote_copy(
            src_ref=source,
            dst_ref=target,
            send_sem=send,
            recv_sem=recv,
            device_id=(self.dp, peer),
            device_id_type=MESH,
        )


class Gather:
    def __init__(self, group, full, send, recv):
        self.group, self.full, self.send, self.recv = group, full, send, recv

    def _copy(self, seq, kind):
        group = self.group
        share = group.far if kind == 2 else group.own
        slot = self.full.at[seq, share]
        peer = group.far if kind == 0 else group.mate
        return group.copy(slot, slot, self.send.at[seq, kind], self.recv.at[seq, kind], peer)

    def start(self, seq):
        self._copy(seq, 0).start()
        self._copy(seq, 1).start()

    def wait(self, seq, turn):
        @pl.when(turn == 0)
        def _():
            self._copy(seq, 0).wait_recv()
            self._copy(seq, 2).start()

        @pl.when(turn == 1)
        def _():
            self._copy(seq, 2).wait_recv()

        @pl.when(turn == 2)
        def _():
            self._copy(seq, 1).wait_recv()

    def close(self, seq):
        for kind in range(3):
            self._copy(seq, kind).wait_send()


class Scatter:
    def __init__(self, group, buffers, send, recv):
        self.group = group
        self.outgoing, self.keep, self.near, self.cross, self.landed = buffers
        self.send, self.recv = send, recv

    def _near(self, seq, index):
        return self.group.copy(
            self.outgoing.at[seq, index],
            self.near.at[seq, index],
            self.send.at[seq, index],
            self.recv.at[seq, index],
            self.group.mate,
        )

    def _cross(self, seq):
        return self.group.copy(
            self.cross.at[seq],
            self.landed.at[seq],
            self.send.at[seq, 2],
            self.recv.at[seq, 2],
            self.group.far,
        )

    def put(self, seq, turn, terms):
        @pl.when((turn == 0) | (turn == 3))
        def _():
            self.keep[seq, turn // 3] = terms

        @pl.when((turn == 1) | (turn == 2))
        def _():
            self.outgoing[seq, turn - 1] = terms.astype(BF)
            self._near(seq, turn - 1).start()

        @pl.when(turn == 2)
        def _():
            self._near(seq, 0).wait_recv()
            total = self.keep[seq, 0] + self.near[seq, 0].astype(F32)
            self.cross[seq] = total.astype(BF)
            self._cross(seq).start()

    def take(self, seq):
        self._near(seq, 1).wait_recv()
        self._cross(seq).wait_recv()
        for index in range(2):
            self._near(seq, index).wait_send()
        self._cross(seq).wait_send()
        return (
            self.keep[seq, 1]
            + self.near[seq, 1].astype(F32)
            + self.landed[seq].astype(F32)
        )


def norm(rows):
    centred = rows - jnp.mean(rows, axis=-1, keepdims=True)
    inverse = lax.rsqrt(jnp.mean(centred * centred, axis=-1, keepdims=True) + EPSILON)
    return centred * inverse, inverse


def norm_back(grad, normed, inverse, gain):
    scaled = grad * gain
    return inverse * (
        scaled
        - jnp.mean(scaled, axis=-1, keepdims=True)
        - normed * jnp.mean(scaled * normed, axis=-1, keepdims=True)
    )


def sum_rows(rows):
    return jnp.sum(rows, axis=0, keepdims=True)


def lane_index(rows, lanes):
    return lax.broadcasted_iota(jnp.int32, (rows, lanes), 1)


class Ring:
    def __init__(self, group, count, own, opening, landed, shared, sems, first, rows):
        self.group, self.count, self.steps = group, count, count - 1
        self.own, self.opening, self.landed, self.shared = own, opening, landed, shared
        self.add_send, self.add_recv, self.share_send, self.share_recv = sems
        self.half = own.shape[0] // (2 * count)
        self.first, self.rows = first, rows
        self.span = pl.ds(first, rows)
        self.place, self.right, self.left = ring_peers(group.dp, count)

    def _own(self, way, step):
        shift = self.count - 1 - step if way == 0 else 1 + step
        chunk = (self.place + shift) % self.count
        start = pl.multiple_of((2 * chunk + way) * self.half + self.first, 16)
        return self.own[pl.ds(start, self.rows)]

    def _copy(self, source, target, send, recv, way):
        return pltpu.make_async_remote_copy(
            src_ref=source,
            dst_ref=target,
            send_sem=send,
            recv_sem=recv,
            device_id=(self.right if way == 0 else self.left, self.group.own),
            device_id_type=MESH,
        )

    def _add(self, way, step, source=None):
        target = self.landed.at[way, step, self.span]
        return self._copy(
            target if source is None else source,
            target,
            self.add_send.at[way, step],
            self.add_recv.at[way, step],
            way,
        )

    def _share(self, way, step):
        shift = self.count - step if way == 0 else step
        slot = self.shared.at[(self.place + shift) % self.count, way, self.span]
        return self._copy(
            slot, slot, self.share_send.at[way, step], self.share_recv.at[way, step], way
        )

    def open(self):
        for way in range(2):
            self.opening[way, self.span] = self._own(way, 0).astype(BF)
            self._add(way, 0, self.opening.at[way, self.span]).start()

    def advance(self, step):
        last = self.steps - 1
        for way in range(2):
            if step < self.steps:
                self._add(way, step).wait_recv()
                total = self.landed[way, step, self.span].astype(F32) + self._own(way, step + 1)
                if step < last:
                    self.landed[way, step, self.span] = total.astype(BF)
                    self._add(way, step + 1, self.landed.at[way, step, self.span]).start()
                else:
                    self.shared[self.place, way, self.span] = total.astype(BF)
                    self._share(way, 0).start()
            else:
                turn = step - self.steps
                self._share(way, turn).wait_recv()
                if turn < last:
                    self._share(way, turn + 1).start()

    def close(self):
        for way in range(2):
            for step in range(self.steps):
                self._add(way, step).wait_send()
                self._share(way, step).wait_send()


def ring_peers(index, count):
    odd = index % 2
    place = (1 - odd) * (index // 2) + odd * (count - 1 - index // 2)

    def at(spot):
        late = spot // (count // 2)
        return (1 - late) * 2 * spot + late * (2 * (count - 1 - spot) + 1)

    return place, at((place + 1) % count), at((place + count - 1) % count)


def halving_peers(index, count):
    peers = []
    bit = 1
    while bit < count:
        peers.append(index + bit * (1 - 2 * ((index // bit) % 2)))
        bit *= 2
    return peers


class Totals:
    def __init__(self, group, peers, outgoing, arriving, send, recv, shared):
        self.group, self.shared = group, shared
        self.outgoing, self.arriving, self.send, self.recv = outgoing, arriving, send, recv
        own = group.own
        self.peers = [(group.dp, group.mate), (group.dp, group.far)] + [(peer, own) for peer in peers]

    def _copy(self, level):
        return pltpu.make_async_remote_copy(
            src_ref=self.outgoing.at[level],
            dst_ref=self.arriving.at[level],
            send_sem=self.send.at[level],
            recv_sem=self.recv.at[level],
            device_id=self.peers[level],
            device_id_type=MESH,
        )

    def begin(self, level, rows):
        self.outgoing[level] = rows
        self._copy(level).start()

    def end(self, level):
        self._copy(level).wait()
        other = self.arriving[level]
        if level < 2:
            place = lax.broadcasted_iota(jnp.int32, other.shape, 0)
            other = jnp.where(place < self.shared, other, 0.0)
        return self.outgoing[level] + other


def layer(count, names, *refs):
    r = types.SimpleNamespace(**dict(zip(names, refs)))
    seqs, share_rows, width = r.frames.shape
    rows = r.full_frames.shape[2]
    length = 4 * rows
    heads_width = r.query_weight.shape[0]
    lanes = r.wide_weight.shape[0] // 3
    heads = heads_width // HEAD_DIM
    group = Group()
    pairs = []
    ring_sides = []
    if count:
        pairs = halving_peers(group.dp, count)
        ring_sides = list(ring_peers(group.dp, count)[1:])
    met = group.greet(ring_sides + pairs)

    out_bias, first_gain, first_shift, down_bias, second_gain, second_shift, up_bias = (
        row[...].reshape(1, row.shape[0])
        for row in (
            r.out_bias, r.first_gain, r.first_shift, r.down_bias, r.second_gain, r.second_shift, r.up_bias,
        )
    )
    buffers = (r.outgoing, r.keep, r.near, r.cross, r.landed)
    gathers = [
        Gather(group, full, r.gather_send.at[index], r.gather_recv.at[index])
        for index, full in enumerate((r.full_frames, r.first_full, r.grad_mixed, r.grad_full))
    ]
    scatters = [
        Scatter(group, buffers, r.scatter_send.at[index], r.scatter_recv.at[index])
        for index in range(4)
    ]
    grad_total = r.hidden.at[0]
    heads_grad = r.hidden.at[1, pl.ds(0, 4 * heads_width)]
    grad_projected = r.activated.at[0]

    def each(stage):
        def body(seq, carry):
            stage(seq)
            return carry

        lax.fori_loop(0, seqs, body, 0)

    def turns(step):
        def body(turn, carry):
            step(turn)
            return carry

        lax.fori_loop(0, 4, body, 0)

    def at_share(share):
        return pl.ds(pl.multiple_of(share * rows, 16), rows)

    def place_frames(seq):
        r.full_frames[seq, group.own] = pad_rows(r.frames[seq].astype(F32), rows).astype(BF)

    each(place_frames)
    met()
    each(gathers[0].start)
    r.wide_weight[...] = jnp.zeros_like(r.wide_weight)
    for index, weight in enumerate((r.query_weight, r.key_weight, r.value_weight)):
        r.wide_weight[index * lanes : index * lanes + heads_width] = weight[...]
    r.wide_out[...] = jnp.zeros_like(r.wide_out)
    r.wide_out[:heads_width] = r.out_weight[...]
    r.projection_bias[...] = jnp.where(
        lane_index(1, 3 * lanes) == heads_width, HEAD_DIM**0.5, 0.0
    )
    r.projection_bias[:, :heads_width] = r.query_bias[...].reshape(1, heads_width)
    r.projection_bias[:, 2 * lanes : 2 * lanes + heads_width] = r.value_bias[...].reshape(1, heads_width)
    r.rows_sum[...] = jnp.zeros_like(r.rows_sum)

    def attention(seq):
        def project(step):
            turn = (1 - step // 2) * (3 - step) + (step // 2) * (step - 2)
            gathers[0].wait(seq, turn)
            share = group.share(turn)
            result = dot_nt(r.full_frames[seq, share], r.wide_weight[...]) + r.projection_bias[...]
            place = lax.broadcasted_iota(jnp.int32, (rows, lanes), 0)
            dead = (place >= share_rows) | (place + share * share_rows >= r.lengths[seq])
            flag = jnp.where(dead & (lane_index(rows, lanes) == heads_width), MASKED, 0.0)
            r.projected[seq, at_share(share), 0:lanes] = (
                result[:, :lanes].astype(BF) * HEAD_DIM ** (-0.5)
            ).astype(BF)
            r.projected[seq, at_share(share), lanes : 2 * lanes] = (
                result[:, lanes : 2 * lanes] + flag
            ).astype(BF)
            r.projected[seq, at_share(share), 2 * lanes : 3 * lanes] = result[:, 2 * lanes :].astype(BF)

        turns(project)

        def attend(block, carry):
            chip = (1 - group.y) * (1 - block) + group.y * block
            span = pl.ds(pl.multiple_of(chip * 2 * rows, 16), 2 * rows)
            queries = r.projected[seq, span, 0:lanes]
            lane = lane_index(2 * rows, lanes)
            mixed = jnp.zeros((2 * rows, lanes), F32)
            for head in range(heads):
                inside = lane // HEAD_DIM == head
                picked = jnp.where(inside | (lane == heads_width), queries, jnp.zeros_like(queries))
                scores = dot_nt(picked, r.projected[seq, :, lanes : 2 * lanes])
                top = jnp.max(scores, axis=-1, keepdims=True)
                exponent = jnp.exp(scores - top)
                weight = jnp.sum(exponent, axis=-1, keepdims=True)
                r.log_total[seq, chip, head : head + 1] = jnp.transpose(top + jnp.log(weight))
                part = dot(exponent.astype(BF), r.projected[seq, :, 2 * lanes : 3 * lanes])
                mixed = jnp.where(inside, part * (1.0 / weight), mixed)
            r.context[seq, span] = mixed.astype(BF)
            for half in range(2):
                turn = 2 * block + half
                mixed = r.context[seq, at_share(group.share(turn))]
                scatters[0].put(seq, turn, dot(mixed, r.wide_out[...]))
            return carry

        lax.fori_loop(0, 2, attend, 0)

    each(attention)

    def first_norm(seq):
        attended = scatters[0].take(seq)
        normed, inverse = norm(r.full_frames[seq, group.own].astype(F32) + attended + out_bias)
        r.first_normed[seq] = normed
        r.first_inverse[seq] = inverse
        r.first_full[seq, group.own] = (normed * first_gain + first_shift).astype(BF)
        gathers[1].start(seq)

    each(first_norm)

    def feed(seq):
        def step(turn):
            gathers[1].wait(seq, turn)
            share = group.share(turn)
            inner = dot(r.first_full[seq, share], r.up_weight[...]) + up_bias
            r.hidden[seq, at_share(share)] = inner
            active = (0.5 * inner * (1.0 + lax.erf(inner * ROOT_HALF))).astype(BF)
            r.activated[seq, at_share(share)] = active
            scatters[1].put(seq, turn, dot(active, r.down_weight[...]))

        turns(step)

    each(feed)

    def second_norm(seq):
        mixed = scatters[1].take(seq)
        first = r.first_normed[seq] * first_gain + first_shift
        normed, inverse = norm(first + mixed + down_bias)
        place = lax.broadcasted_iota(jnp.int32, (rows, width), 0)
        live = (place < share_rows) & (place + group.own * share_rows < r.lengths[seq])
        grad = jnp.where(live, pad_rows(r.cotangent[seq], rows), 0.0)
        back = norm_back(grad, normed, inverse, second_gain)
        r.grad_mixed[seq, group.own] = back.astype(BF)
        gathers[2].start(seq)
        r.grad_rows[seq] = back
        r.layer_output[seq] = (normed * second_gain + second_shift)[:share_rows].astype(BF)
        r.rows_sum[0:1] += sum_rows(grad * normed)
        r.rows_sum[1:2] += sum_rows(grad)
        r.rows_sum[2:3] += sum_rows(back)

    each(second_norm)

    def feed_back(seq):
        def step(turn):
            gathers[2].wait(seq, turn)
            share = group.share(turn)
            grad_active = dot_nt(r.grad_mixed[seq, share], r.down_weight[...])
            inner = r.hidden[seq, at_share(share)]
            slope = (
                0.5 * (1.0 + lax.erf(inner * ROOT_HALF))
                + inner * jnp.exp(-0.5 * inner * inner) * INVERSE_ROOT_TAU
            )
            grad = (grad_active * slope).astype(BF)
            r.grad_hidden[seq, at_share(share)] = grad
            r.rows_sum[6:7] += sum_rows(grad.astype(F32))
            scatters[2].put(seq, turn, dot_nt(grad, r.up_weight[...]))

        turns(step)

    each(feed_back)

    def feed_weights(seq):
        down = dot_tn(r.activated[seq], r.grad_mixed[seq].reshape(length, width))
        r.down_grad[...] = down if seq == 0 else r.down_grad[...] + down
        up = dot_tn(r.first_full[seq].reshape(length, width), r.grad_hidden[seq])
        r.up_grad[...] = up if seq == 0 else r.up_grad[...] + up

    def first_back(seq):
        grad = r.grad_rows[seq] + scatters[2].take(seq)
        normed = r.first_normed[seq]
        back = norm_back(grad, normed, r.first_inverse[seq], first_gain)
        r.grad_full[seq, group.own] = back.astype(BF)
        gathers[3].start(seq)
        r.grad_rows[seq] = back
        r.rows_sum[3:4] += sum_rows(grad * normed)
        r.rows_sum[4:5] += sum_rows(grad)
        r.rows_sum[5:6] += sum_rows(back)

    queue = []

    def advance_both(both, step):
        for ring in both:
            ring.advance(step)

    def poll(times=1):
        for _ in range(times):
            if queue:
                queue.pop(0)()

    for seq in range(seqs):
        feed_weights(seq)
        if seq == seqs - 1 and count:
            half = width // (2 * count)

            def make_ring(index, own, first, size):
                return Ring(
                    group,
                    count,
                    own,
                    r.opening.at[index],
                    r.ring_landed.at[index],
                    r.ring_shared.at[index],
                    [
                        sem.at[index, first // 16]
                        for sem in (r.add_send, r.add_recv, r.share_send, r.share_recv)
                    ],
                    first,
                    size,
                )

            rings = [
                make_ring(index, own, first, 16)
                for first in range(0, half, 16)
                for index, own in enumerate((r.up_grad, r.down_grad))
            ]
            late_rings = [make_ring(2, heads_grad, first, 16) for first in range(0, half, 16)]
            for ring in rings:
                ring.open()
            for step in range(2 * (count - 1)):
                for first in range(0, len(rings), 2):
                    queue.append(functools.partial(advance_both, rings[first : first + 2], step))
        first_back(seq)
    poll(POLLS[0])
    if count:
        totals = Totals(
            group, pairs, r.small_out, r.small_in, r.small_send, r.small_recv, 6
        )
        totals.begin(0, r.rows_sum[...])
    heads_grad[...] = jnp.zeros_like(heads_grad)

    def store_input(seq):
        r.input_grad[seq] = (scatters[3].take(seq) + r.grad_rows[seq])[:share_rows]

    for seq in range(seqs):

        def step(turn):
            gathers[3].wait(seq, turn)
            share = group.share(turn)
            r.grad_context[at_share(share)] = dot_nt(r.grad_full[seq, share], r.wide_out[...]).astype(BF)
            heads_grad[3 * heads_width :] += dot_tn(
                r.context[seq, at_share(share)], r.grad_full[seq, share]
            )[:heads_width]

        turns(step)
        poll(POLLS[1])
        grad_total[...] = jnp.zeros_like(grad_total)
        keys = r.projected[seq, :, lanes : 2 * lanes]
        lane = lane_index(length, lanes)
        key_columns = jnp.transpose(keys.astype(F32) * HEAD_DIM ** (-0.5)).astype(BF)
        for head in range(heads):
            inside = lane // HEAD_DIM == head
            queries = r.projected[seq, :, 0:lanes]
            picked = jnp.where(inside | (lane == heads_width), queries, jnp.zeros_like(queries))
            row = jnp.concatenate(
                [r.log_total[seq, chip, head : head + 1] for chip in range(2)], axis=1
            )
            weights = jnp.exp(dot_nt(keys, picked) - row)
            grads = r.grad_context[...]
            part = dot(weights.astype(BF), grads)
            span = slice(2 * lanes, 3 * lanes)
            grad_total[:, span] = jnp.where(inside, part, grad_total[:, span])
            poll(POLLS[2])
            slopes = weights * dot_nt(
                r.projected[seq, :, 2 * lanes : 3 * lanes],
                jnp.where(inside, grads, jnp.zeros_like(grads)),
            )
            slopes = (slopes - weights * jnp.sum(slopes, axis=0, keepdims=True)).astype(BF)
            part = dot(slopes, queries)
            span = slice(lanes, 2 * lanes)
            grad_total[:, span] = jnp.where(inside, part, grad_total[:, span])
            span = slice(head * HEAD_DIM, (head + 1) * HEAD_DIM)
            grad_total[:, span] = jnp.transpose(dot(key_columns[span], slopes))
            poll(POLLS[3])

        def finish(turn):
            share = group.share(turn)
            grads = grad_total[at_share(share)].astype(BF)
            grad_projected[at_share(share)] = grads
            r.rows_sum[7:8] += sum_rows(grads.astype(F32))
            scatters[3].put(seq, turn, dot(grads, r.wide_weight[...]))

        turns(finish)
        poll(POLLS[4])
        for index in range(3):
            heads_grad[index * heads_width : (index + 1) * heads_width] += dot_tn(
                grad_projected[:, index * lanes : (index + 1) * lanes],
                r.full_frames[seq].reshape(length, width),
            )[:heads_width]
        poll(POLLS[5])
        if seq == 0:
            if count:
                totals.begin(1, totals.end(0))
        else:
            store_input(seq - 1)

    if count:
        for ring in late_rings:
            ring.open()
        place = lax.broadcasted_iota(jnp.int32, r.rows_sum.shape, 0)
        totals.begin(2, jnp.where(place == 7, r.rows_sum[...], totals.end(1)))
        copies = [
            pltpu.make_async_copy(r.ring_shared.at[index], out, r.out_sem.at[index])
            for index, out in enumerate((r.up_sum, r.down_sum, r.heads_sum))
        ]
        level = 2
        last = len(pairs) + 1
        for step in range(2 * (count - 1)):
            for ring in late_rings:
                ring.advance(step)
                poll()
            if step == 2:
                store_input(seqs - 1)
            if step % 3 == 2 and level <= last:
                rows_total = totals.end(level)
                level += 1
                if level <= last:
                    totals.begin(level, rows_total)
                else:
                    r.sums[...] = rows_total
        poll(len(queue))
        for copy in copies:
            copy.start()
        for ring in rings + late_rings:
            ring.close()
    else:
        store_input(seqs - 1)
        r.sums[...] = r.rows_sum[...]
        copies = [
            pltpu.make_async_copy(own, out, r.out_sem.at[index])
            for index, (own, out) in enumerate(
                ((r.up_grad, r.up_sum), (r.down_grad, r.down_sum), (heads_grad, r.heads_sum))
            )
        ]
        for copy in copies:
            copy.start()
    for seq in range(seqs):
        for gather in gathers:
            gather.close(seq)
    for copy in copies:
        copy.wait()


VMEM_SPEC = pl.BlockSpec(memory_space=pltpu.VMEM)
ANY_SPEC = pl.BlockSpec(memory_space=pl.ANY)


def widen(columns, refs, *rest):
    r = types.SimpleNamespace(**dict(zip(refs, rest)))
    heads_width = r.query_bias.shape[0]
    width = r.up.shape[1]
    plain = [
        (r.layer_in, r.layer_stage, r.layer_output),
        (r.input_in, r.input_stage, r.input_grad),
    ]
    plain_loads = [
        pltpu.make_async_copy(source, stage, r.plain_sem.at[index])
        for index, (source, stage, _) in enumerate(plain)
    ]
    loads = [
        pltpu.make_async_copy(source, r.narrow.at[index], r.load_sem.at[index])
        for index, source in enumerate((r.up_in, r.down_in, r.heads_in))
    ]
    for copy in loads + plain_loads:
        copy.start()
    stores = []
    for index, load in enumerate(loads):
        load.wait()
        r.wide[index] = r.narrow[index].astype(F32).reshape(width, width)
        if index < 2:
            parts = [(r.wide.at[index], (r.up, r.down)[index])]
        else:
            parts = [
                (r.wide.at[index, pl.ds(part * heads_width, heads_width)], target)
                for part, target in enumerate((r.query, r.key, r.value, r.out))
            ]
        for source, target in parts:
            store = pltpu.make_async_copy(source, target, r.store_sem.at[len(stores)])
            store.start()
            stores.append(store)
    for load, (_, stage, target) in zip(plain_loads, plain):
        load.wait()
        store = pltpu.make_async_copy(stage, target, r.store_sem.at[len(stores)])
        store.start()
        stores.append(store)
    rows = (
        r.second_gain, r.second_shift, r.down_bias, r.first_gain, r.first_shift, r.out_bias, r.up_bias,
    )
    for index, row in enumerate(rows):
        row[...] = r.sums[index]
    r.query_bias[...] = r.sums[7, 0:heads_width]
    r.value_bias[...] = r.sums[7, columns : columns + heads_width]
    for copy in stores:
        copy.wait()


def shards(
    frames,
    cotangent,
    lengths,
    query_weight,
    query_bias,
    key_weight,
    value_weight,
    value_bias,
    out_weight,
    out_bias,
    first_gain,
    first_shift,
    up_weight,
    up_bias,
    down_weight,
    down_bias,
    second_gain,
    second_shift,
):
    seqs, share_rows, width = frames.shape
    rows = up_to(share_rows, 16)
    length = 4 * rows
    heads_width = query_weight.shape[1]
    inner = up_weight.shape[1]
    lanes = up_to(heads_width + 1, 128)
    shape = jax.ShapeDtypeStruct
    count = lax.axis_size("dp")
    ringed = count & (count - 1) == 0 and width % (32 * count) == 0
    half = width // (2 * count)
    levels = 2 + count.bit_length() - 1
    full = pltpu.VMEM((seqs, 4, rows, width), BF)
    part = pltpu.VMEM((seqs, rows, width), BF)
    stream = pltpu.VMEM((seqs, rows, width), F32)
    inputs = dict(
        lengths=lengths,
        frames=frames,
        cotangent=cotangent,
        query_weight=query_weight.T,
        query_bias=query_bias,
        key_weight=key_weight.T,
        value_weight=value_weight.T,
        value_bias=value_bias,
        out_weight=out_weight,
        out_bias=out_bias,
        first_gain=first_gain,
        first_shift=first_shift,
        up_weight=up_weight,
        up_bias=up_bias,
        down_weight=down_weight,
        down_bias=down_bias,
        second_gain=second_gain,
        second_shift=second_shift,
    )
    summed = (
        shape((count, 2, half, width), BF) if ringed else shape((width, width), F32)
    )
    outputs = dict(
        layer_output=shape(frames.shape, BF),
        input_grad=shape(frames.shape, F32),
        sums=shape((8, width), F32),
        up_sum=summed,
        down_sum=summed,
        heads_sum=summed,
    )
    scratch = dict(
        wide_weight=pltpu.VMEM((3 * lanes, width), BF),
        wide_out=pltpu.VMEM((lanes, width), BF),
        projection_bias=pltpu.VMEM((1, 3 * lanes), F32),
        rows_sum=pltpu.VMEM((8, width), F32),
        full_frames=full,
        first_full=full,
        grad_mixed=full,
        grad_full=full,
        projected=pltpu.VMEM((seqs, length, 3 * lanes), BF),
        context=pltpu.VMEM((seqs, length, lanes), BF),
        log_total=pltpu.VMEM((seqs, 2, 8, 2 * rows), F32),
        first_normed=stream,
        first_inverse=pltpu.VMEM((seqs, rows, 1), F32),
        grad_rows=stream,
        hidden=pltpu.VMEM((seqs, length, inner), F32),
        activated=pltpu.VMEM((seqs, length, inner), BF),
        grad_hidden=pltpu.VMEM((seqs, length, inner), BF),
        grad_context=pltpu.VMEM((length, lanes), BF),
        up_grad=pltpu.VMEM(up_weight.shape, F32),
        down_grad=pltpu.VMEM(down_weight.shape, F32),
        outgoing=pltpu.VMEM((seqs, 2, rows, width), BF),
        keep=pltpu.VMEM((seqs, 2, rows, width), F32),
        near=pltpu.VMEM((seqs, 2, rows, width), BF),
        cross=part,
        landed=part,
        gather_send=pltpu.SemaphoreType.DMA((4, seqs, 3)),
        gather_recv=pltpu.SemaphoreType.DMA((4, seqs, 3)),
        scatter_send=pltpu.SemaphoreType.DMA((4, seqs, 3)),
        scatter_recv=pltpu.SemaphoreType.DMA((4, seqs, 3)),
        out_sem=pltpu.SemaphoreType.DMA((3,)),
    )
    if ringed:
        ring_sem = pltpu.SemaphoreType.DMA((3, half // 16, 2, count - 1))
        scratch.update(
            opening=pltpu.VMEM((3, 2, half, width), BF),
            ring_landed=pltpu.VMEM((3, 2, count - 1, half, width), BF),
            ring_shared=pltpu.VMEM((3, count, 2, half, width), BF),
            add_send=ring_sem,
            add_recv=ring_sem,
            share_send=ring_sem,
            share_recv=ring_sem,
            small_out=pltpu.VMEM((levels, 8, width), F32),
            small_in=pltpu.VMEM((levels, 8, width), F32),
            small_send=pltpu.SemaphoreType.DMA((levels,)),
            small_recv=pltpu.SemaphoreType.DMA((levels,)),
        )
    outs = pl.pallas_call(
        functools.partial(layer, count if ringed else 0, [*inputs, *outputs, *scratch]),
        out_shape=list(outputs.values()),
        in_specs=[pl.BlockSpec(memory_space=pltpu.SMEM)] + [VMEM_SPEC] * (len(inputs) - 1),
        out_specs=[VMEM_SPEC] * 3 + [ANY_SPEC] * 3,
        scratch_shapes=list(scratch.values()),
        compiler_params=pltpu.CompilerParams(
            collective_id=0, has_side_effects=True, vmem_limit_bytes=VMEM_BYTES
        ),
        name="layer",
    )(*inputs.values())
    layer_output, input_grad, sums = outs[:3]
    if not ringed:
        up_grad, down_grad, heads_grad = lax.psum(tuple(outs[3:]), "dp")
        sums = lax.psum(sums, "dp")
        sums = jnp.concatenate([lax.psum(sums[:6], "tensor"), sums[6:]])
        parts = [heads_grad[index * heads_width : (index + 1) * heads_width] for index in range(4)]
        return (
            layer_output, input_grad, parts[0].T, sums[7, :heads_width], parts[1].T, parts[2].T,
            sums[7, 2 * lanes : 2 * lanes + heads_width], parts[3], sums[5], sums[3], sums[4],
            up_grad, sums[6], down_grad, sums[2], sums[0], sums[1],
        )
    row = shape((width,), F32)
    side_row = shape((heads_width,), F32)
    block = shape((heads_width, width), F32)
    square = shape((width, width), F32)
    results = dict(
        layer_output=shape(frames.shape, BF),
        input_grad=shape(frames.shape, F32),
        query=block,
        query_bias=side_row,
        key=block,
        value=block,
        value_bias=side_row,
        out=block,
        out_bias=row,
        first_gain=row,
        first_shift=row,
        up=square,
        up_bias=row,
        down=square,
        down_bias=row,
        second_gain=row,
        second_shift=row,
    )
    given = ["layer_in", "input_in", "sums", "up_in", "down_in", "heads_in"]
    buffers = dict(
        narrow=pltpu.VMEM((3, count, 2, half, width), BF),
        wide=pltpu.VMEM((3, width, width), F32),
        plain_sem=pltpu.SemaphoreType.DMA((2,)),
        load_sem=pltpu.SemaphoreType.DMA((3,)),
        store_sem=pltpu.SemaphoreType.DMA((8,)),
        layer_stage=pltpu.VMEM(frames.shape, BF),
        input_stage=pltpu.VMEM(frames.shape, F32),
    )
    final = pl.pallas_call(
        functools.partial(widen, 2 * lanes, [*given, *results, *buffers]),
        out_shape=list(results.values()),
        in_specs=[ANY_SPEC] * 2 + [VMEM_SPEC] + [ANY_SPEC] * 3,
        out_specs=[VMEM_SPEC if len(item.shape) == 1 else ANY_SPEC for item in results.values()],
        scratch_shapes=list(buffers.values()),
        compiler_params=pltpu.CompilerParams(vmem_limit_bytes=VMEM_BYTES),
        name="widen",
    )(layer_output, input_grad, sums, *outs[3:])
    final = dict(zip(results, final))
    for name in ("query", "key", "value"):
        final[name] = final[name].T
    return tuple(final.values())


def solution(mesh):
    return jax.shard_map(
        shards,
        mesh=mesh,
        in_specs=(
            P("dp", "tensor", None),
            P("dp", "tensor", None),
            P("dp"),
            P(None, "tensor"),
            P("tensor"),
            P(None, "tensor"),
            P(None, "tensor"),
            P("tensor"),
            P("tensor", None),
            P(),
            P(),
            P(),
            P(None, "tensor"),
            P("tensor"),
            P("tensor", None),
            P(),
            P(),
            P(),
        ),
        out_specs=(
            P("dp", "tensor", None),
            P("dp", "tensor", None),
            P(None, "tensor"),
            P("tensor"),
            P(None, "tensor"),
            P(None, "tensor"),
            P("tensor"),
            P("tensor", None),
            P(),
            P(),
            P(),
            P(None, "tensor"),
            P("tensor"),
            P("tensor", None),
            P(),
            P(),
            P(),
        ),
        check_vma=False,
    )
```

```python
import functools
import types

import jax
import jax.numpy as jnp
from jax import lax
from jax.experimental import pallas as pl
from jax.experimental.pallas import tpu as pltpu
from jax.sharding import PartitionSpec as P

MESH = pl.DeviceIdType.MESH
HEAD_DIM = 64
EPSILON = 1e-05
ROOT_HALF = 0.7071067811865476
INVERSE_ROOT_TAU = 0.3989422804014327
MASKED = -1e30
VMEM_BYTES = 62 << 20
POLLS = (3, 2, 1, 2, 2, 1)
BF = jnp.bfloat16
F32 = jnp.float32


def up_to(size, unit):
    return (size + unit - 1) // unit * unit


def dot(left, right):
    return jnp.dot(left, right, preferred_element_type=F32)


def dot_nt(left, right):
    return lax.dot_general(left, right, (((1,), (1,)), ((), ())), preferred_element_type=F32)


def dot_tn(left, right):
    return lax.dot_general(left, right, (((0,), (0,)), ((), ())), preferred_element_type=F32)


def pad_rows(rows, size):
    extra = size - rows.shape[0]
    if extra == 0:
        return rows
    return jnp.concatenate([rows, jnp.zeros((extra, rows.shape[1]), rows.dtype)], axis=0)


class Group:
    def __init__(self):
        self.dp = lax.axis_index("dp")
        self.own = lax.axis_index("tensor")
        self.y = self.own // 2
        self.core = self.own % 2
        self.mate = self.y * 2 + (1 - self.core)
        self.far = (1 - self.y) * 2 + self.core

    def greet(self, dp_peers):
        barrier = pltpu.get_barrier_semaphore()
        peers = [(self.dp, self.mate), (self.dp, self.far)] + [(peer, self.own) for peer in dp_peers]
        for peer in peers:
            pl.semaphore_signal(barrier, inc=1, device_id=peer, device_id_type=MESH)
        return lambda: pl.semaphore_wait(barrier, len(peers))

    def share(self, turn):
        late = turn // 2
        other = ((turn + 1) // 2) % 2
        ybit = (1 - self.y) * (1 - late) + self.y * late
        core = self.core * (1 - other) + (1 - self.core) * other
        return ybit * 2 + core

    def copy(self, source, target, send, recv, peer):
        return pltpu.make_async_remote_copy(
            src_ref=source,
            dst_ref=target,
            send_sem=send,
            recv_sem=recv,
            device_id=(self.dp, peer),
            device_id_type=MESH,
        )


class Gather:
    def __init__(self, group, full, send, recv, real):
        self.group, self.full, self.send, self.recv = group, full, send, recv
        self.real = pl.ds(0, real)

    def _copy(self, seq, kind):
        group = self.group
        share = group.far if kind == 2 else group.own
        slot = self.full.at[seq, share, self.real] if kind == 0 else self.full.at[seq, share]
        peer = group.far if kind == 0 else group.mate
        return group.copy(slot, slot, self.send.at[seq, kind], self.recv.at[seq, kind], peer)

    def start(self, seq):
        self._copy(seq, 0).start()
        self._copy(seq, 1).start()

    def wait(self, seq, turn):
        @pl.when(turn == 0)
        def _():
            self._copy(seq, 0).wait_recv()
            self._copy(seq, 2).start()

        @pl.when(turn == 1)
        def _():
            self._copy(seq, 2).wait_recv()

        @pl.when(turn == 2)
        def _():
            self._copy(seq, 1).wait_recv()

    def close(self, seq):
        for kind in range(3):
            self._copy(seq, kind).wait_send()


class Scatter:
    def __init__(self, group, buffers, send, recv, real):
        self.group = group
        self.real = pl.ds(0, real)
        self.outgoing, self.keep, self.near, self.cross, self.landed = buffers
        self.send, self.recv = send, recv

    def _near(self, seq, index):
        return self.group.copy(
            self.outgoing.at[seq, index],
            self.near.at[seq, index],
            self.send.at[seq, index],
            self.recv.at[seq, index],
            self.group.mate,
        )

    def _cross(self, seq):
        return self.group.copy(
            self.cross.at[seq, self.real],
            self.landed.at[seq, self.real],
            self.send.at[seq, 2],
            self.recv.at[seq, 2],
            self.group.far,
        )

    def put(self, seq, turn, terms):
        @pl.when((turn == 0) | (turn == 3))
        def _():
            self.keep[seq, turn // 3] = terms

        @pl.when((turn == 1) | (turn == 2))
        def _():
            self.outgoing[seq, turn - 1] = terms.astype(BF)
            self._near(seq, turn - 1).start()

        @pl.when(turn == 2)
        def _():
            self._near(seq, 0).wait_recv()
            total = self.keep[seq, 0] + self.near[seq, 0].astype(F32)
            self.cross[seq] = total.astype(BF)
            self._cross(seq).start()

    def take(self, seq):
        self._near(seq, 1).wait_recv()
        self._cross(seq).wait_recv()
        for index in range(2):
            self._near(seq, index).wait_send()
        self._cross(seq).wait_send()
        return (
            self.keep[seq, 1]
            + self.near[seq, 1].astype(F32)
            + self.landed[seq].astype(F32)
        )


def norm(rows):
    centred = rows - jnp.mean(rows, axis=-1, keepdims=True)
    inverse = lax.rsqrt(jnp.mean(centred * centred, axis=-1, keepdims=True) + EPSILON)
    return centred * inverse, inverse


def norm_back(grad, normed, inverse, gain):
    scaled = grad * gain
    return inverse * (
        scaled
        - jnp.mean(scaled, axis=-1, keepdims=True)
        - normed * jnp.mean(scaled * normed, axis=-1, keepdims=True)
    )


def sum_rows(rows):
    return jnp.sum(rows, axis=0, keepdims=True)


def lane_index(rows, lanes):
    return lax.broadcasted_iota(jnp.int32, (rows, lanes), 1)


class Ring:
    def __init__(self, group, count, owns, opening, landed, shared, sends, recvs, first):
        self.group, self.count, self.steps = group, count, count - 1
        self.owns, self.opening, self.landed, self.shared = owns, opening, landed, shared
        self.add_send, self.share_send = sends
        self.add_recv, self.share_recv = recvs
        self.half = owns[0].shape[0] // (2 * count)
        self.first, self.rows = first, landed.shape[3]
        self.place, self.right, self.left = ring_peers(group.dp, count)

    def _own(self, which, way, step):
        shift = self.count - 1 - step if way == 0 else 1 + step
        chunk = (self.place + shift) % self.count
        start = pl.multiple_of((2 * chunk + way) * self.half + self.first, 16)
        return self.owns[which][pl.ds(start, self.rows)]

    def _copy(self, source, target, send, recv, way):
        return pltpu.make_async_remote_copy(
            src_ref=source,
            dst_ref=target,
            send_sem=send,
            recv_sem=recv,
            device_id=(self.right if way == 0 else self.left, self.group.own),
            device_id_type=MESH,
        )

    def _add(self, way, step, source=None):
        target = self.landed.at[way, step]
        return self._copy(
            target if source is None else source, target, self.add_send, self.add_recv.at[way, step], way
        )

    def _share(self, way, step):
        shift = self.count - step if way == 0 else step
        slot = self.shared.at[(self.place + shift) % self.count, way]
        return self._copy(slot, slot, self.share_send, self.share_recv.at[way, step], way)

    def open(self):
        for way in range(2):
            for which in range(len(self.owns)):
                self.opening[way, which] = self._own(which, way, 0).astype(BF)
            self._add(way, 0, self.opening.at[way]).start()

    def advance(self, step):
        last = self.steps - 1
        for way in range(2):
            if step < self.steps:
                self._add(way, step).wait_recv()
                target = self.landed.at[way, step] if step < last else self.shared.at[self.place, way]
                for which in range(len(self.owns)):
                    total = self.landed[way, step, which].astype(F32) + self._own(which, way, step + 1)
                    target[which] = total.astype(BF)
                if step < last:
                    self._add(way, step + 1, target).start()
                else:
                    self._share(way, 0).start()
            else:
                turn = step - self.steps
                self._share(way, turn).wait_recv()
                if turn < last:
                    self._share(way, turn + 1).start()

    def wait_sends(self, landed):
        for send in (self.add_send, self.share_send):
            self._copy(landed, landed, send, self.add_recv.at[0, 0], 0).wait_send()


def ring_peers(index, count):
    odd = index % 2
    place = (1 - odd) * (index // 2) + odd * (count - 1 - index // 2)

    def at(spot):
        late = spot // (count // 2)
        return (1 - late) * 2 * spot + late * (2 * (count - 1 - spot) + 1)

    return place, at((place + 1) % count), at((place + count - 1) % count)


def halving_peers(index, count):
    peers = []
    bit = 1
    while bit < count:
        peers.append(index + bit * (1 - 2 * ((index // bit) % 2)))
        bit *= 2
    return peers


class Totals:
    def __init__(self, group, peers, outgoing, arriving, send, recv, shared):
        self.group, self.shared = group, shared
        self.outgoing, self.arriving, self.send, self.recv = outgoing, arriving, send, recv
        own = group.own
        self.peers = [(group.dp, group.mate), (group.dp, group.far)] + [(peer, own) for peer in peers]

    def _copy(self, level):
        return pltpu.make_async_remote_copy(
            src_ref=self.outgoing.at[level],
            dst_ref=self.arriving.at[level],
            send_sem=self.send.at[level],
            recv_sem=self.recv.at[level],
            device_id=self.peers[level],
            device_id_type=MESH,
        )

    def begin(self, level, rows):
        self.outgoing[level] = rows
        self._copy(level).start()

    def end(self, level):
        self._copy(level).wait()
        other = self.arriving[level]
        if level < 2:
            place = lax.broadcasted_iota(jnp.int32, other.shape, 0)
            other = jnp.where(place < self.shared, other, 0.0)
        return self.outgoing[level] + other


def layer(count, names, *refs):
    r = types.SimpleNamespace(**dict(zip(names, refs)))
    loads = {
        name[:-5]: pltpu.make_async_copy(ref, getattr(r, name[:-5]), r.load_sem.at[index])
        for index, (name, ref) in enumerate(zip(names, refs))
        if name.endswith("_from")
    }

    def loaded(*wanted):
        for name in wanted or list(loads):
            loads.pop(name).wait()

    seqs, share_rows, width = r.frames.shape
    rows = r.full_frames.shape[2]
    length = 4 * rows
    heads_width = r.query_weight.shape[0]
    lanes = r.wide_weight.shape[0] // 3
    heads = heads_width // HEAD_DIM
    group = Group()
    pairs = []
    ring_sides = []
    if count:
        pairs = halving_peers(group.dp, count)
        ring_sides = list(ring_peers(group.dp, count)[1:])
    tail = pl.ds(share_rows, rows - share_rows)
    if rows > share_rows:
        for full in (r.full_frames, r.first_full, r.grad_mixed, r.grad_full):
            full[:, :, tail] = jnp.zeros_like(full[:, :, tail])
        r.landed[:, tail] = jnp.zeros_like(r.landed[:, tail])
    met = group.greet(ring_sides + pairs)

    for load in loads.values():
        load.start()
    buffers = (r.outgoing, r.keep, r.near, r.cross, r.landed)
    gathers = [
        Gather(group, full, r.gather_send.at[index], r.gather_recv.at[index], share_rows)
        for index, full in enumerate((r.full_frames, r.first_full, r.grad_mixed, r.grad_full))
    ]
    scatters = [
        Scatter(group, buffers, r.scatter_send.at[index], r.scatter_recv.at[index], share_rows)
        for index in range(4)
    ]
    grad_total = r.hidden.at[0]
    heads_grad = r.hidden.at[1, pl.ds(0, 4 * heads_width)]
    grad_projected = r.activated.at[0]

    def each(stage):
        def body(seq, carry):
            stage(seq)
            return carry

        lax.fori_loop(0, seqs, body, 0)

    def turns(step):
        def body(turn, carry):
            step(turn)
            return carry

        lax.fori_loop(0, 4, body, 0)

    def at_share(share):
        return pl.ds(pl.multiple_of(share * rows, 16), rows)

    def place_frames(seq):
        r.full_frames[seq, group.own] = pad_rows(r.frames[seq].astype(F32), rows).astype(BF)

    loaded("frames")
    each(place_frames)
    met()
    each(gathers[0].start)
    loaded("query_weight", "key_weight", "value_weight", "query_bias", "value_bias", "out_weight")
    r.wide_weight[...] = jnp.zeros_like(r.wide_weight)
    for index, weight in enumerate((r.query_weight, r.key_weight, r.value_weight)):
        r.wide_weight[index * lanes : index * lanes + heads_width] = weight[...]
    r.wide_out[...] = jnp.zeros_like(r.wide_out)
    r.wide_out[:heads_width] = r.out_weight[...]
    r.projection_bias[...] = jnp.where(
        lane_index(1, 3 * lanes) == heads_width, HEAD_DIM**0.5, 0.0
    )
    r.projection_bias[:, :heads_width] = r.query_bias[...].reshape(1, heads_width)
    r.projection_bias[:, 2 * lanes : 2 * lanes + heads_width] = r.value_bias[...].reshape(1, heads_width)
    r.rows_sum[...] = jnp.zeros_like(r.rows_sum)

    def attention(seq):
        def project(step):
            turn = (1 - step // 2) * (3 - step) + (step // 2) * (step - 2)
            gathers[0].wait(seq, turn)
            share = group.share(turn)
            result = dot_nt(r.full_frames[seq, share], r.wide_weight[...]) + r.projection_bias[...]
            place = lax.broadcasted_iota(jnp.int32, (rows, lanes), 0)
            dead = (place >= share_rows) | (place + share * share_rows >= r.lengths[seq])
            flag = jnp.where(dead & (lane_index(rows, lanes) == heads_width), MASKED, 0.0)
            r.projected[seq, at_share(share), 0:lanes] = (
                result[:, :lanes].astype(BF) * HEAD_DIM ** (-0.5)
            ).astype(BF)
            r.projected[seq, at_share(share), lanes : 2 * lanes] = (
                result[:, lanes : 2 * lanes] + flag
            ).astype(BF)
            r.projected[seq, at_share(share), 2 * lanes : 3 * lanes] = result[:, 2 * lanes :].astype(BF)

        turns(project)

        def attend(block, carry):
            chip = (1 - group.y) * (1 - block) + group.y * block
            span = pl.ds(pl.multiple_of(chip * 2 * rows, 16), 2 * rows)
            queries = r.projected[seq, span, 0:lanes]
            lane = lane_index(2 * rows, lanes)
            mixed = jnp.zeros((2 * rows, lanes), F32)
            for head in range(heads):
                inside = lane // HEAD_DIM == head
                picked = jnp.where(inside | (lane == heads_width), queries, jnp.zeros_like(queries))
                scores = dot_nt(picked, r.projected[seq, :, lanes : 2 * lanes])
                top = jnp.max(scores, axis=-1, keepdims=True)
                exponent = jnp.exp(scores - top)
                weight = jnp.sum(exponent, axis=-1, keepdims=True)
                r.log_total[seq, chip, head : head + 1] = jnp.transpose(top + jnp.log(weight))
                part = dot(exponent.astype(BF), r.projected[seq, :, 2 * lanes : 3 * lanes])
                mixed = jnp.where(inside, part * (1.0 / weight), mixed)
            r.context[seq, span] = mixed.astype(BF)
            for half in range(2):
                turn = 2 * block + half
                mixed = r.context[seq, at_share(group.share(turn))]
                scatters[0].put(seq, turn, dot(mixed, r.wide_out[...]))
            return carry

        lax.fori_loop(0, 2, attend, 0)

    each(attention)

    def first_norm(seq):
        attended = scatters[0].take(seq)
        normed, inverse = norm(r.full_frames[seq, group.own].astype(F32) + attended + out_bias)
        r.first_normed[seq] = normed
        r.first_inverse[seq] = inverse
        r.first_full[seq, group.own] = (normed * first_gain + first_shift).astype(BF)
        gathers[1].start(seq)

    loaded()
    out_bias, first_gain, first_shift, down_bias, second_gain, second_shift, up_bias = (
        row[...].reshape(1, row.shape[0])
        for row in (
            r.out_bias, r.first_gain, r.first_shift, r.down_bias, r.second_gain, r.second_shift, r.up_bias,
        )
    )
    each(first_norm)

    def feed(seq):
        def step(turn):
            gathers[1].wait(seq, turn)
            share = group.share(turn)
            inner = dot(r.first_full[seq, share], r.up_weight[...]) + up_bias
            r.hidden[seq, at_share(share)] = inner
            active = (0.5 * inner * (1.0 + lax.erf(inner * ROOT_HALF))).astype(BF)
            r.activated[seq, at_share(share)] = active
            scatters[1].put(seq, turn, dot(active, r.down_weight[...]))

        turns(step)

    each(feed)

    def second_norm(seq):
        mixed = scatters[1].take(seq)
        first = r.first_normed[seq] * first_gain + first_shift
        normed, inverse = norm(first + mixed + down_bias)
        place = lax.broadcasted_iota(jnp.int32, (rows, width), 0)
        live = (place < share_rows) & (place + group.own * share_rows < r.lengths[seq])
        grad = jnp.where(live, pad_rows(r.cotangent[seq], rows), 0.0)
        back = norm_back(grad, normed, inverse, second_gain)
        r.grad_mixed[seq, group.own] = back.astype(BF)
        gathers[2].start(seq)
        r.grad_rows[seq] = back
        r.output_rows[seq] = (normed * second_gain + second_shift)[:share_rows].astype(BF)
        r.rows_sum[0:1] += sum_rows(grad * normed)
        r.rows_sum[1:2] += sum_rows(grad)
        r.rows_sum[2:3] += sum_rows(back)

    each(second_norm)

    def feed_back(seq):
        def step(turn):
            gathers[2].wait(seq, turn)
            share = group.share(turn)
            grad_active = dot_nt(r.grad_mixed[seq, share], r.down_weight[...])
            inner = r.hidden[seq, at_share(share)]
            slope = (
                0.5 * (1.0 + lax.erf(inner * ROOT_HALF))
                + inner * jnp.exp(-0.5 * inner * inner) * INVERSE_ROOT_TAU
            )
            grad = (grad_active * slope).astype(BF)
            r.grad_hidden[seq, at_share(share)] = grad
            r.rows_sum[6:7] += sum_rows(grad.astype(F32))
            scatters[2].put(seq, turn, dot_nt(grad, r.up_weight[...]))

        turns(step)

    each(feed_back)

    def feed_weights(seq):
        down = dot_tn(r.activated[seq], r.grad_mixed[seq].reshape(length, width))
        r.down_grad[...] = down if seq == 0 else r.down_grad[...] + down
        up = dot_tn(r.first_full[seq].reshape(length, width), r.grad_hidden[seq])
        r.up_grad[...] = up if seq == 0 else r.up_grad[...] + up

    def first_back(seq):
        grad = r.grad_rows[seq] + scatters[2].take(seq)
        normed = r.first_normed[seq]
        back = norm_back(grad, normed, r.first_inverse[seq], first_gain)
        r.grad_full[seq, group.own] = back.astype(BF)
        gathers[3].start(seq)
        r.grad_rows[seq] = back
        r.rows_sum[3:4] += sum_rows(grad * normed)
        r.rows_sum[4:5] += sum_rows(grad)
        r.rows_sum[5:6] += sum_rows(back)

    queue = []

    def poll(times=1):
        for _ in range(times):
            if queue:
                queue.pop(0)()

    for seq in range(seqs):
        feed_weights(seq)
    if count:
        def make_rings(owns, opening, landed, shared, index):
            return [
                Ring(
                    group,
                    count,
                    owns,
                    opening.at[part],
                    landed.at[part],
                    shared.at[part],
                    (r.ring_send.at[index, 0], r.ring_send.at[index, 1]),
                    (r.ring_recv.at[index, part, 0], r.ring_recv.at[index, part, 1]),
                    part * landed.shape[4],
                )
                for part in range(landed.shape[0])
            ]

        rings = make_rings(
            (r.up_grad, r.down_grad), r.feed_opening, r.feed_landed, r.feed_shared, 0
        )
        late_rings = make_rings(
            (heads_grad,), r.heads_opening, r.heads_landed, r.heads_shared, 1
        )
        for ring in rings:
            ring.open()
        for step in range(2 * (count - 1)):
            for ring in rings:
                queue.append(functools.partial(ring.advance, step))
    for seq in range(seqs):
        poll(POLLS[0])
        first_back(seq)
    poll(POLLS[0])
    if count:
        totals = Totals(
            group, pairs, r.small_out, r.small_in, r.small_send, r.small_recv, 6
        )
        totals.begin(0, r.rows_sum[...])
    heads_grad[...] = jnp.zeros_like(heads_grad)

    def output_copy(seq):
        return pltpu.make_async_copy(r.output_rows.at[seq], r.layer_output.at[seq], r.out_sem.at[3, seq])

    def input_copy(seq):
        return pltpu.make_async_copy(r.input_rows.at[seq], r.input_grad.at[seq], r.out_sem.at[4, seq])

    def store_input(seq):
        r.input_rows[seq] = (scatters[3].take(seq) + r.grad_rows[seq])[:share_rows]
        input_copy(seq).start()

    for seq in range(seqs):
        output_copy(seq).start()

        def step(turn):
            gathers[3].wait(seq, turn)
            share = group.share(turn)
            r.grad_context[at_share(share)] = dot_nt(r.grad_full[seq, share], r.wide_out[...]).astype(BF)
            heads_grad[3 * heads_width :] += dot_tn(
                r.context[seq, at_share(share)], r.grad_full[seq, share]
            )[:heads_width]

        turns(step)
        poll(POLLS[1])
        grad_total[...] = jnp.zeros_like(grad_total)
        keys = r.projected[seq, :, lanes : 2 * lanes]
        lane = lane_index(length, lanes)
        key_columns = jnp.transpose(keys.astype(F32) * HEAD_DIM ** (-0.5)).astype(BF)
        for head in range(heads):
            inside = lane // HEAD_DIM == head
            queries = r.projected[seq, :, 0:lanes]
            picked = jnp.where(inside | (lane == heads_width), queries, jnp.zeros_like(queries))
            row = jnp.concatenate(
                [r.log_total[seq, chip, head : head + 1] for chip in range(2)], axis=1
            )
            weights = jnp.exp(dot_nt(keys, picked) - row)
            grads = r.grad_context[...]
            part = dot(weights.astype(BF), grads)
            span = slice(2 * lanes, 3 * lanes)
            grad_total[:, span] = jnp.where(inside, part, grad_total[:, span])
            poll(POLLS[2])
            slopes = weights * dot_nt(
                r.projected[seq, :, 2 * lanes : 3 * lanes],
                jnp.where(inside, grads, jnp.zeros_like(grads)),
            )
            slopes = (slopes - weights * jnp.sum(slopes, axis=0, keepdims=True)).astype(BF)
            part = dot(slopes, queries)
            span = slice(lanes, 2 * lanes)
            grad_total[:, span] = jnp.where(inside, part, grad_total[:, span])
            span = slice(head * HEAD_DIM, (head + 1) * HEAD_DIM)
            grad_total[:, span] = jnp.transpose(dot(key_columns[span], slopes))
            poll(POLLS[3])

        def finish(turn):
            share = group.share(turn)
            grads = grad_total[at_share(share)].astype(BF)
            grad_projected[at_share(share)] = grads
            r.rows_sum[7:8] += sum_rows(grads.astype(F32))
            scatters[3].put(seq, turn, dot(grads, r.wide_weight[...]))

        turns(finish)
        poll(POLLS[4])
        for index in range(3):
            heads_grad[index * heads_width : (index + 1) * heads_width] += dot_tn(
                grad_projected[:, index * lanes : (index + 1) * lanes],
                r.full_frames[seq].reshape(length, width),
            )[:heads_width]
        poll(POLLS[5])
        if seq == 0:
            if count:
                totals.begin(1, totals.end(0))
        else:
            store_input(seq - 1)

    if count:
        for ring in late_rings:
            ring.open()
        place = lax.broadcasted_iota(jnp.int32, r.rows_sum.shape, 0)
        totals.begin(2, jnp.where(place == 7, r.rows_sum[...], totals.end(1)))
        copies = [
            pltpu.make_async_copy(shared, out, r.out_sem.at[index, 0])
            for index, (shared, out) in enumerate(
                ((r.feed_shared, r.feed_sum), (r.heads_shared, r.heads_sum))
            )
        ]
        level = 2
        last = len(pairs) + 1
        for step in range(2 * (count - 1)):
            for ring in late_rings:
                ring.advance(step)
                poll()
            if step == 2:
                store_input(seqs - 1)
            if step % 3 == 2 and level <= last:
                rows_total = totals.end(level)
                level += 1
                if level <= last:
                    totals.begin(level, rows_total)
                else:
                    r.sums[...] = rows_total
        poll(len(queue))
        for copy in copies:
            copy.start()
        rings[0].wait_sends(r.feed_landed)
        late_rings[0].wait_sends(r.heads_landed)
    else:
        store_input(seqs - 1)
        r.sums[...] = r.rows_sum[...]
        copies = [
            pltpu.make_async_copy(own, out, r.out_sem.at[index, 0])
            for index, (own, out) in enumerate(
                ((r.up_grad, r.up_sum), (r.down_grad, r.down_sum), (heads_grad, r.heads_sum))
            )
        ]
        for copy in copies:
            copy.start()
    for seq in range(seqs):
        for gather in gathers:
            gather.close(seq)
        output_copy(seq).wait()
        input_copy(seq).wait()
    for copy in copies:
        copy.wait()


VMEM_SPEC = pl.BlockSpec(memory_space=pltpu.VMEM)
ANY_SPEC = pl.BlockSpec(memory_space=pl.ANY)


def widen(columns, refs, *rest):
    r = types.SimpleNamespace(**dict(zip(refs, rest)))
    heads_width = r.query_bias.shape[0]
    width = r.up.shape[1]
    plain = [
        (r.layer_in, r.layer_stage, r.layer_output),
        (r.input_in, r.input_stage, r.input_grad),
    ]
    plain_loads = [
        pltpu.make_async_copy(source, stage, r.plain_sem.at[index])
        for index, (source, stage, _) in enumerate(plain)
    ]
    loads = []
    for index, (source, which) in enumerate(((r.feed_in, 0), (r.feed_in, 1), (r.heads_in, 0))):
        loads.append(
            [
                pltpu.make_async_copy(
                    source.at[part, :, :, which],
                    r.narrow.at[index, :, :, pl.ds(part * 16, 16)],
                    r.load_sem.at[index, part],
                )
                for part in range(source.shape[0])
            ]
        )
    for copy in sum(loads, plain_loads):
        copy.start()
    stores = []
    for index, pieces in enumerate(loads):
        for load in pieces:
            load.wait()
        r.wide[index] = r.narrow[index].astype(F32).reshape(width, width)
        if index < 2:
            parts = [(r.wide.at[index], (r.up, r.down)[index])]
        else:
            parts = [
                (r.wide.at[index, pl.ds(part * heads_width, heads_width)], target)
                for part, target in enumerate((r.query, r.key, r.value, r.out))
            ]
        for source, target in parts:
            store = pltpu.make_async_copy(source, target, r.store_sem.at[len(stores)])
            store.start()
            stores.append(store)
    for load, (_, stage, target) in zip(plain_loads, plain):
        load.wait()
        store = pltpu.make_async_copy(stage, target, r.store_sem.at[len(stores)])
        store.start()
        stores.append(store)
    rows = (
        r.second_gain, r.second_shift, r.down_bias, r.first_gain, r.first_shift, r.out_bias, r.up_bias,
    )
    for index, row in enumerate(rows):
        row[...] = r.sums[index]
    r.query_bias[...] = r.sums[7, 0:heads_width]
    r.value_bias[...] = r.sums[7, columns : columns + heads_width]
    for copy in stores:
        copy.wait()


def shards(
    frames,
    cotangent,
    lengths,
    query_weight,
    query_bias,
    key_weight,
    value_weight,
    value_bias,
    out_weight,
    out_bias,
    first_gain,
    first_shift,
    up_weight,
    up_bias,
    down_weight,
    down_bias,
    second_gain,
    second_shift,
):
    seqs, share_rows, width = frames.shape
    rows = up_to(share_rows, 16)
    length = 4 * rows
    heads_width = query_weight.shape[1]
    inner = up_weight.shape[1]
    lanes = up_to(heads_width + 1, 128)
    shape = jax.ShapeDtypeStruct
    count = lax.axis_size("dp")
    ringed = count & (count - 1) == 0 and width % (32 * count) == 0
    half = width // (2 * count)
    levels = 2 + count.bit_length() - 1
    full = pltpu.VMEM((seqs, 4, rows, width), BF)
    part = pltpu.VMEM((seqs, rows, width), BF)
    stream = pltpu.VMEM((seqs, rows, width), F32)
    inputs = dict(
        lengths=lengths,
        frames=frames,
        cotangent=cotangent,
        query_weight=query_weight.T,
        query_bias=query_bias,
        key_weight=key_weight.T,
        value_weight=value_weight.T,
        value_bias=value_bias,
        out_weight=out_weight,
        out_bias=out_bias,
        first_gain=first_gain,
        first_shift=first_shift,
        up_weight=up_weight,
        up_bias=up_bias,
        down_weight=down_weight,
        down_bias=down_bias,
        second_gain=second_gain,
        second_shift=second_shift,
    )
    outputs = dict(
        layer_output=shape(frames.shape, BF),
        input_grad=shape(frames.shape, F32),
        sums=shape((8, width), F32),
    )
    if ringed:
        outputs.update(
            feed_sum=shape((half // 16, count, 2, 2, 16, width), BF),
            heads_sum=shape((half // 16, count, 2, 1, 16, width), BF),
        )
    else:
        outputs.update(
            {name: shape((width, width), F32) for name in ("up_sum", "down_sum", "heads_sum")}
        )
    scratch = dict(
        wide_weight=pltpu.VMEM((3 * lanes, width), BF),
        wide_out=pltpu.VMEM((lanes, width), BF),
        projection_bias=pltpu.VMEM((1, 3 * lanes), F32),
        rows_sum=pltpu.VMEM((8, width), F32),
        full_frames=full,
        first_full=full,
        grad_mixed=full,
        grad_full=full,
        projected=pltpu.VMEM((seqs, length, 3 * lanes), BF),
        context=pltpu.VMEM((seqs, length, lanes), BF),
        log_total=pltpu.VMEM((seqs, 2, 8, 2 * rows), F32),
        first_normed=stream,
        first_inverse=pltpu.VMEM((seqs, rows, 1), F32),
        grad_rows=stream,
        hidden=pltpu.VMEM((seqs, length, inner), F32),
        activated=pltpu.VMEM((seqs, length, inner), BF),
        grad_hidden=pltpu.VMEM((seqs, length, inner), BF),
        grad_context=pltpu.VMEM((length, lanes), BF),
        up_grad=pltpu.VMEM(up_weight.shape, F32),
        down_grad=pltpu.VMEM(down_weight.shape, F32),
        outgoing=pltpu.VMEM((seqs, 2, rows, width), BF),
        keep=pltpu.VMEM((seqs, 2, rows, width), F32),
        near=pltpu.VMEM((seqs, 2, rows, width), BF),
        cross=part,
        landed=part,
        gather_send=pltpu.SemaphoreType.DMA((4, seqs, 3)),
        gather_recv=pltpu.SemaphoreType.DMA((4, seqs, 3)),
        scatter_send=pltpu.SemaphoreType.DMA((4, seqs, 3)),
        scatter_recv=pltpu.SemaphoreType.DMA((4, seqs, 3)),
        out_sem=pltpu.SemaphoreType.DMA((5, seqs)),
        load_sem=pltpu.SemaphoreType.DMA((len(inputs),)),
        output_rows=pltpu.VMEM(frames.shape, BF),
        input_rows=pltpu.VMEM(frames.shape, F32),
    )
    scratch.update(
        {name: pltpu.VMEM(item.shape, item.dtype) for name, item in inputs.items() if name != "lengths"}
    )
    given = [name if name == "lengths" else name + "_from" for name in inputs]
    if ringed:
        parts = half // 16
        scratch.update(
            feed_opening=pltpu.VMEM((parts, 2, 2, 16, width), BF),
            heads_opening=pltpu.VMEM((parts, 2, 1, 16, width), BF),
            feed_landed=pltpu.VMEM((parts, 2, count - 1, 2, 16, width), BF),
            heads_landed=pltpu.VMEM((parts, 2, count - 1, 1, 16, width), BF),
            feed_shared=pltpu.VMEM((parts, count, 2, 2, 16, width), BF),
            heads_shared=pltpu.VMEM((parts, count, 2, 1, 16, width), BF),
            ring_send=pltpu.SemaphoreType.DMA((2, 2)),
            ring_recv=pltpu.SemaphoreType.DMA((2, parts, 2, 2, count - 1)),
            small_out=pltpu.VMEM((levels, 8, width), F32),
            small_in=pltpu.VMEM((levels, 8, width), F32),
            small_send=pltpu.SemaphoreType.DMA((levels,)),
            small_recv=pltpu.SemaphoreType.DMA((levels,)),
        )
    outs = pl.pallas_call(
        functools.partial(layer, count if ringed else 0, [*given, *outputs, *scratch]),
        out_shape=list(outputs.values()),
        in_specs=[pl.BlockSpec(memory_space=pltpu.SMEM)] + [ANY_SPEC] * (len(inputs) - 1),
        out_specs=[VMEM_SPEC if name == "sums" else ANY_SPEC for name in outputs],
        scratch_shapes=list(scratch.values()),
        compiler_params=pltpu.CompilerParams(
            collective_id=0, has_side_effects=True, vmem_limit_bytes=VMEM_BYTES
        ),
        name="layer",
    )(*inputs.values())
    layer_output, input_grad, sums = outs[:3]
    if not ringed:
        up_grad, down_grad, heads_grad = lax.psum(tuple(outs[3:]), "dp")
        sums = lax.psum(sums, "dp")
        sums = jnp.concatenate([lax.psum(sums[:6], "tensor"), sums[6:]])
        parts = [heads_grad[index * heads_width : (index + 1) * heads_width] for index in range(4)]
        return (
            layer_output, input_grad, parts[0].T, sums[7, :heads_width], parts[1].T, parts[2].T,
            sums[7, 2 * lanes : 2 * lanes + heads_width], parts[3], sums[5], sums[3], sums[4],
            up_grad, sums[6], down_grad, sums[2], sums[0], sums[1],
        )
    row = shape((width,), F32)
    side_row = shape((heads_width,), F32)
    block = shape((heads_width, width), F32)
    square = shape((width, width), F32)
    results = dict(
        layer_output=shape(frames.shape, BF),
        input_grad=shape(frames.shape, F32),
        query=block,
        query_bias=side_row,
        key=block,
        value=block,
        value_bias=side_row,
        out=block,
        out_bias=row,
        first_gain=row,
        first_shift=row,
        up=square,
        up_bias=row,
        down=square,
        down_bias=row,
        second_gain=row,
        second_shift=row,
    )
    given = ["layer_in", "input_in", "sums", "feed_in", "heads_in"]
    buffers = dict(
        narrow=pltpu.VMEM((3, count, 2, half, width), BF),
        wide=pltpu.VMEM((3, width, width), F32),
        plain_sem=pltpu.SemaphoreType.DMA((2,)),
        load_sem=pltpu.SemaphoreType.DMA((3, half // 16)),
        store_sem=pltpu.SemaphoreType.DMA((8,)),
        layer_stage=pltpu.VMEM(frames.shape, BF),
        input_stage=pltpu.VMEM(frames.shape, F32),
    )
    final = pl.pallas_call(
        functools.partial(widen, 2 * lanes, [*given, *results, *buffers]),
        out_shape=list(results.values()),
        in_specs=[ANY_SPEC] * 2 + [VMEM_SPEC] + [ANY_SPEC] * 2,
        out_specs=[VMEM_SPEC if len(item.shape) == 1 else ANY_SPEC for item in results.values()],
        scratch_shapes=list(buffers.values()),
        compiler_params=pltpu.CompilerParams(vmem_limit_bytes=VMEM_BYTES),
        name="widen",
    )(layer_output, input_grad, sums, *outs[3:])
    final = dict(zip(results, final))
    for name in ("query", "key", "value"):
        final[name] = final[name].T
    return tuple(final.values())


def solution(mesh):
    return jax.shard_map(
        shards,
        mesh=mesh,
        in_specs=(
            P("dp", "tensor", None),
            P("dp", "tensor", None),
            P("dp"),
            P(None, "tensor"),
            P("tensor"),
            P(None, "tensor"),
            P(None, "tensor"),
            P("tensor"),
            P("tensor", None),
            P(),
            P(),
            P(),
            P(None, "tensor"),
            P("tensor"),
            P("tensor", None),
            P(),
            P(),
            P(),
        ),
        out_specs=(
            P("dp", "tensor", None),
            P("dp", "tensor", None),
            P(None, "tensor"),
            P("tensor"),
            P(None, "tensor"),
            P(None, "tensor"),
            P("tensor"),
            P("tensor", None),
            P(),
            P(),
            P(),
            P(None, "tensor"),
            P("tensor"),
            P("tensor", None),
            P(),
            P(),
            P(),
        ),
        check_vma=False,
    )
```

```python
import functools
import types

import jax
import jax.numpy as jnp
from jax import lax
from jax.experimental import pallas as pl
from jax.experimental.pallas import tpu as pltpu
from jax.sharding import PartitionSpec as P

MESH = pl.DeviceIdType.MESH
HEAD_DIM = 64
EPSILON = 1e-05
ROOT_HALF = 0.7071067811865476
INVERSE_ROOT_TAU = 0.3989422804014327
MASKED = -1e30
VMEM_BYTES = 62 << 20
POLLS = (3, 1, 0, 1, 1, 1, 2)
TAIL = (
    (1, 1), (0, 3), (2, 1), (1, 2), (3, 1), (2, 2), (1, 3), (3, 2), (2, 3), (3, 3),
)
BF = jnp.bfloat16
F32 = jnp.float32


def up_to(size, unit):
    return (size + unit - 1) // unit * unit


def dot(left, right):
    return jnp.dot(left, right, preferred_element_type=F32)


def dot_nt(left, right):
    return lax.dot_general(left, right, (((1,), (1,)), ((), ())), preferred_element_type=F32)


def dot_tn(left, right):
    return lax.dot_general(left, right, (((0,), (0,)), ((), ())), preferred_element_type=F32)


def pad_rows(rows, size):
    extra = size - rows.shape[0]
    if extra == 0:
        return rows
    return jnp.concatenate([rows, jnp.zeros((extra, rows.shape[1]), rows.dtype)], axis=0)


class Group:
    def __init__(self):
        self.dp = lax.axis_index("dp")
        self.own = lax.axis_index("tensor")
        self.y = self.own // 2
        self.core = self.own % 2
        self.mate = self.y * 2 + (1 - self.core)
        self.far = (1 - self.y) * 2 + self.core

    def greet(self, dp_peers):
        barrier = pltpu.get_barrier_semaphore()
        peers = [(self.dp, self.mate), (self.dp, self.far)] + [(peer, self.own) for peer in dp_peers]
        for peer in peers:
            pl.semaphore_signal(barrier, inc=1, device_id=peer, device_id_type=MESH)
        return lambda: pl.semaphore_wait(barrier, len(peers))

    def share(self, turn):
        late = turn // 2
        other = ((turn + 1) // 2) % 2
        ybit = (1 - self.y) * (1 - late) + self.y * late
        core = self.core * (1 - other) + (1 - self.core) * other
        return ybit * 2 + core

    def copy(self, source, target, send, recv, peer):
        return pltpu.make_async_remote_copy(
            src_ref=source,
            dst_ref=target,
            send_sem=send,
            recv_sem=recv,
            device_id=(self.dp, peer),
            device_id_type=MESH,
        )


class Gather:
    def __init__(self, group, full, send, recv, real):
        self.group, self.full, self.send, self.recv = group, full, send, recv
        self.real = pl.ds(0, real)

    def _copy(self, seq, kind):
        group = self.group
        share = group.far if kind == 2 else group.own
        slot = self.full.at[seq, share, self.real] if kind == 0 else self.full.at[seq, share]
        peer = group.far if kind == 0 else group.mate
        return group.copy(slot, slot, self.send.at[seq, kind], self.recv.at[seq, kind], peer)

    def start(self, seq):
        self._copy(seq, 0).start()
        self._copy(seq, 1).start()

    def wait(self, seq, turn):
        @pl.when(turn == 0)
        def _():
            self._copy(seq, 0).wait_recv()
            self._copy(seq, 2).start()

        @pl.when(turn == 1)
        def _():
            self._copy(seq, 2).wait_recv()

        @pl.when(turn == 2)
        def _():
            self._copy(seq, 1).wait_recv()

    def close(self, seq):
        for kind in range(3):
            self._copy(seq, kind).wait_send()


class Scatter:
    def __init__(self, group, buffers, send, recv, real):
        self.group = group
        self.real = pl.ds(0, real)
        self.outgoing, self.keep, self.near, self.cross, self.landed = buffers
        self.send, self.recv = send, recv

    def _near(self, seq, index):
        return self.group.copy(
            self.outgoing.at[seq, index],
            self.near.at[seq, index],
            self.send.at[seq, index],
            self.recv.at[seq, index],
            self.group.mate,
        )

    def _cross(self, seq):
        return self.group.copy(
            self.cross.at[seq, self.real],
            self.landed.at[seq, self.real],
            self.send.at[seq, 2],
            self.recv.at[seq, 2],
            self.group.far,
        )

    def put(self, seq, turn, terms):
        @pl.when((turn == 0) | (turn == 3))
        def _():
            self.keep[seq, turn // 3] = terms

        @pl.when((turn == 1) | (turn == 2))
        def _():
            self.outgoing[seq, turn - 1] = terms.astype(BF)
            self._near(seq, turn - 1).start()

        @pl.when(turn == 2)
        def _():
            self._near(seq, 0).wait_recv()
            total = self.keep[seq, 0] + self.near[seq, 0].astype(F32)
            self.cross[seq] = total.astype(BF)
            self._cross(seq).start()

    def take(self, seq):
        self._near(seq, 1).wait_recv()
        self._cross(seq).wait_recv()
        for index in range(2):
            self._near(seq, index).wait_send()
        self._cross(seq).wait_send()
        return (
            self.keep[seq, 1]
            + self.near[seq, 1].astype(F32)
            + self.landed[seq].astype(F32)
        )


def norm(rows):
    centred = rows - jnp.mean(rows, axis=-1, keepdims=True)
    inverse = lax.rsqrt(jnp.mean(centred * centred, axis=-1, keepdims=True) + EPSILON)
    return centred * inverse, inverse


def norm_back(grad, normed, inverse, gain):
    scaled = grad * gain
    return inverse * (
        scaled
        - jnp.mean(scaled, axis=-1, keepdims=True)
        - normed * jnp.mean(scaled * normed, axis=-1, keepdims=True)
    )


def sum_rows(rows):
    return jnp.sum(rows, axis=0, keepdims=True)


def lane_index(rows, lanes):
    return lax.broadcasted_iota(jnp.int32, (rows, lanes), 1)


class Ring:
    def __init__(self, group, count, owns, opening, landed, shared, sends, recvs, first):
        self.group, self.count, self.steps = group, count, count - 1
        self.owns, self.opening, self.landed, self.shared = owns, opening, landed, shared
        self.add_send, self.share_send = sends
        self.add_recv, self.share_recv = recvs
        self.half = owns[0].shape[0] // (2 * count)
        self.first, self.rows = first, landed.shape[3]
        self.place, self.right, self.left = ring_peers(group.dp, count)

    def _own(self, which, way, step):
        shift = self.count - 1 - step if way == 0 else 1 + step
        chunk = (self.place + shift) % self.count
        start = pl.multiple_of((2 * chunk + way) * self.half + self.first, 16)
        return self.owns[which][pl.ds(start, self.rows)]

    def _copy(self, source, target, send, recv, way):
        return pltpu.make_async_remote_copy(
            src_ref=source,
            dst_ref=target,
            send_sem=send,
            recv_sem=recv,
            device_id=(self.right if way == 0 else self.left, self.group.own),
            device_id_type=MESH,
        )

    def _add(self, way, step, source=None):
        target = self.landed.at[way, step]
        return self._copy(
            target if source is None else source, target, self.add_send, self.add_recv.at[way, step], way
        )

    def _share(self, way, step):
        shift = self.count - step if way == 0 else step
        slot = self.shared.at[(self.place + shift) % self.count, way]
        return self._copy(slot, slot, self.share_send, self.share_recv.at[way, step], way)

    def open(self):
        for way in range(2):
            for which in range(len(self.owns)):
                self.opening[way, which] = self._own(which, way, 0).astype(BF)
            self._add(way, 0, self.opening.at[way]).start()

    def advance(self, step):
        last = self.steps - 1
        for way in range(2):
            if step < self.steps:
                self._add(way, step).wait_recv()
                target = self.landed.at[way, step] if step < last else self.shared.at[self.place, way]
                for which in range(len(self.owns)):
                    total = self.landed[way, step, which].astype(F32) + self._own(which, way, step + 1)
                    target[which] = total.astype(BF)
                if step < last:
                    self._add(way, step + 1, target).start()
                else:
                    self._share(way, 0).start()
            else:
                turn = step - self.steps
                self._share(way, turn).wait_recv()
                if turn < last:
                    self._share(way, turn + 1).start()

    def wait_sends(self, landed):
        for send in (self.add_send, self.share_send):
            self._copy(landed, landed, send, self.add_recv.at[0, 0], 0).wait_send()


class Pairwise:
    def __init__(self, group, count, terms, outgoing, half, quarter, shared, send, recv):
        self.group, self.spots = group, count // 2
        self.terms, self.outgoing, self.half, self.quarter = terms, outgoing, half, quarter
        self.shared, self.send, self.recv = shared, send, recv
        self.arrays = half.shape[1]
        self.spot, self.side = group.dp // 2, group.dp % 2

    def _copy(self, source, target, index, spot, side):
        return pltpu.make_async_remote_copy(
            src_ref=source,
            dst_ref=target,
            send_sem=self.send.at[index],
            recv_sem=self.recv.at[index],
            device_id=(spot * 2 + side, self.group.own),
            device_id_type=MESH,
        )

    def _out(self):
        return self._copy(self.outgoing, self.half, 0, self.spot, 1 - self.side)

    def _add(self, offset):
        spot = (self.spot + offset) % self.spots
        return self._copy(
            self.half.at[spot], self.quarter.at[offset - 1], offset, spot, self.side
        )

    def _share(self, offset):
        spot = (self.spot + offset) % self.spots
        slot = self.shared.at[self.side, self.spot]
        return self._copy(slot, slot, self.spots - 1 + offset, spot, self.side)

    def _back(self):
        slot = self.shared.at[self.side]
        return self._copy(slot, slot, 2 * self.spots - 1, self.spot, 1 - self.side)

    def act(self, phase):
        others = range(1, self.spots)
        if phase == 0:
            for spot in range(self.spots):
                for which in range(self.arrays):
                    self.outgoing[spot, which] = self.terms(which, 1 - self.side, spot).astype(BF)
            self._out().start()
        elif phase == 1:
            self._out().wait_recv()
            for offset in others:
                spot = (self.spot + offset) % self.spots
                for which in range(self.arrays):
                    total = self.half[spot, which].astype(F32) + self.terms(which, self.side, spot)
                    self.half[spot, which] = total.astype(BF)
                self._add(offset).start()
        elif phase == 2:
            for offset in others:
                self._add(offset).wait_recv()
            for which in range(self.arrays):
                total = self.half[self.spot, which].astype(F32) + self.terms(
                    which, self.side, self.spot
                )
                for offset in others:
                    total = total + self.quarter[offset - 1, which].astype(F32)
                self.shared[self.side, self.spot, which] = total.astype(BF)
            for offset in others:
                self._share(offset).start()
        elif phase == 3:
            for offset in others:
                self._share(offset).wait_recv()
            self._back().start()
        else:
            self._back().wait_recv()
            self._out().wait_send()
            self._back().wait_send()
            for offset in others:
                self._add(offset).wait_send()
                self._share(offset).wait_send()


def ring_peers(index, count):
    odd = index % 2
    place = (1 - odd) * (index // 2) + odd * (count - 1 - index // 2)

    def at(spot):
        late = spot // (count // 2)
        return (1 - late) * 2 * spot + late * (2 * (count - 1 - spot) + 1)

    return place, at((place + 1) % count), at((place + count - 1) % count)


def halving_peers(index, count):
    peers = []
    bit = 1
    while bit < count:
        peers.append(index + bit * (1 - 2 * ((index // bit) % 2)))
        bit *= 2
    return peers


class Totals:
    def __init__(self, group, peers, outgoing, arriving, send, recv, shared):
        self.group, self.shared = group, shared
        self.outgoing, self.arriving, self.send, self.recv = outgoing, arriving, send, recv
        own = group.own
        self.peers = [(group.dp, group.mate), (group.dp, group.far)] + [(peer, own) for peer in peers]

    def _copy(self, level):
        return pltpu.make_async_remote_copy(
            src_ref=self.outgoing.at[level],
            dst_ref=self.arriving.at[level],
            send_sem=self.send.at[level],
            recv_sem=self.recv.at[level],
            device_id=self.peers[level],
            device_id_type=MESH,
        )

    def begin(self, level, rows):
        self.outgoing[level] = rows
        self._copy(level).start()

    def end(self, level):
        self._copy(level).wait()
        other = self.arriving[level]
        if level < 2:
            place = lax.broadcasted_iota(jnp.int32, other.shape, 0)
            other = jnp.where(place < self.shared, other, 0.0)
        return self.outgoing[level] + other


def layer(count, names, *refs):
    r = types.SimpleNamespace(**dict(zip(names, refs)))
    loads = {
        name[:-5]: pltpu.make_async_copy(ref, getattr(r, name[:-5]), r.load_sem.at[index])
        for index, (name, ref) in enumerate(zip(names, refs))
        if name.endswith("_from")
    }

    def loaded(*wanted):
        for name in wanted or list(loads):
            loads.pop(name).wait()

    seqs, share_rows, width = r.frames.shape
    rows = r.full_frames.shape[2]
    length = 4 * rows
    heads_width = r.query_weight.shape[0]
    lanes = r.wide_weight.shape[0] // 3
    heads = heads_width // HEAD_DIM
    group = Group()
    pairs = []
    ring_sides = []
    if count:
        pairs = halving_peers(group.dp, count)
        ring_sides = list(ring_peers(group.dp, count)[1:])
        ring_sides += [
            (group.dp + 2 * offset) % count for offset in range(1, count // 2)
        ]
    tail = pl.ds(share_rows, rows - share_rows)
    if rows > share_rows:
        for full in (r.full_frames, r.first_full, r.grad_mixed, r.grad_full):
            full[:, :, tail] = jnp.zeros_like(full[:, :, tail])
        r.landed[:, tail] = jnp.zeros_like(r.landed[:, tail])
    met = group.greet(ring_sides + pairs)

    for load in loads.values():
        load.start()
    buffers = (r.outgoing, r.keep, r.near, r.cross, r.landed)
    gathers = [
        Gather(group, full, r.gather_send.at[index], r.gather_recv.at[index], share_rows)
        for index, full in enumerate((r.full_frames, r.first_full, r.grad_mixed, r.grad_full))
    ]
    scatters = [
        Scatter(group, buffers, r.scatter_send.at[index], r.scatter_recv.at[index], share_rows)
        for index in range(4)
    ]
    grad_total = r.hidden.at[0]
    heads_grad = r.hidden.at[1, pl.ds(0, 4 * heads_width)]

    def each(stage):
        def body(seq, carry):
            stage(seq)
            return carry

        lax.fori_loop(0, seqs, body, 0)

    def turns(step):
        def body(turn, carry):
            step(turn)
            return carry

        lax.fori_loop(0, 4, body, 0)

    def at_share(share):
        return pl.ds(pl.multiple_of(share * rows, 16), rows)

    def place_frames(seq):
        r.full_frames[seq, group.own] = pad_rows(r.frames[seq].astype(F32), rows).astype(BF)

    loaded("frames")
    each(place_frames)
    met()
    each(gathers[0].start)
    loaded("query_weight", "key_weight", "value_weight", "query_bias", "value_bias", "out_weight")
    r.wide_weight[...] = jnp.zeros_like(r.wide_weight)
    for index, weight in enumerate((r.query_weight, r.key_weight, r.value_weight)):
        r.wide_weight[index * lanes : index * lanes + heads_width] = weight[...]
    r.wide_out[...] = jnp.zeros_like(r.wide_out)
    r.wide_out[:heads_width] = r.out_weight[...]
    r.projection_bias[...] = jnp.where(
        lane_index(1, 3 * lanes) == heads_width, HEAD_DIM**0.5, 0.0
    )
    r.projection_bias[:, :heads_width] = r.query_bias[...].reshape(1, heads_width)
    r.projection_bias[:, 2 * lanes : 2 * lanes + heads_width] = r.value_bias[...].reshape(1, heads_width)
    r.rows_sum[...] = jnp.zeros_like(r.rows_sum)

    def attention(seq):
        def project(step):
            turn = (1 - step // 2) * (3 - step) + (step // 2) * (step - 2)
            gathers[0].wait(seq, turn)
            share = group.share(turn)
            result = dot_nt(r.full_frames[seq, share], r.wide_weight[...]) + r.projection_bias[...]
            place = lax.broadcasted_iota(jnp.int32, (rows, lanes), 0)
            dead = (place >= share_rows) | (place + share * share_rows >= r.lengths[seq])
            flag = jnp.where(dead & (lane_index(rows, lanes) == heads_width), MASKED, 0.0)
            r.projected[seq, at_share(share), 0:lanes] = (
                result[:, :lanes].astype(BF) * HEAD_DIM ** (-0.5)
            ).astype(BF)
            r.projected[seq, at_share(share), lanes : 2 * lanes] = (
                result[:, lanes : 2 * lanes] + flag
            ).astype(BF)
            r.projected[seq, at_share(share), 2 * lanes : 3 * lanes] = result[:, 2 * lanes :].astype(BF)

        turns(project)

        def attend(block, carry):
            chip = (1 - group.y) * (1 - block) + group.y * block
            span = pl.ds(pl.multiple_of(chip * 2 * rows, 16), 2 * rows)
            queries = r.projected[seq, span, 0:lanes]
            lane = lane_index(2 * rows, lanes)
            mixed = jnp.zeros((2 * rows, lanes), F32)
            for head in range(heads):
                inside = lane // HEAD_DIM == head
                picked = jnp.where(inside | (lane == heads_width), queries, jnp.zeros_like(queries))
                scores = dot_nt(picked, r.projected[seq, :, lanes : 2 * lanes])
                top = jnp.max(scores, axis=-1, keepdims=True)
                exponent = jnp.exp(scores - top)
                weight = jnp.sum(exponent, axis=-1, keepdims=True)
                r.log_total[seq, chip, head : head + 1] = jnp.transpose(top + jnp.log(weight))
                part = dot(exponent.astype(BF), r.projected[seq, :, 2 * lanes : 3 * lanes])
                mixed = jnp.where(inside, part * (1.0 / weight), mixed)
            r.context[seq, span] = mixed.astype(BF)
            for half in range(2):
                turn = 2 * block + half
                mixed = r.context[seq, at_share(group.share(turn))]
                scatters[0].put(seq, turn, dot(mixed, r.wide_out[...]))
            return carry

        lax.fori_loop(0, 2, attend, 0)

    each(attention)

    def first_norm(seq):
        attended = scatters[0].take(seq)
        normed, inverse = norm(r.full_frames[seq, group.own].astype(F32) + attended + out_bias)
        r.first_normed[seq] = normed
        r.first_inverse[seq] = inverse
        r.first_full[seq, group.own] = (normed * first_gain + first_shift).astype(BF)
        gathers[1].start(seq)

    loaded()
    out_bias, first_gain, first_shift, down_bias, second_gain, second_shift, up_bias = (
        row[...].reshape(1, row.shape[0])
        for row in (
            r.out_bias, r.first_gain, r.first_shift, r.down_bias, r.second_gain, r.second_shift, r.up_bias,
        )
    )
    each(first_norm)

    def feed(seq):
        def step(turn):
            gathers[1].wait(seq, turn)
            share = group.share(turn)
            inner = dot(r.first_full[seq, share], r.up_weight[...]) + up_bias
            r.hidden[seq, at_share(share)] = inner
            active = (0.5 * inner * (1.0 + lax.erf(inner * ROOT_HALF))).astype(BF)
            r.activated[seq, at_share(share)] = active
            scatters[1].put(seq, turn, dot(active, r.down_weight[...]))

        turns(step)

    each(feed)

    def second_norm(seq):
        mixed = scatters[1].take(seq)
        first = r.first_normed[seq] * first_gain + first_shift
        normed, inverse = norm(first + mixed + down_bias)
        place = lax.broadcasted_iota(jnp.int32, (rows, width), 0)
        live = (place < share_rows) & (place + group.own * share_rows < r.lengths[seq])
        grad = jnp.where(live, pad_rows(r.cotangent[seq], rows), 0.0)
        back = norm_back(grad, normed, inverse, second_gain)
        r.grad_mixed[seq, group.own] = back.astype(BF)
        gathers[2].start(seq)
        r.grad_rows[seq] = back
        r.frames[seq] = (normed * second_gain + second_shift)[:share_rows].astype(BF)
        r.rows_sum[0:1] += sum_rows(grad * normed)
        r.rows_sum[1:2] += sum_rows(grad)
        r.rows_sum[2:3] += sum_rows(back)

    each(second_norm)

    def feed_back(seq):
        def step(turn):
            gathers[2].wait(seq, turn)
            share = group.share(turn)
            grad_active = dot_nt(r.grad_mixed[seq, share], r.down_weight[...])
            inner = r.hidden[seq, at_share(share)]
            slope = (
                0.5 * (1.0 + lax.erf(inner * ROOT_HALF))
                + inner * jnp.exp(-0.5 * inner * inner) * INVERSE_ROOT_TAU
            )
            grad = (grad_active * slope).astype(BF)
            r.grad_hidden[seq, at_share(share)] = grad
            r.rows_sum[6:7] += sum_rows(grad.astype(F32))
            scatters[2].put(seq, turn, dot_nt(grad, r.up_weight[...]))

        turns(step)

    each(feed_back)

    def feed_weights(seq):
        down = dot_tn(r.activated[seq], r.grad_mixed[seq].reshape(length, width))
        r.down_grad[...] = down if seq == 0 else r.down_grad[...] + down
        up = dot_tn(r.first_full[seq].reshape(length, width), r.grad_hidden[seq])
        r.up_grad[...] = up if seq == 0 else r.up_grad[...] + up

    def first_back(seq):
        grad = r.grad_rows[seq] + scatters[2].take(seq)
        normed = r.first_normed[seq]
        back = norm_back(grad, normed, r.first_inverse[seq], first_gain)
        r.grad_full[seq, group.own] = back.astype(BF)
        gathers[3].start(seq)
        r.grad_rows[seq] = back
        r.rows_sum[3:4] += sum_rows(grad * normed)
        r.rows_sum[4:5] += sum_rows(grad)
        r.rows_sum[5:6] += sum_rows(back)

    queue = []

    def poll(times=1):
        for _ in range(times):
            if queue:
                queue.pop(0)()

    def act(part, phase):
        if count:
            pieces[part].act(phase)

    for seq in range(seqs):
        feed_weights(seq)
    if count:
        def make_rings(owns, opening, landed, shared, index):
            return [
                Ring(
                    group,
                    count,
                    owns,
                    opening.at[part],
                    landed.at[part],
                    shared.at[part],
                    (r.ring_send.at[index, 0], r.ring_send.at[index, 1]),
                    (r.ring_recv.at[index, part, 0], r.ring_recv.at[index, part, 1]),
                    part * landed.shape[4],
                )
                for part in range(landed.shape[0])
            ]

        rings = make_rings(
            (r.up_grad, r.down_grad), r.feed_opening, r.feed_landed, r.feed_shared, 0
        )
        def heads_terms(first, size, which, side, spot):
            start = first + (side * (count // 2) + spot) * size
            return heads_grad[pl.ds(pl.multiple_of(start, 8), size)]

        pieces = [
            Pairwise(
                group,
                count,
                functools.partial(heads_terms, part * heads_width, r.heads_half.shape[3]),
                r.heads_out.at[part],
                r.heads_half.at[part],
                r.heads_quarter.at[part],
                r.heads_shared.at[part],
                r.pair_send.at[part],
                r.pair_recv.at[part],
            )
            for part in range(1 + heads)
        ]
        for ring in rings:
            ring.open()
        for step in range(2 * (count - 1)):
            for ring in rings:
                queue.append(functools.partial(ring.advance, step))
    for seq in range(seqs):
        poll(POLLS[0])
        first_back(seq)
    poll(POLLS[0])
    if count:
        totals = Totals(
            group, pairs, r.small_out, r.small_in, r.small_send, r.small_recv, 6
        )
        totals.begin(0, r.rows_sum[...])
    def output_copy(seq):
        return pltpu.make_async_copy(r.frames.at[seq], r.layer_output.at[seq], r.out_sem.at[3, seq])

    def input_copy(seq):
        return pltpu.make_async_copy(r.cotangent.at[seq], r.input_grad.at[seq], r.out_sem.at[4, seq])

    def store_input(seq):
        r.cotangent[seq] = (scatters[3].take(seq) + r.grad_rows[seq])[:share_rows]
        input_copy(seq).start()

    for seq in range(seqs):
        output_copy(seq).start()

        def step(turn):
            gathers[3].wait(seq, turn)
            share = group.share(turn)
            r.grad_context[at_share(share)] = dot_nt(r.grad_full[seq, share], r.wide_out[...]).astype(BF)

        turns(step)
        part = dot_tn(r.context[seq], r.grad_full[seq].reshape(length, width))[:heads_width]
        if seq == 0:
            heads_grad[:heads_width] = part
        else:
            heads_grad[:heads_width] += part
        if seq == seqs - 1:
            act(0, 0)
        poll(POLLS[1])
        grad_total[...] = jnp.zeros_like(grad_total)
        keys = r.projected[seq, :, lanes : 2 * lanes]
        lane = lane_index(length, lanes)
        key_columns = jnp.transpose(keys.astype(F32) * HEAD_DIM ** (-0.5)).astype(BF)
        for head in range(heads):
            inside = lane // HEAD_DIM == head
            queries = r.projected[seq, :, 0:lanes]
            picked = jnp.where(inside | (lane == heads_width), queries, jnp.zeros_like(queries))
            row = jnp.concatenate(
                [r.log_total[seq, chip, head : head + 1] for chip in range(2)], axis=1
            )
            weights = jnp.exp(dot_nt(keys, picked) - row)
            grads = r.grad_context[...]
            part = dot(weights.astype(BF), grads)
            span = slice(2 * lanes, 3 * lanes)
            grad_total[:, span] = jnp.where(inside, part, grad_total[:, span])
            poll(POLLS[2])
            slopes = weights * dot_nt(
                r.projected[seq, :, 2 * lanes : 3 * lanes],
                jnp.where(inside, grads, jnp.zeros_like(grads)),
            )
            slopes = (slopes - weights * jnp.sum(slopes, axis=0, keepdims=True)).astype(BF)
            part = dot(slopes, queries)
            span = slice(lanes, 2 * lanes)
            grad_total[:, span] = jnp.where(inside, part, grad_total[:, span])
            span = slice(head * HEAD_DIM, (head + 1) * HEAD_DIM)
            grad_total[:, span] = jnp.transpose(dot(key_columns[span], slopes))
            block = slice((1 + head) * heads_width, (2 + head) * heads_width)
            columns = jnp.concatenate(
                [
                    grad_total[:, index * lanes + head * HEAD_DIM : index * lanes + (head + 1) * HEAD_DIM]
                    for index in range(3)
                ],
                axis=1,
            ).astype(BF)
            part = dot_tn(columns, r.full_frames[seq].reshape(length, width))
            if seq == 0:
                heads_grad[block] = part
            else:
                heads_grad[block] += part
            if seq == seqs - 1:
                act(1 + head, 0)
                if head:
                    act(0, head)
            poll(POLLS[3])

        def finish(turn):
            share = group.share(turn)
            grads = grad_total[at_share(share)].astype(BF)
            r.rows_sum[7:8] += sum_rows(grads.astype(F32))
            scatters[3].put(seq, turn, dot(grads, r.wide_weight[...]))

        turns(finish)
        poll(POLLS[4])
        poll(POLLS[5])
        if seq == 0:
            if count:
                totals.begin(1, totals.end(0))
        else:
            store_input(seq - 1)

    if count:
        place = lax.broadcasted_iota(jnp.int32, r.rows_sum.shape, 0)
        totals.begin(2, jnp.where(place == 7, r.rows_sum[...], totals.end(1)))
        copies = [
            pltpu.make_async_copy(shared, out, r.out_sem.at[index, 0])
            for index, (shared, out) in enumerate(
                ((r.feed_shared, r.feed_sum), (r.heads_shared, r.heads_sum))
            )
        ]
        level = 2
        last = len(pairs) + 1
        for at, (part, phase) in enumerate(TAIL):
            pieces[part].act(phase)
            poll(POLLS[6])
            if at == 1:
                store_input(seqs - 1)
            if at % 2 == 1 and level <= last:
                rows_total = totals.end(level)
                level += 1
                if level <= last:
                    totals.begin(level, rows_total)
                else:
                    r.sums[...] = rows_total
        poll(len(queue))
        for piece in pieces:
            piece.act(4)
        for copy in copies:
            copy.start()
        rings[0].wait_sends(r.feed_landed)
    else:
        store_input(seqs - 1)
        r.sums[...] = r.rows_sum[...]
        copies = [
            pltpu.make_async_copy(own, out, r.out_sem.at[index, 0])
            for index, (own, out) in enumerate(
                ((r.up_grad, r.up_sum), (r.down_grad, r.down_sum), (heads_grad, r.heads_sum))
            )
        ]
        for copy in copies:
            copy.start()
    for seq in range(seqs):
        for gather in gathers:
            gather.close(seq)
        output_copy(seq).wait()
        input_copy(seq).wait()
    for copy in copies:
        copy.wait()


VMEM_SPEC = pl.BlockSpec(memory_space=pltpu.VMEM)
ANY_SPEC = pl.BlockSpec(memory_space=pl.ANY)


def widen(columns, refs, *rest):
    r = types.SimpleNamespace(**dict(zip(refs, rest)))
    heads_width = r.query_bias.shape[0]
    width = r.up.shape[1]
    plain = [
        (r.layer_in, r.layer_stage, r.layer_output),
        (r.input_in, r.input_stage, r.input_grad),
    ]
    plain_loads = [
        pltpu.make_async_copy(source, stage, r.plain_sem.at[index])
        for index, (source, stage, _) in enumerate(plain)
    ]
    loads = []
    for index, (source, which) in enumerate(((r.feed_in, 0), (r.feed_in, 1))):
        loads.append(
            [
                pltpu.make_async_copy(
                    source.at[part, :, :, which],
                    r.narrow.at[index, :, :, pl.ds(part * 16, 16)],
                    r.load_sem.at[index, part],
                )
                for part in range(source.shape[0])
            ]
        )
    heads_load = pltpu.make_async_copy(r.heads_in, r.heads, r.plain_sem.at[2])
    for copy in sum(loads, plain_loads + [heads_load]):
        copy.start()
    stores = []
    for index, pieces in enumerate(loads):
        for load in pieces:
            load.wait()
        r.wide[index] = r.narrow[index].astype(F32).reshape(width, width)
        store = pltpu.make_async_copy(r.wide.at[index], (r.up, r.down)[index], r.store_sem.at[len(stores)])
        store.start()
        stores.append(store)
    heads_load.wait()
    heads = heads_width // HEAD_DIM
    for piece in range(1 + heads):
        rows = r.heads[piece].astype(F32).reshape(heads_width, width)
        for kind in range(3):
            place = 3 * heads + kind if piece == 0 else kind * heads + piece - 1
            r.wide[2, place * HEAD_DIM : (place + 1) * HEAD_DIM] = rows[
                kind * HEAD_DIM : (kind + 1) * HEAD_DIM
            ]
    parts = [
        (r.wide.at[2, pl.ds(part * heads_width, heads_width)], target)
        for part, target in enumerate((r.query, r.key, r.value, r.out))
    ]
    for source, target in parts:
        store = pltpu.make_async_copy(source, target, r.store_sem.at[len(stores)])
        store.start()
        stores.append(store)
    for load, (_, stage, target) in zip(plain_loads, plain):
        load.wait()
        store = pltpu.make_async_copy(stage, target, r.store_sem.at[len(stores)])
        store.start()
        stores.append(store)
    rows = (
        r.second_gain, r.second_shift, r.down_bias, r.first_gain, r.first_shift, r.out_bias, r.up_bias,
    )
    for index, row in enumerate(rows):
        row[...] = r.sums[index]
    r.query_bias[...] = r.sums[7, 0:heads_width]
    r.value_bias[...] = r.sums[7, columns : columns + heads_width]
    for copy in stores:
        copy.wait()


def shards(
    frames,
    cotangent,
    lengths,
    query_weight,
    query_bias,
    key_weight,
    value_weight,
    value_bias,
    out_weight,
    out_bias,
    first_gain,
    first_shift,
    up_weight,
    up_bias,
    down_weight,
    down_bias,
    second_gain,
    second_shift,
):
    seqs, share_rows, width = frames.shape
    rows = up_to(share_rows, 16)
    length = 4 * rows
    heads_width = query_weight.shape[1]
    inner = up_weight.shape[1]
    lanes = up_to(heads_width + 1, 128)
    shape = jax.ShapeDtypeStruct
    count = lax.axis_size("dp")
    ringed = count & (count - 1) == 0 and width % (32 * count) == 0 and count >= 4
    ringed = ringed and heads_width == 3 * HEAD_DIM and heads_width % (8 * count) == 0
    half = width // (2 * count)
    heads_parts = 1 + heads_width // HEAD_DIM
    levels = 2 + count.bit_length() - 1
    full = pltpu.VMEM((seqs, 4, rows, width), BF)
    part = pltpu.VMEM((seqs, rows, width), BF)
    stream = pltpu.VMEM((seqs, rows, width), F32)
    inputs = dict(
        lengths=lengths,
        frames=frames,
        cotangent=cotangent,
        query_weight=query_weight.T,
        query_bias=query_bias,
        key_weight=key_weight.T,
        value_weight=value_weight.T,
        value_bias=value_bias,
        out_weight=out_weight,
        out_bias=out_bias,
        first_gain=first_gain,
        first_shift=first_shift,
        up_weight=up_weight,
        up_bias=up_bias,
        down_weight=down_weight,
        down_bias=down_bias,
        second_gain=second_gain,
        second_shift=second_shift,
    )
    outputs = dict(
        layer_output=shape(frames.shape, BF),
        input_grad=shape(frames.shape, F32),
        sums=shape((8, width), F32),
    )
    if ringed:
        outputs.update(
            feed_sum=shape((half // 16, count, 2, 2, 16, width), BF),
            heads_sum=shape((heads_parts, 2, count // 2, 1, heads_width // count, width), BF),
        )
    else:
        outputs.update(
            {name: shape((width, width), F32) for name in ("up_sum", "down_sum", "heads_sum")}
        )
    scratch = dict(
        wide_weight=pltpu.VMEM((3 * lanes, width), BF),
        wide_out=pltpu.VMEM((lanes, width), BF),
        projection_bias=pltpu.VMEM((1, 3 * lanes), F32),
        rows_sum=pltpu.VMEM((8, width), F32),
        full_frames=full,
        first_full=full,
        grad_mixed=full,
        grad_full=full,
        projected=pltpu.VMEM((seqs, length, 3 * lanes), BF),
        context=pltpu.VMEM((seqs, length, lanes), BF),
        log_total=pltpu.VMEM((seqs, 2, 8, 2 * rows), F32),
        first_normed=stream,
        first_inverse=pltpu.VMEM((seqs, rows, 1), F32),
        grad_rows=stream,
        hidden=pltpu.VMEM((seqs, length, inner), F32),
        activated=pltpu.VMEM((seqs, length, inner), BF),
        grad_hidden=pltpu.VMEM((seqs, length, inner), BF),
        grad_context=pltpu.VMEM((length, lanes), BF),
        up_grad=pltpu.VMEM(up_weight.shape, F32),
        down_grad=pltpu.VMEM(down_weight.shape, F32),
        outgoing=pltpu.VMEM((seqs, 2, rows, width), BF),
        keep=pltpu.VMEM((seqs, 2, rows, width), F32),
        near=pltpu.VMEM((seqs, 2, rows, width), BF),
        cross=part,
        landed=part,
        gather_send=pltpu.SemaphoreType.DMA((4, seqs, 3)),
        gather_recv=pltpu.SemaphoreType.DMA((4, seqs, 3)),
        scatter_send=pltpu.SemaphoreType.DMA((4, seqs, 3)),
        scatter_recv=pltpu.SemaphoreType.DMA((4, seqs, 3)),
        out_sem=pltpu.SemaphoreType.DMA((5, seqs)),
        load_sem=pltpu.SemaphoreType.DMA((len(inputs),)),
    )
    scratch.update(
        {name: pltpu.VMEM(item.shape, item.dtype) for name, item in inputs.items() if name != "lengths"}
    )
    given = [name if name == "lengths" else name + "_from" for name in inputs]
    if ringed:
        parts = half // 16
        spots, small = count // 2, heads_width // count
        scratch.update(
            feed_opening=pltpu.VMEM((parts, 2, 2, 16, width), BF),
            heads_out=pltpu.VMEM((heads_parts, spots, 1, small, width), BF),
            heads_half=pltpu.VMEM((heads_parts, spots, 1, small, width), BF),
            feed_landed=pltpu.VMEM((parts, 2, count - 1, 2, 16, width), BF),
            heads_quarter=pltpu.VMEM((heads_parts, spots - 1, 1, small, width), BF),
            feed_shared=pltpu.VMEM((parts, count, 2, 2, 16, width), BF),
            heads_shared=pltpu.VMEM((heads_parts, 2, spots, 1, small, width), BF),
            pair_send=pltpu.SemaphoreType.DMA((heads_parts, 2 * spots)),
            pair_recv=pltpu.SemaphoreType.DMA((heads_parts, 2 * spots)),
            ring_send=pltpu.SemaphoreType.DMA((1, 2)),
            ring_recv=pltpu.SemaphoreType.DMA((1, parts, 2, 2, count - 1)),
            small_out=pltpu.VMEM((levels, 8, width), F32),
            small_in=pltpu.VMEM((levels, 8, width), F32),
            small_send=pltpu.SemaphoreType.DMA((levels,)),
            small_recv=pltpu.SemaphoreType.DMA((levels,)),
        )
    outs = pl.pallas_call(
        functools.partial(layer, count if ringed else 0, [*given, *outputs, *scratch]),
        out_shape=list(outputs.values()),
        in_specs=[pl.BlockSpec(memory_space=pltpu.SMEM)] + [ANY_SPEC] * (len(inputs) - 1),
        out_specs=[VMEM_SPEC if name == "sums" else ANY_SPEC for name in outputs],
        scratch_shapes=list(scratch.values()),
        compiler_params=pltpu.CompilerParams(
            collective_id=0, has_side_effects=True, vmem_limit_bytes=VMEM_BYTES
        ),
        name="layer",
    )(*inputs.values())
    layer_output, input_grad, sums = outs[:3]
    if not ringed:
        up_grad, down_grad, heads_grad = lax.psum(tuple(outs[3:]), "dp")
        sums = lax.psum(sums, "dp")
        sums = jnp.concatenate([lax.psum(sums[:6], "tensor"), sums[6:]])
        mixed = heads_grad[heads_width:].reshape(-1, 3, HEAD_DIM, width)
        parts = [mixed[:, index].reshape(heads_width, width) for index in range(3)]
        parts.append(heads_grad[:heads_width])
        return (
            layer_output, input_grad, parts[0].T, sums[7, :heads_width], parts[1].T, parts[2].T,
            sums[7, 2 * lanes : 2 * lanes + heads_width], parts[3], sums[5], sums[3], sums[4],
            up_grad, sums[6], down_grad, sums[2], sums[0], sums[1],
        )
    row = shape((width,), F32)
    side_row = shape((heads_width,), F32)
    block = shape((heads_width, width), F32)
    square = shape((width, width), F32)
    results = dict(
        layer_output=shape(frames.shape, BF),
        input_grad=shape(frames.shape, F32),
        query=block,
        query_bias=side_row,
        key=block,
        value=block,
        value_bias=side_row,
        out=block,
        out_bias=row,
        first_gain=row,
        first_shift=row,
        up=square,
        up_bias=row,
        down=square,
        down_bias=row,
        second_gain=row,
        second_shift=row,
    )
    given = ["layer_in", "input_in", "sums", "feed_in", "heads_in"]
    buffers = dict(
        narrow=pltpu.VMEM((2, count, 2, half, width), BF),
        heads=pltpu.VMEM(outs[4].shape, BF),
        wide=pltpu.VMEM((3, width, width), F32),
        plain_sem=pltpu.SemaphoreType.DMA((3,)),
        load_sem=pltpu.SemaphoreType.DMA((2, half // 16)),
        store_sem=pltpu.SemaphoreType.DMA((8,)),
        layer_stage=pltpu.VMEM(frames.shape, BF),
        input_stage=pltpu.VMEM(frames.shape, F32),
    )
    final = pl.pallas_call(
        functools.partial(widen, 2 * lanes, [*given, *results, *buffers]),
        out_shape=list(results.values()),
        in_specs=[ANY_SPEC] * 2 + [VMEM_SPEC] + [ANY_SPEC] * 2,
        out_specs=[VMEM_SPEC if len(item.shape) == 1 else ANY_SPEC for item in results.values()],
        scratch_shapes=list(buffers.values()),
        compiler_params=pltpu.CompilerParams(vmem_limit_bytes=VMEM_BYTES),
        name="widen",
    )(layer_output, input_grad, sums, *outs[3:])
    final = dict(zip(results, final))
    for name in ("query", "key", "value"):
        final[name] = final[name].T
    return tuple(final.values())


def solution(mesh):
    return jax.shard_map(
        shards,
        mesh=mesh,
        in_specs=(
            P("dp", "tensor", None),
            P("dp", "tensor", None),
            P("dp"),
            P(None, "tensor"),
            P("tensor"),
            P(None, "tensor"),
            P(None, "tensor"),
            P("tensor"),
            P("tensor", None),
            P(),
            P(),
            P(),
            P(None, "tensor"),
            P("tensor"),
            P("tensor", None),
            P(),
            P(),
            P(),
        ),
        out_specs=(
            P("dp", "tensor", None),
            P("dp", "tensor", None),
            P(None, "tensor"),
            P("tensor"),
            P(None, "tensor"),
            P(None, "tensor"),
            P("tensor"),
            P("tensor", None),
            P(),
            P(),
            P(),
            P(None, "tensor"),
            P("tensor"),
            P("tensor", None),
            P(),
            P(),
            P(),
        ),
        check_vma=False,
    )
```

```python
import functools
import types

import jax
import jax.numpy as jnp
from jax import lax
from jax.experimental import pallas as pl
from jax.experimental.pallas import tpu as pltpu
from jax.sharding import PartitionSpec as P

MESH = pl.DeviceIdType.MESH
HEAD_DIM = 64
EPSILON = 1e-05
ROOT_HALF = 0.7071067811865476
INVERSE_ROOT_TAU = 0.3989422804014327
MASKED = -1e30
VMEM_BYTES = 62 << 20
POLLS = (1, 1, 0, 1, 1, 1, 1, 1)
TAIL = (
    (1, 1), (0, 3), (2, 1), (1, 2), (3, 1), (2, 2), (1, 3), (3, 2), (2, 3), (3, 3),
)
BF = jnp.bfloat16
F32 = jnp.float32


def up_to(size, unit):
    return (size + unit - 1) // unit * unit


def dot(left, right):
    return jnp.dot(left, right, preferred_element_type=F32)


def dot_nt(left, right):
    return lax.dot_general(left, right, (((1,), (1,)), ((), ())), preferred_element_type=F32)


def dot_tn(left, right):
    return lax.dot_general(left, right, (((0,), (0,)), ((), ())), preferred_element_type=F32)


def pad_rows(rows, size):
    extra = size - rows.shape[0]
    if extra == 0:
        return rows
    return jnp.concatenate([rows, jnp.zeros((extra, rows.shape[1]), rows.dtype)], axis=0)


class Group:
    def __init__(self):
        self.dp = lax.axis_index("dp")
        self.own = lax.axis_index("tensor")
        self.y = self.own // 2
        self.core = self.own % 2
        self.mate = self.y * 2 + (1 - self.core)
        self.far = (1 - self.y) * 2 + self.core

    def greet(self, dp_peers):
        barrier = pltpu.get_barrier_semaphore()
        peers = [(self.dp, self.mate), (self.dp, self.far)] + [(peer, self.own) for peer in dp_peers]
        for peer in peers:
            pl.semaphore_signal(barrier, inc=1, device_id=peer, device_id_type=MESH)
        return lambda: pl.semaphore_wait(barrier, len(peers))

    def share(self, turn):
        late = turn // 2
        other = ((turn + 1) // 2) % 2
        ybit = (1 - self.y) * (1 - late) + self.y * late
        core = self.core * (1 - other) + (1 - self.core) * other
        return ybit * 2 + core

    def copy(self, source, target, send, recv, peer):
        return pltpu.make_async_remote_copy(
            src_ref=source,
            dst_ref=target,
            send_sem=send,
            recv_sem=recv,
            device_id=(self.dp, peer),
            device_id_type=MESH,
        )


class Gather:
    def __init__(self, group, full, send, recv, real):
        self.group, self.full, self.send, self.recv = group, full, send, recv
        self.real = pl.ds(0, real)

    def _copy(self, seq, kind):
        group = self.group
        share = group.far if kind == 2 else group.own
        slot = self.full.at[seq, share, self.real] if kind == 0 else self.full.at[seq, share]
        peer = group.far if kind == 0 else group.mate
        return group.copy(slot, slot, self.send.at[seq, kind], self.recv.at[seq, kind], peer)

    def start(self, seq):
        self._copy(seq, 0).start()
        self._copy(seq, 1).start()

    def wait(self, seq, turn):
        @pl.when(turn == 0)
        def _():
            self._copy(seq, 0).wait_recv()
            self._copy(seq, 2).start()

        @pl.when(turn == 1)
        def _():
            self._copy(seq, 2).wait_recv()

        @pl.when(turn == 2)
        def _():
            self._copy(seq, 1).wait_recv()

    def close(self, seq):
        for kind in range(3):
            self._copy(seq, kind).wait_send()


class Scatter:
    def __init__(self, group, buffers, send, recv, real):
        self.group = group
        self.real = pl.ds(0, real)
        self.outgoing, self.keep, self.near, self.cross, self.landed = buffers
        self.send, self.recv = send, recv

    def _near(self, seq, index):
        return self.group.copy(
            self.outgoing.at[seq, index],
            self.near.at[seq, index],
            self.send.at[seq, index],
            self.recv.at[seq, index],
            self.group.mate,
        )

    def _cross(self, seq):
        return self.group.copy(
            self.cross.at[seq, self.real],
            self.landed.at[seq, self.real],
            self.send.at[seq, 2],
            self.recv.at[seq, 2],
            self.group.far,
        )

    def put(self, seq, turn, terms):
        @pl.when((turn == 0) | (turn == 3))
        def _():
            self.keep[seq, turn // 3] = terms

        @pl.when((turn == 1) | (turn == 2))
        def _():
            self.outgoing[seq, turn - 1] = terms.astype(BF)
            self._near(seq, turn - 1).start()

        @pl.when(turn == 2)
        def _():
            self._near(seq, 0).wait_recv()
            total = self.keep[seq, 0] + self.near[seq, 0].astype(F32)
            self.cross[seq] = total.astype(BF)
            self._cross(seq).start()

    def take(self, seq):
        self._near(seq, 1).wait_recv()
        self._cross(seq).wait_recv()
        for index in range(2):
            self._near(seq, index).wait_send()
        self._cross(seq).wait_send()
        return (
            self.keep[seq, 1]
            + self.near[seq, 1].astype(F32)
            + self.landed[seq].astype(F32)
        )


def norm(rows):
    centred = rows - jnp.mean(rows, axis=-1, keepdims=True)
    inverse = lax.rsqrt(jnp.mean(centred * centred, axis=-1, keepdims=True) + EPSILON)
    return centred * inverse, inverse


def norm_back(grad, normed, inverse, gain):
    scaled = grad * gain
    return inverse * (
        scaled
        - jnp.mean(scaled, axis=-1, keepdims=True)
        - normed * jnp.mean(scaled * normed, axis=-1, keepdims=True)
    )


def sum_rows(rows):
    return jnp.sum(rows, axis=0, keepdims=True)


def lane_index(rows, lanes):
    return lax.broadcasted_iota(jnp.int32, (rows, lanes), 1)


class Ring:
    def __init__(self, group, count, owns, opening, landed, shared, sends, recvs, first):
        self.group, self.count, self.steps = group, count, count - 1
        self.owns, self.opening, self.landed, self.shared = owns, opening, landed, shared
        self.add_send, self.share_send = sends
        self.add_recv, self.share_recv = recvs
        self.half = owns[0].shape[0] // (2 * count)
        self.first, self.rows = first, landed.shape[3]
        self.place, self.right, self.left = ring_peers(group.dp, count)

    def _own(self, which, way, step):
        shift = self.count - 1 - step if way == 0 else 1 + step
        chunk = (self.place + shift) % self.count
        start = pl.multiple_of((2 * chunk + way) * self.half + self.first, 16)
        return self.owns[which][pl.ds(start, self.rows)]

    def _copy(self, source, target, send, recv, way):
        return pltpu.make_async_remote_copy(
            src_ref=source,
            dst_ref=target,
            send_sem=send,
            recv_sem=recv,
            device_id=(self.right if way == 0 else self.left, self.group.own),
            device_id_type=MESH,
        )

    def _add(self, way, step, source=None):
        target = self.landed.at[way, step]
        return self._copy(
            target if source is None else source, target, self.add_send, self.add_recv.at[way, step], way
        )

    def _share(self, way, step):
        shift = self.count - step if way == 0 else step
        slot = self.shared.at[(self.place + shift) % self.count, way]
        return self._copy(slot, slot, self.share_send, self.share_recv.at[way, step], way)

    def open(self):
        for way in range(2):
            for which in range(len(self.owns)):
                self.opening[way, which] = self._own(which, way, 0).astype(BF)
            self._add(way, 0, self.opening.at[way]).start()

    def advance(self, step):
        last = self.steps - 1
        for way in range(2):
            if step < self.steps:
                self._add(way, step).wait_recv()
                target = self.landed.at[way, step] if step < last else self.shared.at[self.place, way]
                for which in range(len(self.owns)):
                    total = self.landed[way, step, which].astype(F32) + self._own(which, way, step + 1)
                    target[which] = total.astype(BF)
                if step < last:
                    self._add(way, step + 1, target).start()
                else:
                    self._share(way, 0).start()
            else:
                turn = step - self.steps
                self._share(way, turn).wait_recv()
                if turn < last:
                    self._share(way, turn + 1).start()

    def wait_sends(self, landed):
        for send in (self.add_send, self.share_send):
            self._copy(landed, landed, send, self.add_recv.at[0, 0], 0).wait_send()


class Pairwise:
    def __init__(self, group, count, terms, outgoing, half, quarter, shared, send, recv):
        self.group, self.spots = group, count // 2
        self.terms, self.outgoing, self.half, self.quarter = terms, outgoing, half, quarter
        self.shared, self.send, self.recv = shared, send, recv
        self.arrays = half.shape[1]
        self.spot, self.side = group.dp // 2, group.dp % 2

    def _copy(self, source, target, index, spot, side):
        return pltpu.make_async_remote_copy(
            src_ref=source,
            dst_ref=target,
            send_sem=self.send.at[index],
            recv_sem=self.recv.at[index],
            device_id=(spot * 2 + side, self.group.own),
            device_id_type=MESH,
        )

    def _out(self):
        return self._copy(self.outgoing, self.half, 0, self.spot, 1 - self.side)

    def _add(self, offset):
        spot = (self.spot + offset) % self.spots
        return self._copy(
            self.half.at[spot], self.quarter.at[offset - 1], offset, spot, self.side
        )

    def _share(self, offset):
        spot = (self.spot + offset) % self.spots
        slot = self.shared.at[self.side, self.spot]
        return self._copy(slot, slot, self.spots - 1 + offset, spot, self.side)

    def _back(self):
        slot = self.shared.at[self.side]
        return self._copy(slot, slot, 2 * self.spots - 1, self.spot, 1 - self.side)

    def act(self, phase):
        others = range(1, self.spots)
        if phase == 0:
            for spot in range(self.spots):
                for which in range(self.arrays):
                    self.outgoing[spot, which] = self.terms(which, 1 - self.side, spot).astype(BF)
            self._out().start()
        elif phase == 1:
            self._out().wait_recv()
            for offset in others:
                spot = (self.spot + offset) % self.spots
                for which in range(self.arrays):
                    total = self.half[spot, which].astype(F32) + self.terms(which, self.side, spot)
                    self.half[spot, which] = total.astype(BF)
                self._add(offset).start()
        elif phase == 2:
            for offset in others:
                self._add(offset).wait_recv()
            for which in range(self.arrays):
                total = self.half[self.spot, which].astype(F32) + self.terms(
                    which, self.side, self.spot
                )
                for offset in others:
                    total = total + self.quarter[offset - 1, which].astype(F32)
                self.shared[self.side, self.spot, which] = total.astype(BF)
            for offset in others:
                self._share(offset).start()
        elif phase == 3:
            for offset in others:
                self._share(offset).wait_recv()
            self._back().start()
        else:
            self._back().wait_recv()
            self._out().wait_send()
            self._back().wait_send()
            for offset in others:
                self._add(offset).wait_send()
                self._share(offset).wait_send()


def ring_peers(index, count):
    odd = index % 2
    place = (1 - odd) * (index // 2) + odd * (count - 1 - index // 2)

    def at(spot):
        late = spot // (count // 2)
        return (1 - late) * 2 * spot + late * (2 * (count - 1 - spot) + 1)

    return place, at((place + 1) % count), at((place + count - 1) % count)


def halving_peers(index, count):
    peers = []
    bit = 1
    while bit < count:
        peers.append(index + bit * (1 - 2 * ((index // bit) % 2)))
        bit *= 2
    return peers


class Totals:
    def __init__(self, group, peers, outgoing, arriving, send, recv, shared):
        self.group, self.shared = group, shared
        self.outgoing, self.arriving, self.send, self.recv = outgoing, arriving, send, recv
        own = group.own
        self.peers = [(group.dp, group.mate), (group.dp, group.far)] + [(peer, own) for peer in peers]

    def _copy(self, level):
        return pltpu.make_async_remote_copy(
            src_ref=self.outgoing.at[level],
            dst_ref=self.arriving.at[level],
            send_sem=self.send.at[level],
            recv_sem=self.recv.at[level],
            device_id=self.peers[level],
            device_id_type=MESH,
        )

    def begin(self, level, rows):
        self.outgoing[level] = rows
        self._copy(level).start()

    def end(self, level):
        self._copy(level).wait()
        other = self.arriving[level]
        if level < 2:
            place = lax.broadcasted_iota(jnp.int32, other.shape, 0)
            other = jnp.where(place < self.shared, other, 0.0)
        return self.outgoing[level] + other


def layer(count, names, *refs):
    r = types.SimpleNamespace(**dict(zip(names, refs)))
    loads = {
        name[:-5]: pltpu.make_async_copy(ref, getattr(r, name[:-5]), r.load_sem.at[index])
        for index, (name, ref) in enumerate(zip(names, refs))
        if name.endswith("_from")
    }

    def loaded(*wanted):
        for name in wanted or list(loads):
            loads.pop(name).wait()

    seqs, share_rows, width = r.frames.shape
    rows = r.full_frames.shape[2]
    length = 4 * rows
    heads_width = r.query_weight.shape[0]
    lanes = r.wide_weight.shape[0] // 3
    heads = heads_width // HEAD_DIM
    group = Group()
    pairs = []
    ring_sides = []
    if count:
        pairs = halving_peers(group.dp, count)
        ring_sides = list(ring_peers(group.dp, count)[1:])
        ring_sides += [
            (group.dp + 2 * offset) % count for offset in range(1, count // 2)
        ]
    tail = pl.ds(share_rows, rows - share_rows)
    if rows > share_rows:
        for full in (r.full_frames, r.first_full, r.grad_mixed, r.grad_full):
            full[:, :, tail] = jnp.zeros_like(full[:, :, tail])
        r.landed[:, tail] = jnp.zeros_like(r.landed[:, tail])
    met = group.greet(ring_sides + pairs)

    for load in loads.values():
        load.start()
    buffers = (r.outgoing, r.keep, r.near, r.cross, r.landed)
    gathers = [
        Gather(group, full, r.gather_send.at[index], r.gather_recv.at[index], share_rows)
        for index, full in enumerate((r.full_frames, r.first_full, r.grad_mixed, r.grad_full))
    ]
    scatters = [
        Scatter(group, buffers, r.scatter_send.at[index], r.scatter_recv.at[index], share_rows)
        for index in range(4)
    ]
    grad_total = r.hidden.at[0]
    heads_grad = r.hidden.at[1, pl.ds(0, 4 * heads_width)]

    def each(stage):
        def body(seq, carry):
            stage(seq)
            return carry

        lax.fori_loop(0, seqs, body, 0)

    def turns(step):
        def body(turn, carry):
            step(turn)
            return carry

        lax.fori_loop(0, 4, body, 0)

    def at_share(share):
        return pl.ds(pl.multiple_of(share * rows, 16), rows)

    def place_frames(seq):
        r.full_frames[seq, group.own] = pad_rows(r.frames[seq].astype(F32), rows).astype(BF)

    loaded("frames")
    each(place_frames)
    met()
    each(gathers[0].start)
    loaded("query_weight", "key_weight", "value_weight", "query_bias", "value_bias", "out_weight")
    r.wide_weight[...] = jnp.zeros_like(r.wide_weight)
    for index, weight in enumerate((r.query_weight, r.key_weight, r.value_weight)):
        r.wide_weight[index * lanes : index * lanes + heads_width] = weight[...]
    r.wide_out[...] = jnp.zeros_like(r.wide_out)
    r.wide_out[:heads_width] = r.out_weight[...]
    r.projection_bias[...] = jnp.where(
        lane_index(1, 3 * lanes) == heads_width, HEAD_DIM**0.5, 0.0
    )
    r.projection_bias[:, :heads_width] = r.query_bias[...].reshape(1, heads_width)
    r.projection_bias[:, 2 * lanes : 2 * lanes + heads_width] = r.value_bias[...].reshape(1, heads_width)
    r.rows_sum[...] = jnp.zeros_like(r.rows_sum)

    def attention(seq):
        def project(step):
            turn = (1 - step // 2) * (3 - step) + (step // 2) * (step - 2)
            gathers[0].wait(seq, turn)
            share = group.share(turn)
            result = dot_nt(r.full_frames[seq, share], r.wide_weight[...]) + r.projection_bias[...]
            place = lax.broadcasted_iota(jnp.int32, (rows, lanes), 0)
            dead = (place >= share_rows) | (place + share * share_rows >= r.lengths[seq])
            flag = jnp.where(dead & (lane_index(rows, lanes) == heads_width), MASKED, 0.0)
            r.projected[seq, at_share(share), 0:lanes] = (
                result[:, :lanes].astype(BF) * HEAD_DIM ** (-0.5)
            ).astype(BF)
            r.projected[seq, at_share(share), lanes : 2 * lanes] = (
                result[:, lanes : 2 * lanes] + flag
            ).astype(BF)
            r.projected[seq, at_share(share), 2 * lanes : 3 * lanes] = result[:, 2 * lanes :].astype(BF)

        turns(project)

        def attend(block, carry):
            chip = (1 - group.y) * (1 - block) + group.y * block
            span = pl.ds(pl.multiple_of(chip * 2 * rows, 16), 2 * rows)
            queries = r.projected[seq, span, 0:lanes]
            lane = lane_index(2 * rows, lanes)
            mixed = jnp.zeros((2 * rows, lanes), F32)
            for head in range(heads):
                inside = lane // HEAD_DIM == head
                picked = jnp.where(inside | (lane == heads_width), queries, jnp.zeros_like(queries))
                scores = dot_nt(picked, r.projected[seq, :, lanes : 2 * lanes])
                top = jnp.max(scores, axis=-1, keepdims=True)
                exponent = jnp.exp(scores - top)
                weight = jnp.sum(exponent, axis=-1, keepdims=True)
                r.log_total[seq, chip, head : head + 1] = jnp.transpose(top + jnp.log(weight))
                part = dot(exponent.astype(BF), r.projected[seq, :, 2 * lanes : 3 * lanes])
                mixed = jnp.where(inside, part * (1.0 / weight), mixed)
            r.context[seq, span] = mixed.astype(BF)
            for half in range(2):
                turn = 2 * block + half
                mixed = r.context[seq, at_share(group.share(turn))]
                scatters[0].put(seq, turn, dot(mixed, r.wide_out[...]))
            return carry

        lax.fori_loop(0, 2, attend, 0)

    each(attention)

    def first_norm(seq):
        attended = scatters[0].take(seq)
        normed, inverse = norm(r.full_frames[seq, group.own].astype(F32) + attended + out_bias)
        r.first_normed[seq] = normed
        r.first_inverse[seq] = inverse
        r.first_full[seq, group.own] = (normed * first_gain + first_shift).astype(BF)
        gathers[1].start(seq)

    loaded()
    out_bias, first_gain, first_shift, down_bias, second_gain, second_shift, up_bias = (
        row[...].reshape(1, row.shape[0])
        for row in (
            r.out_bias, r.first_gain, r.first_shift, r.down_bias, r.second_gain, r.second_shift, r.up_bias,
        )
    )
    each(first_norm)

    def feed(seq):
        def step(turn):
            gathers[1].wait(seq, turn)
            share = group.share(turn)
            inner = dot(r.first_full[seq, share], r.up_weight[...]) + up_bias
            r.hidden[seq, at_share(share)] = inner
            active = (0.5 * inner * (1.0 + lax.erf(inner * ROOT_HALF))).astype(BF)
            r.activated[seq, at_share(share)] = active
            scatters[1].put(seq, turn, dot(active, r.down_weight[...]))

        turns(step)

    each(feed)

    def second_norm(seq):
        mixed = scatters[1].take(seq)
        first = r.first_normed[seq] * first_gain + first_shift
        normed, inverse = norm(first + mixed + down_bias)
        place = lax.broadcasted_iota(jnp.int32, (rows, width), 0)
        live = (place < share_rows) & (place + group.own * share_rows < r.lengths[seq])
        grad = jnp.where(live, pad_rows(r.cotangent[seq], rows), 0.0)
        back = norm_back(grad, normed, inverse, second_gain)
        r.grad_mixed[seq, group.own] = back.astype(BF)
        gathers[2].start(seq)
        r.grad_rows[seq] = back
        r.frames[seq] = (normed * second_gain + second_shift)[:share_rows].astype(BF)
        r.rows_sum[0:1] += sum_rows(grad * normed)
        r.rows_sum[1:2] += sum_rows(grad)
        r.rows_sum[2:3] += sum_rows(back)

    each(second_norm)

    def feed_back(seq, waited):
        def step(turn):
            if not waited:
                gathers[2].wait(seq, turn)
            share = group.share(turn)
            grad_active = dot_nt(r.grad_mixed[seq, share], r.down_weight[...])
            inner = r.hidden[seq, at_share(share)]
            slope = (
                0.5 * (1.0 + lax.erf(inner * ROOT_HALF))
                + inner * jnp.exp(-0.5 * inner * inner) * INVERSE_ROOT_TAU
            )
            grad = (grad_active * slope).astype(BF)
            r.grad_hidden[seq, at_share(share)] = grad
            r.rows_sum[6:7] += sum_rows(grad.astype(F32))
            scatters[2].put(seq, turn, dot_nt(grad, r.up_weight[...]))

        turns(step)


    def down_weights(seq):
        down = dot_tn(r.activated[seq], r.grad_mixed[seq].reshape(length, width))
        r.down_grad[...] = down if seq == 0 else r.down_grad[...] + down

    def up_weights(seq):
        up = dot_tn(r.first_full[seq].reshape(length, width), r.grad_hidden[seq])
        r.up_grad[...] = up if seq == 0 else r.up_grad[...] + up

    def first_back(seq):
        grad = r.grad_rows[seq] + scatters[2].take(seq)
        normed = r.first_normed[seq]
        back = norm_back(grad, normed, r.first_inverse[seq], first_gain)
        r.grad_full[seq, group.own] = back.astype(BF)
        gathers[3].start(seq)
        r.grad_rows[seq] = back
        r.rows_sum[3:4] += sum_rows(grad * normed)
        r.rows_sum[4:5] += sum_rows(grad)
        r.rows_sum[5:6] += sum_rows(back)

    queue = []

    def poll(times=1):
        for _ in range(times):
            if queue:
                queue.pop(0)()

    def act(part, phase):
        if count:
            pieces[part].act(phase)

    if count:
        rings = [
            Ring(
                group,
                count,
                (own,),
                r.feed_opening.at[part],
                r.feed_landed.at[part],
                r.feed_shared.at[part],
                (r.ring_send.at[0], r.ring_send.at[1]),
                (r.ring_recv.at[part, 0], r.ring_recv.at[part, 1]),
                0,
            )
            for part, own in enumerate((r.up_grad, r.down_grad))
        ]

        def heads_terms(first, size, which, side, spot):
            start = first + (side * (count // 2) + spot) * size
            return heads_grad[pl.ds(pl.multiple_of(start, 8), size)]

        pieces = [
            Pairwise(
                group,
                count,
                functools.partial(heads_terms, part * heads_width, r.heads_half.shape[3]),
                r.heads_out.at[part],
                r.heads_half.at[part],
                r.heads_quarter.at[part],
                r.heads_shared.at[part],
                r.pair_send.at[part],
                r.pair_recv.at[part],
            )
            for part in range(1 + heads)
        ]

    def join(part):
        if count:
            rings[part].open()
            waiting = list(queue)
            queue.clear()
            for step in range(2 * (count - 1)):
                queue.extend(waiting[step : step + 1])
                queue.append(functools.partial(rings[part].advance, step))

    for seq in range(seqs):
        if seq == seqs - 1:
            for turn in range(3):
                gathers[2].wait(seq, turn)
            down_weights(seq)
            join(1)
            feed_back(seq, True)
        else:
            feed_back(seq, False)
            down_weights(seq)
    poll(POLLS[7])
    for seq in range(seqs):
        up_weights(seq)
    join(0)
    for seq in range(seqs):
        poll(POLLS[0])
        first_back(seq)
    poll(POLLS[0])
    if count:
        totals = Totals(
            group, pairs, r.small_out, r.small_in, r.small_send, r.small_recv, 6
        )
        totals.begin(0, r.rows_sum[...])
    def output_copy(seq):
        return pltpu.make_async_copy(r.frames.at[seq], r.layer_output.at[seq], r.out_sem.at[3, seq])

    def input_copy(seq):
        return pltpu.make_async_copy(r.cotangent.at[seq], r.input_grad.at[seq], r.out_sem.at[4, seq])

    def store_input(seq):
        r.cotangent[seq] = (scatters[3].take(seq) + r.grad_rows[seq])[:share_rows]
        input_copy(seq).start()

    for seq in range(seqs):
        output_copy(seq).start()

        def step(turn):
            gathers[3].wait(seq, turn)
            share = group.share(turn)
            r.grad_context[at_share(share)] = dot_nt(r.grad_full[seq, share], r.wide_out[...]).astype(BF)

        turns(step)
        part = dot_tn(r.context[seq], r.grad_full[seq].reshape(length, width))[:heads_width]
        if seq == 0:
            heads_grad[:heads_width] = part
        else:
            heads_grad[:heads_width] += part
        if seq == seqs - 1:
            act(0, 0)
        poll(POLLS[1])
        grad_total[...] = jnp.zeros_like(grad_total)
        keys = r.projected[seq, :, lanes : 2 * lanes]
        lane = lane_index(length, lanes)
        key_columns = jnp.transpose(keys.astype(F32) * HEAD_DIM ** (-0.5)).astype(BF)
        for head in range(heads):
            inside = lane // HEAD_DIM == head
            queries = r.projected[seq, :, 0:lanes]
            picked = jnp.where(inside | (lane == heads_width), queries, jnp.zeros_like(queries))
            row = jnp.concatenate(
                [r.log_total[seq, chip, head : head + 1] for chip in range(2)], axis=1
            )
            weights = jnp.exp(dot_nt(keys, picked) - row)
            grads = r.grad_context[...]
            part = dot(weights.astype(BF), grads)
            span = slice(2 * lanes, 3 * lanes)
            grad_total[:, span] = jnp.where(inside, part, grad_total[:, span])
            poll(POLLS[2])
            slopes = weights * dot_nt(
                r.projected[seq, :, 2 * lanes : 3 * lanes],
                jnp.where(inside, grads, jnp.zeros_like(grads)),
            )
            slopes = (slopes - weights * jnp.sum(slopes, axis=0, keepdims=True)).astype(BF)
            part = dot(slopes, queries)
            span = slice(lanes, 2 * lanes)
            grad_total[:, span] = jnp.where(inside, part, grad_total[:, span])
            span = slice(head * HEAD_DIM, (head + 1) * HEAD_DIM)
            grad_total[:, span] = jnp.transpose(dot(key_columns[span], slopes))
            block = slice((1 + head) * heads_width, (2 + head) * heads_width)
            columns = jnp.concatenate(
                [
                    grad_total[:, index * lanes + head * HEAD_DIM : index * lanes + (head + 1) * HEAD_DIM]
                    for index in range(3)
                ],
                axis=1,
            ).astype(BF)
            part = dot_tn(columns, r.full_frames[seq].reshape(length, width))
            if seq == 0:
                heads_grad[block] = part
            else:
                heads_grad[block] += part
            if seq == seqs - 1:
                act(1 + head, 0)
                if head:
                    act(0, head)
            poll(POLLS[3])

        def finish(turn):
            share = group.share(turn)
            grads = grad_total[at_share(share)].astype(BF)
            r.rows_sum[7:8] += sum_rows(grads.astype(F32))
            scatters[3].put(seq, turn, dot(grads, r.wide_weight[...]))

        turns(finish)
        poll(POLLS[4])
        poll(POLLS[5])
        if seq == 0:
            if count:
                totals.begin(1, totals.end(0))
        else:
            store_input(seq - 1)

    if count:
        place = lax.broadcasted_iota(jnp.int32, r.rows_sum.shape, 0)
        totals.begin(2, jnp.where(place == 7, r.rows_sum[...], totals.end(1)))
        copies = [
            pltpu.make_async_copy(shared, out, r.out_sem.at[index, 0])
            for index, (shared, out) in enumerate(
                ((r.feed_shared, r.feed_sum), (r.heads_shared, r.heads_sum))
            )
        ]
        level = 2
        last = len(pairs) + 1
        for at, (part, phase) in enumerate(TAIL):
            pieces[part].act(phase)
            poll(POLLS[6])
            if at == 1:
                store_input(seqs - 1)
            if at % 2 == 1 and level <= last:
                rows_total = totals.end(level)
                level += 1
                if level <= last:
                    totals.begin(level, rows_total)
                else:
                    r.sums[...] = rows_total
        poll(len(queue))
        for piece in pieces:
            piece.act(4)
        for copy in copies:
            copy.start()
        rings[0].wait_sends(r.feed_landed)
    else:
        store_input(seqs - 1)
        r.sums[...] = r.rows_sum[...]
        copies = [
            pltpu.make_async_copy(own, out, r.out_sem.at[index, 0])
            for index, (own, out) in enumerate(
                ((r.up_grad, r.up_sum), (r.down_grad, r.down_sum), (heads_grad, r.heads_sum))
            )
        ]
        for copy in copies:
            copy.start()
    for seq in range(seqs):
        for gather in gathers:
            gather.close(seq)
        output_copy(seq).wait()
        input_copy(seq).wait()
    for copy in copies:
        copy.wait()


VMEM_SPEC = pl.BlockSpec(memory_space=pltpu.VMEM)
ANY_SPEC = pl.BlockSpec(memory_space=pl.ANY)


def widen(columns, refs, *rest):
    r = types.SimpleNamespace(**dict(zip(refs, rest)))
    heads_width = r.query_bias.shape[0]
    width = r.up.shape[1]
    plain = [
        (r.layer_in, r.layer_stage, r.layer_output),
        (r.input_in, r.input_stage, r.input_grad),
    ]
    plain_loads = [
        pltpu.make_async_copy(source, stage, r.plain_sem.at[index])
        for index, (source, stage, _) in enumerate(plain)
    ]
    loads = [
        pltpu.make_async_copy(r.feed_in.at[index, :, :, 0], r.narrow.at[index], r.load_sem.at[index])
        for index in range(2)
    ]
    heads_load = pltpu.make_async_copy(r.heads_in, r.heads, r.plain_sem.at[2])
    for copy in plain_loads + loads + [heads_load]:
        copy.start()
    stores = []
    for load, (_, stage, target) in zip(plain_loads, plain):
        load.wait()
        store = pltpu.make_async_copy(stage, target, r.store_sem.at[len(stores)])
        store.start()
        stores.append(store)
    for index, load in enumerate(loads):
        load.wait()
        r.wide[index] = r.narrow[index].astype(F32).reshape(width, width)
        store = pltpu.make_async_copy(r.wide.at[index], (r.up, r.down)[index], r.store_sem.at[len(stores)])
        store.start()
        stores.append(store)
    heads_load.wait()
    heads = heads_width // HEAD_DIM
    for piece in range(1 + heads):
        rows = r.heads[piece].astype(F32).reshape(heads_width, width)
        for kind in range(3):
            place = 3 * heads + kind if piece == 0 else kind * heads + piece - 1
            r.wide[2, place * HEAD_DIM : (place + 1) * HEAD_DIM] = rows[
                kind * HEAD_DIM : (kind + 1) * HEAD_DIM
            ]
    parts = [
        (r.wide.at[2, pl.ds(part * heads_width, heads_width)], target)
        for part, target in enumerate((r.query, r.key, r.value, r.out))
    ]
    for source, target in parts:
        store = pltpu.make_async_copy(source, target, r.store_sem.at[len(stores)])
        store.start()
        stores.append(store)
    rows = (
        r.second_gain, r.second_shift, r.down_bias, r.first_gain, r.first_shift, r.out_bias, r.up_bias,
    )
    for index, row in enumerate(rows):
        row[...] = r.sums[index]
    r.query_bias[...] = r.sums[7, 0:heads_width]
    r.value_bias[...] = r.sums[7, columns : columns + heads_width]
    for copy in stores:
        copy.wait()


def shards(
    frames,
    cotangent,
    lengths,
    query_weight,
    query_bias,
    key_weight,
    value_weight,
    value_bias,
    out_weight,
    out_bias,
    first_gain,
    first_shift,
    up_weight,
    up_bias,
    down_weight,
    down_bias,
    second_gain,
    second_shift,
):
    seqs, share_rows, width = frames.shape
    rows = up_to(share_rows, 16)
    length = 4 * rows
    heads_width = query_weight.shape[1]
    inner = up_weight.shape[1]
    lanes = up_to(heads_width + 1, 128)
    shape = jax.ShapeDtypeStruct
    count = lax.axis_size("dp")
    ringed = count & (count - 1) == 0 and width % (32 * count) == 0 and count >= 4
    ringed = ringed and heads_width == 3 * HEAD_DIM and heads_width % (8 * count) == 0
    half = width // (2 * count)
    heads_parts = 1 + heads_width // HEAD_DIM
    levels = 2 + count.bit_length() - 1
    full = pltpu.VMEM((seqs, 4, rows, width), BF)
    part = pltpu.VMEM((seqs, rows, width), BF)
    stream = pltpu.VMEM((seqs, rows, width), F32)
    inputs = dict(
        lengths=lengths,
        frames=frames,
        cotangent=cotangent,
        query_weight=query_weight.T,
        query_bias=query_bias,
        key_weight=key_weight.T,
        value_weight=value_weight.T,
        value_bias=value_bias,
        out_weight=out_weight,
        out_bias=out_bias,
        first_gain=first_gain,
        first_shift=first_shift,
        up_weight=up_weight,
        up_bias=up_bias,
        down_weight=down_weight,
        down_bias=down_bias,
        second_gain=second_gain,
        second_shift=second_shift,
    )
    outputs = dict(
        layer_output=shape(frames.shape, BF),
        input_grad=shape(frames.shape, F32),
        sums=shape((8, width), F32),
    )
    if ringed:
        outputs.update(
            feed_sum=shape((2, count, 2, 1, half, width), BF),
            heads_sum=shape((heads_parts, 2, count // 2, 1, heads_width // count, width), BF),
        )
    else:
        outputs.update(
            {name: shape((width, width), F32) for name in ("up_sum", "down_sum", "heads_sum")}
        )
    scratch = dict(
        wide_weight=pltpu.VMEM((3 * lanes, width), BF),
        wide_out=pltpu.VMEM((lanes, width), BF),
        projection_bias=pltpu.VMEM((1, 3 * lanes), F32),
        rows_sum=pltpu.VMEM((8, width), F32),
        full_frames=full,
        first_full=full,
        grad_mixed=full,
        grad_full=full,
        projected=pltpu.VMEM((seqs, length, 3 * lanes), BF),
        context=pltpu.VMEM((seqs, length, lanes), BF),
        log_total=pltpu.VMEM((seqs, 2, 8, 2 * rows), F32),
        first_normed=stream,
        first_inverse=pltpu.VMEM((seqs, rows, 1), F32),
        grad_rows=stream,
        hidden=pltpu.VMEM((seqs, length, inner), F32),
        activated=pltpu.VMEM((seqs, length, inner), BF),
        grad_hidden=pltpu.VMEM((seqs, length, inner), BF),
        grad_context=pltpu.VMEM((length, lanes), BF),
        up_grad=pltpu.VMEM(up_weight.shape, F32),
        down_grad=pltpu.VMEM(down_weight.shape, F32),
        outgoing=pltpu.VMEM((seqs, 2, rows, width), BF),
        keep=pltpu.VMEM((seqs, 2, rows, width), F32),
        near=pltpu.VMEM((seqs, 2, rows, width), BF),
        cross=part,
        landed=part,
        gather_send=pltpu.SemaphoreType.DMA((4, seqs, 3)),
        gather_recv=pltpu.SemaphoreType.DMA((4, seqs, 3)),
        scatter_send=pltpu.SemaphoreType.DMA((4, seqs, 3)),
        scatter_recv=pltpu.SemaphoreType.DMA((4, seqs, 3)),
        out_sem=pltpu.SemaphoreType.DMA((5, seqs)),
        load_sem=pltpu.SemaphoreType.DMA((len(inputs),)),
    )
    scratch.update(
        {name: pltpu.VMEM(item.shape, item.dtype) for name, item in inputs.items() if name != "lengths"}
    )
    given = [name if name == "lengths" else name + "_from" for name in inputs]
    if ringed:
        spots, small = count // 2, heads_width // count
        scratch.update(
            feed_opening=pltpu.VMEM((2, 2, 1, half, width), BF),
            heads_out=pltpu.VMEM((heads_parts, spots, 1, small, width), BF),
            heads_half=pltpu.VMEM((heads_parts, spots, 1, small, width), BF),
            feed_landed=pltpu.VMEM((2, 2, count - 1, 1, half, width), BF),
            heads_quarter=pltpu.VMEM((heads_parts, spots - 1, 1, small, width), BF),
            feed_shared=pltpu.VMEM((2, count, 2, 1, half, width), BF),
            heads_shared=pltpu.VMEM((heads_parts, 2, spots, 1, small, width), BF),
            pair_send=pltpu.SemaphoreType.DMA((heads_parts, 2 * spots)),
            pair_recv=pltpu.SemaphoreType.DMA((heads_parts, 2 * spots)),
            ring_send=pltpu.SemaphoreType.DMA((2,)),
            ring_recv=pltpu.SemaphoreType.DMA((2, 2, 2, count - 1)),
            small_out=pltpu.VMEM((levels, 8, width), F32),
            small_in=pltpu.VMEM((levels, 8, width), F32),
            small_send=pltpu.SemaphoreType.DMA((levels,)),
            small_recv=pltpu.SemaphoreType.DMA((levels,)),
        )
    outs = pl.pallas_call(
        functools.partial(layer, count if ringed else 0, [*given, *outputs, *scratch]),
        out_shape=list(outputs.values()),
        in_specs=[pl.BlockSpec(memory_space=pltpu.SMEM)] + [ANY_SPEC] * (len(inputs) - 1),
        out_specs=[VMEM_SPEC if name == "sums" else ANY_SPEC for name in outputs],
        scratch_shapes=list(scratch.values()),
        compiler_params=pltpu.CompilerParams(
            collective_id=0, has_side_effects=True, vmem_limit_bytes=VMEM_BYTES
        ),
        name="layer",
    )(*inputs.values())
    layer_output, input_grad, sums = outs[:3]
    if not ringed:
        up_grad, down_grad, heads_grad = lax.psum(tuple(outs[3:]), "dp")
        sums = lax.psum(sums, "dp")
        sums = jnp.concatenate([lax.psum(sums[:6], "tensor"), sums[6:]])
        mixed = heads_grad[heads_width:].reshape(-1, 3, HEAD_DIM, width)
        parts = [mixed[:, index].reshape(heads_width, width) for index in range(3)]
        parts.append(heads_grad[:heads_width])
        return (
            layer_output, input_grad, parts[0].T, sums[7, :heads_width], parts[1].T, parts[2].T,
            sums[7, 2 * lanes : 2 * lanes + heads_width], parts[3], sums[5], sums[3], sums[4],
            up_grad, sums[6], down_grad, sums[2], sums[0], sums[1],
        )
    row = shape((width,), F32)
    side_row = shape((heads_width,), F32)
    block = shape((heads_width, width), F32)
    square = shape((width, width), F32)
    results = dict(
        layer_output=shape(frames.shape, BF),
        input_grad=shape(frames.shape, F32),
        query=block,
        query_bias=side_row,
        key=block,
        value=block,
        value_bias=side_row,
        out=block,
        out_bias=row,
        first_gain=row,
        first_shift=row,
        up=square,
        up_bias=row,
        down=square,
        down_bias=row,
        second_gain=row,
        second_shift=row,
    )
    given = ["layer_in", "input_in", "sums", "feed_in", "heads_in"]
    buffers = dict(
        narrow=pltpu.VMEM((2, count, 2, half, width), BF),
        heads=pltpu.VMEM(outs[4].shape, BF),
        wide=pltpu.VMEM((3, width, width), F32),
        plain_sem=pltpu.SemaphoreType.DMA((3,)),
        load_sem=pltpu.SemaphoreType.DMA((2,)),
        store_sem=pltpu.SemaphoreType.DMA((8,)),
        layer_stage=pltpu.VMEM(frames.shape, BF),
        input_stage=pltpu.VMEM(frames.shape, F32),
    )
    final = pl.pallas_call(
        functools.partial(widen, 2 * lanes, [*given, *results, *buffers]),
        out_shape=list(results.values()),
        in_specs=[ANY_SPEC] * 2 + [VMEM_SPEC] + [ANY_SPEC] * 2,
        out_specs=[VMEM_SPEC if len(item.shape) == 1 else ANY_SPEC for item in results.values()],
        scratch_shapes=list(buffers.values()),
        compiler_params=pltpu.CompilerParams(vmem_limit_bytes=VMEM_BYTES),
        name="widen",
    )(layer_output, input_grad, sums, *outs[3:])
    final = dict(zip(results, final))
    for name in ("query", "key", "value"):
        final[name] = final[name].T
    return tuple(final.values())


def solution(mesh):
    return jax.shard_map(
        shards,
        mesh=mesh,
        in_specs=(
            P("dp", "tensor", None),
            P("dp", "tensor", None),
            P("dp"),
            P(None, "tensor"),
            P("tensor"),
            P(None, "tensor"),
            P(None, "tensor"),
            P("tensor"),
            P("tensor", None),
            P(),
            P(),
            P(),
            P(None, "tensor"),
            P("tensor"),
            P("tensor", None),
            P(),
            P(),
            P(),
        ),
        out_specs=(
            P("dp", "tensor", None),
            P("dp", "tensor", None),
            P(None, "tensor"),
            P("tensor"),
            P(None, "tensor"),
            P(None, "tensor"),
            P("tensor"),
            P("tensor", None),
            P(),
            P(),
            P(),
            P(None, "tensor"),
            P("tensor"),
            P("tensor", None),
            P(),
            P(),
            P(),
        ),
        check_vma=False,
    )
```

```python
import functools
import types

import jax
import jax.numpy as jnp
from jax import lax
from jax.experimental import pallas as pl
from jax.experimental.pallas import tpu as pltpu
from jax.sharding import PartitionSpec as P

MESH = pl.DeviceIdType.MESH
HEAD_DIM = 64
EPSILON = 1e-05
ROOT_HALF = 0.7071067811865476
INVERSE_ROOT_TAU = 0.3989422804014327
MASKED = -1e30
VMEM_BYTES = 62 << 20
POLLS = (1, 2, 0, 1, 1, 1, 1, 1)
TAIL = (
    (1, 1), (2, 1), (0, 3), (1, 2), (3, 1), (2, 2), (3, 2), (1, 3), (2, 3), (3, 3),
)
BF = jnp.bfloat16
F32 = jnp.float32


def up_to(size, unit):
    return (size + unit - 1) // unit * unit


def dot(left, right):
    return jnp.dot(left, right, preferred_element_type=F32)


def dot_nt(left, right):
    return lax.dot_general(left, right, (((1,), (1,)), ((), ())), preferred_element_type=F32)


def dot_tn(left, right):
    return lax.dot_general(left, right, (((0,), (0,)), ((), ())), preferred_element_type=F32)


def pad_rows(rows, size):
    extra = size - rows.shape[0]
    if extra == 0:
        return rows
    return jnp.concatenate([rows, jnp.zeros((extra, rows.shape[1]), rows.dtype)], axis=0)


class Group:
    def __init__(self):
        self.dp = lax.axis_index("dp")
        self.own = lax.axis_index("tensor")
        self.y = self.own // 2
        self.core = self.own % 2
        self.mate = self.y * 2 + (1 - self.core)
        self.far = (1 - self.y) * 2 + self.core

    def greet(self, dp_peers):
        barrier = pltpu.get_barrier_semaphore()
        peers = [(self.dp, self.mate), (self.dp, self.far)] + [(peer, self.own) for peer in dp_peers]
        for peer in peers:
            pl.semaphore_signal(barrier, inc=1, device_id=peer, device_id_type=MESH)
        return lambda: pl.semaphore_wait(barrier, len(peers))

    def share(self, turn):
        late = turn // 2
        other = ((turn + 1) // 2) % 2
        ybit = (1 - self.y) * (1 - late) + self.y * late
        core = self.core * (1 - other) + (1 - self.core) * other
        return ybit * 2 + core

    def copy(self, source, target, send, recv, peer):
        return pltpu.make_async_remote_copy(
            src_ref=source,
            dst_ref=target,
            send_sem=send,
            recv_sem=recv,
            device_id=(self.dp, peer),
            device_id_type=MESH,
        )


class Gather:
    def __init__(self, group, full, send, recv, real):
        self.group, self.full, self.send, self.recv = group, full, send, recv
        self.real = pl.ds(0, real)

    def _copy(self, seq, kind):
        group = self.group
        share = group.far if kind == 2 else group.own
        slot = self.full.at[seq, share, self.real] if kind == 0 else self.full.at[seq, share]
        peer = group.far if kind == 0 else group.mate
        return group.copy(slot, slot, self.send.at[seq, kind], self.recv.at[seq, kind], peer)

    def start(self, seq):
        self._copy(seq, 0).start()
        self._copy(seq, 1).start()

    def wait(self, seq, turn):
        @pl.when(turn == 0)
        def _():
            self._copy(seq, 0).wait_recv()
            self._copy(seq, 2).start()

        @pl.when(turn == 1)
        def _():
            self._copy(seq, 2).wait_recv()

        @pl.when(turn == 2)
        def _():
            self._copy(seq, 1).wait_recv()

    def close(self, seq):
        for kind in range(3):
            self._copy(seq, kind).wait_send()


class Scatter:
    def __init__(self, group, buffers, send, recv, real):
        self.group = group
        self.real = pl.ds(0, real)
        self.outgoing, self.keep, self.near, self.cross, self.landed = buffers
        self.send, self.recv = send, recv

    def _near(self, seq, index):
        return self.group.copy(
            self.outgoing.at[seq, index],
            self.near.at[seq, index],
            self.send.at[seq, index],
            self.recv.at[seq, index],
            self.group.mate,
        )

    def _cross(self, seq):
        return self.group.copy(
            self.cross.at[seq, self.real],
            self.landed.at[seq, self.real],
            self.send.at[seq, 2],
            self.recv.at[seq, 2],
            self.group.far,
        )

    def put(self, seq, turn, terms):
        @pl.when((turn == 0) | (turn == 3))
        def _():
            self.keep[seq, turn // 3] = terms

        @pl.when((turn == 1) | (turn == 2))
        def _():
            self.outgoing[seq, turn - 1] = terms.astype(BF)
            self._near(seq, turn - 1).start()

        @pl.when(turn == 2)
        def _():
            self._near(seq, 0).wait_recv()
            total = self.keep[seq, 0] + self.near[seq, 0].astype(F32)
            self.cross[seq] = total.astype(BF)
            self._cross(seq).start()

    def take(self, seq):
        self._near(seq, 1).wait_recv()
        self._cross(seq).wait_recv()
        for index in range(2):
            self._near(seq, index).wait_send()
        self._cross(seq).wait_send()
        return (
            self.keep[seq, 1]
            + self.near[seq, 1].astype(F32)
            + self.landed[seq].astype(F32)
        )


def norm(rows):
    centred = rows - jnp.mean(rows, axis=-1, keepdims=True)
    inverse = lax.rsqrt(jnp.mean(centred * centred, axis=-1, keepdims=True) + EPSILON)
    return centred * inverse, inverse


def norm_back(grad, normed, inverse, gain):
    scaled = grad * gain
    return inverse * (
        scaled
        - jnp.mean(scaled, axis=-1, keepdims=True)
        - normed * jnp.mean(scaled * normed, axis=-1, keepdims=True)
    )


def sum_rows(rows):
    return jnp.sum(rows, axis=0, keepdims=True)


def lane_index(rows, lanes):
    return lax.broadcasted_iota(jnp.int32, (rows, lanes), 1)


class Ring:
    def __init__(self, group, count, owns, opening, landed, shared, sends, recvs, first):
        self.group, self.count, self.steps = group, count, count - 1
        self.owns, self.opening, self.landed, self.shared = owns, opening, landed, shared
        self.add_send, self.share_send = sends
        self.add_recv, self.share_recv = recvs
        self.half = owns[0].shape[0] // (2 * count)
        self.first, self.rows = first, landed.shape[3]
        self.place, self.right, self.left = ring_peers(group.dp, count)

    def _own(self, which, way, step):
        shift = self.count - 1 - step if way == 0 else 1 + step
        chunk = (self.place + shift) % self.count
        start = pl.multiple_of((2 * chunk + way) * self.half + self.first, 16)
        return self.owns[which][pl.ds(start, self.rows)]

    def _copy(self, source, target, send, recv, way):
        return pltpu.make_async_remote_copy(
            src_ref=source,
            dst_ref=target,
            send_sem=send,
            recv_sem=recv,
            device_id=(self.right if way == 0 else self.left, self.group.own),
            device_id_type=MESH,
        )

    def _add(self, way, step, source=None):
        target = self.landed.at[way, step]
        return self._copy(
            target if source is None else source, target, self.add_send, self.add_recv.at[way, step], way
        )

    def _share(self, way, step):
        shift = self.count - step if way == 0 else step
        slot = self.shared.at[(self.place + shift) % self.count, way]
        return self._copy(slot, slot, self.share_send, self.share_recv.at[way, step], way)

    def open(self):
        for way in range(2):
            for which in range(len(self.owns)):
                self.opening[way, which] = self._own(which, way, 0).astype(BF)
            self._add(way, 0, self.opening.at[way]).start()

    def advance(self, step):
        last = self.steps - 1
        for way in range(2):
            if step < self.steps:
                self._add(way, step).wait_recv()
                target = self.landed.at[way, step] if step < last else self.shared.at[self.place, way]
                for which in range(len(self.owns)):
                    total = self.landed[way, step, which].astype(F32) + self._own(which, way, step + 1)
                    target[which] = total.astype(BF)
                if step < last:
                    self._add(way, step + 1, target).start()
                else:
                    self._share(way, 0).start()
            else:
                turn = step - self.steps
                self._share(way, turn).wait_recv()
                if turn < last:
                    self._share(way, turn + 1).start()

    def wait_sends(self, landed):
        for send in (self.add_send, self.share_send):
            self._copy(landed, landed, send, self.add_recv.at[0, 0], 0).wait_send()


class Pairwise:
    def __init__(self, group, count, terms, outgoing, half, quarter, shared, send, recv):
        self.group, self.spots = group, count // 2
        self.terms, self.outgoing, self.half, self.quarter = terms, outgoing, half, quarter
        self.shared, self.send, self.recv = shared, send, recv
        self.arrays = half.shape[1]
        self.spot, self.side = group.dp // 2, group.dp % 2

    def _copy(self, source, target, index, spot, side):
        return pltpu.make_async_remote_copy(
            src_ref=source,
            dst_ref=target,
            send_sem=self.send.at[index],
            recv_sem=self.recv.at[index],
            device_id=(spot * 2 + side, self.group.own),
            device_id_type=MESH,
        )

    def _out(self):
        return self._copy(self.outgoing, self.half, 0, self.spot, 1 - self.side)

    def _add(self, offset):
        spot = (self.spot + offset) % self.spots
        return self._copy(
            self.half.at[spot], self.quarter.at[offset - 1], offset, spot, self.side
        )

    def _share(self, offset):
        spot = (self.spot + offset) % self.spots
        slot = self.shared.at[self.side, self.spot]
        return self._copy(slot, slot, self.spots - 1 + offset, spot, self.side)

    def _back(self):
        slot = self.shared.at[self.side]
        return self._copy(slot, slot, 2 * self.spots - 1, self.spot, 1 - self.side)

    def act(self, phase):
        others = range(1, self.spots)
        if phase == 0:
            for spot in range(self.spots):
                for which in range(self.arrays):
                    self.outgoing[spot, which] = self.terms(which, 1 - self.side, spot).astype(BF)
            self._out().start()
        elif phase == 1:
            self._out().wait_recv()
            for offset in others:
                spot = (self.spot + offset) % self.spots
                for which in range(self.arrays):
                    total = self.half[spot, which].astype(F32) + self.terms(which, self.side, spot)
                    self.half[spot, which] = total.astype(BF)
                self._add(offset).start()
        elif phase == 2:
            for offset in others:
                self._add(offset).wait_recv()
            for which in range(self.arrays):
                total = self.half[self.spot, which].astype(F32) + self.terms(
                    which, self.side, self.spot
                )
                for offset in others:
                    total = total + self.quarter[offset - 1, which].astype(F32)
                self.shared[self.side, self.spot, which] = total.astype(BF)
            for offset in others:
                self._share(offset).start()
        elif phase == 3:
            for offset in others:
                self._share(offset).wait_recv()
            self._back().start()
        else:
            self._back().wait_recv()
            self._out().wait_send()
            self._back().wait_send()
            for offset in others:
                self._add(offset).wait_send()
                self._share(offset).wait_send()


def ring_peers(index, count):
    odd = index % 2
    place = (1 - odd) * (index // 2) + odd * (count - 1 - index // 2)

    def at(spot):
        late = spot // (count // 2)
        return (1 - late) * 2 * spot + late * (2 * (count - 1 - spot) + 1)

    return place, at((place + 1) % count), at((place + count - 1) % count)


def halving_peers(index, count):
    peers = []
    bit = 1
    while bit < count:
        peers.append(index + bit * (1 - 2 * ((index // bit) % 2)))
        bit *= 2
    return peers


class Totals:
    def __init__(self, group, peers, outgoing, arriving, send, recv, shared):
        self.group, self.shared = group, shared
        self.outgoing, self.arriving, self.send, self.recv = outgoing, arriving, send, recv
        own = group.own
        self.peers = [(group.dp, group.mate), (group.dp, group.far)] + [(peer, own) for peer in peers]

    def _copy(self, level):
        return pltpu.make_async_remote_copy(
            src_ref=self.outgoing.at[level],
            dst_ref=self.arriving.at[level],
            send_sem=self.send.at[level],
            recv_sem=self.recv.at[level],
            device_id=self.peers[level],
            device_id_type=MESH,
        )

    def begin(self, level, rows):
        self.outgoing[level] = rows
        self._copy(level).start()

    def end(self, level):
        self._copy(level).wait()
        other = self.arriving[level]
        if level < 2:
            place = lax.broadcasted_iota(jnp.int32, other.shape, 0)
            other = jnp.where(place < self.shared, other, 0.0)
        return self.outgoing[level] + other


def layer(count, names, *refs):
    r = types.SimpleNamespace(**dict(zip(names, refs)))
    loads = {
        name[:-5]: pltpu.make_async_copy(ref, getattr(r, name[:-5]), r.load_sem.at[index])
        for index, (name, ref) in enumerate(zip(names, refs))
        if name.endswith("_from")
    }

    def loaded(*wanted):
        for name in wanted or list(loads):
            loads.pop(name).wait()

    seqs, share_rows, width = r.frames.shape
    rows = r.full_frames.shape[2]
    length = 4 * rows
    heads_width = r.query_weight.shape[0]
    lanes = r.wide_weight.shape[0] // 3
    heads = heads_width // HEAD_DIM
    group = Group()
    pairs = []
    ring_sides = []
    if count:
        pairs = halving_peers(group.dp, count)
        ring_sides = list(ring_peers(group.dp, count)[1:])
        ring_sides += [
            (group.dp + 2 * offset) % count for offset in range(1, count // 2)
        ]
    tail = pl.ds(share_rows, rows - share_rows)
    if rows > share_rows:
        for full in (r.full_frames, r.first_full, r.grad_mixed, r.grad_full):
            full[:, :, tail] = jnp.zeros_like(full[:, :, tail])
        r.landed[:, tail] = jnp.zeros_like(r.landed[:, tail])
    met = group.greet(ring_sides + pairs)

    for load in loads.values():
        load.start()
    buffers = (r.outgoing, r.keep, r.near, r.cross, r.landed)
    gathers = [
        Gather(group, full, r.gather_send.at[index], r.gather_recv.at[index], share_rows)
        for index, full in enumerate((r.full_frames, r.first_full, r.grad_mixed, r.grad_full))
    ]
    scatters = [
        Scatter(group, buffers, r.scatter_send.at[index], r.scatter_recv.at[index], share_rows)
        for index in range(4)
    ]
    grad_total = r.hidden.at[0]
    heads_grad = r.hidden.at[1, pl.ds(0, 4 * heads_width)]

    def each(stage):
        def body(seq, carry):
            stage(seq)
            return carry

        lax.fori_loop(0, seqs, body, 0)

    def turns(step):
        def body(turn, carry):
            step(turn)
            return carry

        lax.fori_loop(0, 4, body, 0)

    def at_share(share):
        return pl.ds(pl.multiple_of(share * rows, 16), rows)

    def place_frames(seq):
        r.full_frames[seq, group.own] = pad_rows(r.frames[seq].astype(F32), rows).astype(BF)

    loaded("frames")
    each(place_frames)
    met()
    each(gathers[0].start)
    loaded("query_weight", "key_weight", "value_weight", "query_bias", "value_bias", "out_weight")
    r.wide_weight[...] = jnp.zeros_like(r.wide_weight)
    for index, weight in enumerate((r.query_weight, r.key_weight, r.value_weight)):
        r.wide_weight[index * lanes : index * lanes + heads_width] = weight[...]
    r.wide_out[...] = jnp.zeros_like(r.wide_out)
    r.wide_out[:heads_width] = r.out_weight[...]
    r.projection_bias[...] = jnp.where(
        lane_index(1, 3 * lanes) == heads_width, HEAD_DIM**0.5, 0.0
    )
    r.projection_bias[:, :heads_width] = r.query_bias[...].reshape(1, heads_width)
    r.projection_bias[:, 2 * lanes : 2 * lanes + heads_width] = r.value_bias[...].reshape(1, heads_width)
    r.rows_sum[...] = jnp.zeros_like(r.rows_sum)

    def attention(seq):
        def project(step):
            turn = (1 - step // 2) * (3 - step) + (step // 2) * (step - 2)
            gathers[0].wait(seq, turn)
            share = group.share(turn)
            result = dot_nt(r.full_frames[seq, share], r.wide_weight[...]) + r.projection_bias[...]
            place = lax.broadcasted_iota(jnp.int32, (rows, lanes), 0)
            dead = (place >= share_rows) | (place + share * share_rows >= r.lengths[seq])
            flag = jnp.where(dead & (lane_index(rows, lanes) == heads_width), MASKED, 0.0)
            r.projected[seq, at_share(share), 0:lanes] = (
                result[:, :lanes].astype(BF) * HEAD_DIM ** (-0.5)
            ).astype(BF)
            r.projected[seq, at_share(share), lanes : 2 * lanes] = (
                result[:, lanes : 2 * lanes] + flag
            ).astype(BF)
            r.projected[seq, at_share(share), 2 * lanes : 3 * lanes] = result[:, 2 * lanes :].astype(BF)

        turns(project)

        def attend(block, carry):
            chip = (1 - group.y) * (1 - block) + group.y * block
            span = pl.ds(pl.multiple_of(chip * 2 * rows, 16), 2 * rows)
            queries = r.projected[seq, span, 0:lanes]
            lane = lane_index(2 * rows, lanes)
            mixed = jnp.zeros((2 * rows, lanes), F32)
            for head in range(heads):
                inside = lane // HEAD_DIM == head
                picked = jnp.where(inside | (lane == heads_width), queries, jnp.zeros_like(queries))
                scores = dot_nt(picked, r.projected[seq, :, lanes : 2 * lanes])
                top = jnp.max(scores, axis=-1, keepdims=True)
                exponent = jnp.exp(scores - top)
                weight = jnp.sum(exponent, axis=-1, keepdims=True)
                r.log_total[seq, chip, head : head + 1] = jnp.transpose(top + jnp.log(weight))
                part = dot(exponent.astype(BF), r.projected[seq, :, 2 * lanes : 3 * lanes])
                mixed = jnp.where(inside, part * (1.0 / weight), mixed)
            r.context[seq, span] = mixed.astype(BF)
            for half in range(2):
                turn = 2 * block + half
                mixed = r.context[seq, at_share(group.share(turn))]
                scatters[0].put(seq, turn, dot(mixed, r.wide_out[...]))
            return carry

        lax.fori_loop(0, 2, attend, 0)

    each(attention)

    def first_norm(seq):
        attended = scatters[0].take(seq)
        normed, inverse = norm(r.full_frames[seq, group.own].astype(F32) + attended + out_bias)
        r.first_normed[seq] = normed
        r.first_inverse[seq] = inverse
        r.first_full[seq, group.own] = (normed * first_gain + first_shift).astype(BF)
        gathers[1].start(seq)

    loaded()
    out_bias, first_gain, first_shift, down_bias, second_gain, second_shift, up_bias = (
        row[...].reshape(1, row.shape[0])
        for row in (
            r.out_bias, r.first_gain, r.first_shift, r.down_bias, r.second_gain, r.second_shift, r.up_bias,
        )
    )
    each(first_norm)

    def feed(seq):
        def step(turn):
            gathers[1].wait(seq, turn)
            share = group.share(turn)
            inner = dot(r.first_full[seq, share], r.up_weight[...]) + up_bias
            r.hidden[seq, at_share(share)] = inner
            active = (0.5 * inner * (1.0 + lax.erf(inner * ROOT_HALF))).astype(BF)
            r.activated[seq, at_share(share)] = active
            scatters[1].put(seq, turn, dot(active, r.down_weight[...]))

        turns(step)

    each(feed)

    def second_norm(seq):
        mixed = scatters[1].take(seq)
        first = r.first_normed[seq] * first_gain + first_shift
        normed, inverse = norm(first + mixed + down_bias)
        place = lax.broadcasted_iota(jnp.int32, (rows, width), 0)
        live = (place < share_rows) & (place + group.own * share_rows < r.lengths[seq])
        grad = jnp.where(live, pad_rows(r.cotangent[seq], rows), 0.0)
        back = norm_back(grad, normed, inverse, second_gain)
        r.grad_mixed[seq, group.own] = back.astype(BF)
        gathers[2].start(seq)
        r.grad_rows[seq] = back
        r.frames[seq] = (normed * second_gain + second_shift)[:share_rows].astype(BF)
        r.rows_sum[0:1] += sum_rows(grad * normed)
        r.rows_sum[1:2] += sum_rows(grad)
        r.rows_sum[2:3] += sum_rows(back)

    each(second_norm)

    def feed_back(seq, waited):
        def step(turn):
            if not waited:
                gathers[2].wait(seq, turn)
            share = group.share(turn)
            grad_active = dot_nt(r.grad_mixed[seq, share], r.down_weight[...])
            inner = r.hidden[seq, at_share(share)]
            slope = (
                0.5 * (1.0 + lax.erf(inner * ROOT_HALF))
                + inner * jnp.exp(-0.5 * inner * inner) * INVERSE_ROOT_TAU
            )
            grad = (grad_active * slope).astype(BF)
            r.grad_hidden[seq, at_share(share)] = grad
            r.rows_sum[6:7] += sum_rows(grad.astype(F32))
            scatters[2].put(seq, turn, dot_nt(grad, r.up_weight[...]))

        turns(step)


    def down_weights(seq):
        down = dot_tn(r.activated[seq], r.grad_mixed[seq].reshape(length, width))
        r.down_grad[...] = down if seq == 0 else r.down_grad[...] + down

    def up_weights(seq):
        up = dot_tn(r.first_full[seq].reshape(length, width), r.grad_hidden[seq])
        r.up_grad[...] = up if seq == 0 else r.up_grad[...] + up

    def first_back(seq):
        grad = r.grad_rows[seq] + scatters[2].take(seq)
        normed = r.first_normed[seq]
        back = norm_back(grad, normed, r.first_inverse[seq], first_gain)
        r.grad_full[seq, group.own] = back.astype(BF)
        gathers[3].start(seq)
        r.grad_rows[seq] = back
        r.rows_sum[3:4] += sum_rows(grad * normed)
        r.rows_sum[4:5] += sum_rows(grad)
        r.rows_sum[5:6] += sum_rows(back)

    queue = []

    def poll(times=1):
        for _ in range(times):
            if queue:
                queue.pop(0)()

    def act(part, phase):
        if count:
            pieces[part].act(phase)

    if count:
        rings = [
            Ring(
                group,
                count,
                (own,),
                r.feed_opening.at[part],
                r.feed_landed.at[part],
                r.feed_shared.at[part],
                (r.ring_send.at[0], r.ring_send.at[1]),
                (r.ring_recv.at[part, 0], r.ring_recv.at[part, 1]),
                0,
            )
            for part, own in enumerate((r.up_grad, r.down_grad))
        ]

        def heads_terms(first, size, which, side, spot):
            start = first + (side * (count // 2) + spot) * size
            return heads_grad[pl.ds(pl.multiple_of(start, 8), size)]

        pieces = [
            Pairwise(
                group,
                count,
                functools.partial(heads_terms, part * heads_width, r.heads_half.shape[3]),
                r.heads_out.at[part],
                r.heads_half.at[part],
                r.heads_quarter.at[part],
                r.heads_shared.at[part],
                r.pair_send.at[part],
                r.pair_recv.at[part],
            )
            for part in range(1 + heads)
        ]

    def join(part):
        if count:
            rings[part].open()
            waiting = list(queue)
            queue.clear()
            for step in range(2 * (count - 1)):
                queue.extend(waiting[step : step + 1])
                queue.append(functools.partial(rings[part].advance, step))

    for seq in range(seqs):
        if seq == seqs - 1:
            for turn in range(3):
                gathers[2].wait(seq, turn)
            down_weights(seq)
            join(1)
            feed_back(seq, True)
        else:
            feed_back(seq, False)
            down_weights(seq)
    poll(POLLS[7])
    for seq in range(seqs):
        up_weights(seq)
    join(0)
    for seq in range(seqs):
        poll(POLLS[0])
        first_back(seq)
    poll(POLLS[0])
    if count:
        totals = Totals(
            group, pairs, r.small_out, r.small_in, r.small_send, r.small_recv, 6
        )
        totals.begin(0, r.rows_sum[...])
    def output_copy(seq):
        return pltpu.make_async_copy(r.frames.at[seq], r.layer_output.at[seq], r.out_sem.at[3, seq])

    def input_copy(seq):
        return pltpu.make_async_copy(r.cotangent.at[seq], r.input_grad.at[seq], r.out_sem.at[4, seq])

    def store_input(seq):
        r.cotangent[seq] = (scatters[3].take(seq) + r.grad_rows[seq])[:share_rows]
        input_copy(seq).start()

    for seq in range(seqs):
        output_copy(seq).start()

        def step(turn):
            gathers[3].wait(seq, turn)
            share = group.share(turn)
            r.grad_context[at_share(share)] = dot_nt(r.grad_full[seq, share], r.wide_out[...]).astype(BF)

        turns(step)
        part = dot_tn(r.context[seq], r.grad_full[seq].reshape(length, width))[:heads_width]
        if seq == 0:
            heads_grad[:heads_width] = part
        else:
            heads_grad[:heads_width] += part
        if seq == seqs - 1:
            act(0, 0)
        poll(POLLS[1])
        grad_total[...] = jnp.zeros_like(grad_total)
        keys = r.projected[seq, :, lanes : 2 * lanes]
        lane = lane_index(length, lanes)
        key_columns = jnp.transpose(keys.astype(F32) * HEAD_DIM ** (-0.5)).astype(BF)
        for head in range(heads):
            inside = lane // HEAD_DIM == head
            queries = r.projected[seq, :, 0:lanes]
            picked = jnp.where(inside | (lane == heads_width), queries, jnp.zeros_like(queries))
            row = jnp.concatenate(
                [r.log_total[seq, chip, head : head + 1] for chip in range(2)], axis=1
            )
            weights = jnp.exp(dot_nt(keys, picked) - row)
            grads = r.grad_context[...]
            part = dot(weights.astype(BF), grads)
            span = slice(2 * lanes, 3 * lanes)
            grad_total[:, span] = jnp.where(inside, part, grad_total[:, span])
            poll(POLLS[2])
            slopes = weights * dot_nt(
                r.projected[seq, :, 2 * lanes : 3 * lanes],
                jnp.where(inside, grads, jnp.zeros_like(grads)),
            )
            slopes = (slopes - weights * jnp.sum(slopes, axis=0, keepdims=True)).astype(BF)
            part = dot(slopes, queries)
            span = slice(lanes, 2 * lanes)
            grad_total[:, span] = jnp.where(inside, part, grad_total[:, span])
            span = slice(head * HEAD_DIM, (head + 1) * HEAD_DIM)
            grad_total[:, span] = jnp.transpose(dot(key_columns[span], slopes))
            block = slice((1 + head) * heads_width, (2 + head) * heads_width)
            columns = jnp.concatenate(
                [
                    grad_total[:, index * lanes + head * HEAD_DIM : index * lanes + (head + 1) * HEAD_DIM]
                    for index in range(3)
                ],
                axis=1,
            ).astype(BF)
            part = dot_tn(columns, r.full_frames[seq].reshape(length, width))
            if seq == 0:
                heads_grad[block] = part
            else:
                heads_grad[block] += part
            if seq == seqs - 1:
                act(1 + head, 0)
                if head:
                    act(0, head)
            poll(POLLS[3])

        def finish(turn):
            share = group.share(turn)
            grads = grad_total[at_share(share)].astype(BF)
            r.rows_sum[7:8] += sum_rows(grads.astype(F32))
            scatters[3].put(seq, turn, dot(grads, r.wide_weight[...]))

        turns(finish)
        poll(POLLS[4])
        poll(POLLS[5])
        if seq == 0:
            if count:
                totals.begin(1, totals.end(0))
        else:
            store_input(seq - 1)

    if count:
        place = lax.broadcasted_iota(jnp.int32, r.rows_sum.shape, 0)
        totals.begin(2, jnp.where(place == 7, r.rows_sum[...], totals.end(1)))
        copies = [
            pltpu.make_async_copy(shared, out, r.out_sem.at[index, 0])
            for index, (shared, out) in enumerate(
                ((r.feed_shared, r.feed_sum), (r.heads_shared, r.heads_sum))
            )
        ]
        level = 2
        last = len(pairs) + 1
        sent = []
        for at, (part, phase) in enumerate(TAIL):
            pieces[part].act(phase)
            poll(POLLS[6])
            if not queue and not sent:
                copies[0].start()
                sent.append(1)
            if at == 1:
                store_input(seqs - 1)
            if at % 2 == 1 and level <= last:
                rows_total = totals.end(level)
                level += 1
                if level <= last:
                    totals.begin(level, rows_total)
                else:
                    r.sums[...] = rows_total
        poll(len(queue))
        if not sent:
            copies[0].start()
        for piece in pieces:
            piece.act(4)
        copies[1].start()
        rings[0].wait_sends(r.feed_landed)
    else:
        store_input(seqs - 1)
        r.sums[...] = r.rows_sum[...]
        copies = [
            pltpu.make_async_copy(own, out, r.out_sem.at[index, 0])
            for index, (own, out) in enumerate(
                ((r.up_grad, r.up_sum), (r.down_grad, r.down_sum), (heads_grad, r.heads_sum))
            )
        ]
        for copy in copies:
            copy.start()
    for seq in range(seqs):
        for gather in gathers:
            gather.close(seq)
        output_copy(seq).wait()
        input_copy(seq).wait()
    for copy in copies:
        copy.wait()


VMEM_SPEC = pl.BlockSpec(memory_space=pltpu.VMEM)
ANY_SPEC = pl.BlockSpec(memory_space=pl.ANY)


def widen(columns, refs, *rest):
    r = types.SimpleNamespace(**dict(zip(refs, rest)))
    heads_width = r.query_bias.shape[0]
    width = r.up.shape[1]
    plain = [
        (r.layer_in, r.layer_stage, r.layer_output),
        (r.input_in, r.input_stage, r.input_grad),
    ]
    plain_loads = [
        pltpu.make_async_copy(source, stage, r.plain_sem.at[index])
        for index, (source, stage, _) in enumerate(plain)
    ]
    loads = [
        pltpu.make_async_copy(r.feed_in.at[index, :, :, 0], r.narrow.at[index], r.load_sem.at[index])
        for index in range(2)
    ]
    heads_load = pltpu.make_async_copy(r.heads_in, r.heads, r.plain_sem.at[2])
    for copy in plain_loads + loads + [heads_load]:
        copy.start()
    stores = []
    for load, (_, stage, target) in zip(plain_loads, plain):
        load.wait()
        store = pltpu.make_async_copy(stage, target, r.store_sem.at[len(stores)])
        store.start()
        stores.append(store)
    for index, load in enumerate(loads):
        load.wait()
        r.wide[index] = r.narrow[index].astype(F32).reshape(width, width)
        store = pltpu.make_async_copy(r.wide.at[index], (r.up, r.down)[index], r.store_sem.at[len(stores)])
        store.start()
        stores.append(store)
    heads_load.wait()
    heads = heads_width // HEAD_DIM
    for piece in range(1 + heads):
        rows = r.heads[piece].astype(F32).reshape(heads_width, width)
        for kind in range(3):
            place = 3 * heads + kind if piece == 0 else kind * heads + piece - 1
            r.wide[2, place * HEAD_DIM : (place + 1) * HEAD_DIM] = rows[
                kind * HEAD_DIM : (kind + 1) * HEAD_DIM
            ]
    parts = [
        (r.wide.at[2, pl.ds(part * heads_width, heads_width)], target)
        for part, target in enumerate((r.query, r.key, r.value, r.out))
    ]
    for source, target in parts:
        store = pltpu.make_async_copy(source, target, r.store_sem.at[len(stores)])
        store.start()
        stores.append(store)
    rows = (
        r.second_gain, r.second_shift, r.down_bias, r.first_gain, r.first_shift, r.out_bias, r.up_bias,
    )
    for index, row in enumerate(rows):
        row[...] = r.sums[index]
    r.query_bias[...] = r.sums[7, 0:heads_width]
    r.value_bias[...] = r.sums[7, columns : columns + heads_width]
    for copy in stores:
        copy.wait()


def shards(
    frames,
    cotangent,
    lengths,
    query_weight,
    query_bias,
    key_weight,
    value_weight,
    value_bias,
    out_weight,
    out_bias,
    first_gain,
    first_shift,
    up_weight,
    up_bias,
    down_weight,
    down_bias,
    second_gain,
    second_shift,
):
    seqs, share_rows, width = frames.shape
    rows = up_to(share_rows, 16)
    length = 4 * rows
    heads_width = query_weight.shape[1]
    inner = up_weight.shape[1]
    lanes = up_to(heads_width + 1, 128)
    shape = jax.ShapeDtypeStruct
    count = lax.axis_size("dp")
    ringed = count & (count - 1) == 0 and width % (32 * count) == 0 and count >= 4
    ringed = ringed and heads_width == 3 * HEAD_DIM and heads_width % (8 * count) == 0
    half = width // (2 * count)
    heads_parts = 1 + heads_width // HEAD_DIM
    levels = 2 + count.bit_length() - 1
    full = pltpu.VMEM((seqs, 4, rows, width), BF)
    part = pltpu.VMEM((seqs, rows, width), BF)
    stream = pltpu.VMEM((seqs, rows, width), F32)
    inputs = dict(
        lengths=lengths,
        frames=frames,
        cotangent=cotangent,
        query_weight=query_weight.T,
        query_bias=query_bias,
        key_weight=key_weight.T,
        value_weight=value_weight.T,
        value_bias=value_bias,
        out_weight=out_weight,
        out_bias=out_bias,
        first_gain=first_gain,
        first_shift=first_shift,
        up_weight=up_weight,
        up_bias=up_bias,
        down_weight=down_weight,
        down_bias=down_bias,
        second_gain=second_gain,
        second_shift=second_shift,
    )
    outputs = dict(
        layer_output=shape(frames.shape, BF),
        input_grad=shape(frames.shape, F32),
        sums=shape((8, width), F32),
    )
    if ringed:
        outputs.update(
            feed_sum=shape((2, count, 2, 1, half, width), BF),
            heads_sum=shape((heads_parts, 2, count // 2, 1, heads_width // count, width), BF),
        )
    else:
        outputs.update(
            {name: shape((width, width), F32) for name in ("up_sum", "down_sum", "heads_sum")}
        )
    scratch = dict(
        wide_weight=pltpu.VMEM((3 * lanes, width), BF),
        wide_out=pltpu.VMEM((lanes, width), BF),
        projection_bias=pltpu.VMEM((1, 3 * lanes), F32),
        rows_sum=pltpu.VMEM((8, width), F32),
        full_frames=full,
        first_full=full,
        grad_mixed=full,
        grad_full=full,
        projected=pltpu.VMEM((seqs, length, 3 * lanes), BF),
        context=pltpu.VMEM((seqs, length, lanes), BF),
        log_total=pltpu.VMEM((seqs, 2, 8, 2 * rows), F32),
        first_normed=stream,
        first_inverse=pltpu.VMEM((seqs, rows, 1), F32),
        grad_rows=stream,
        hidden=pltpu.VMEM((seqs, length, inner), F32),
        activated=pltpu.VMEM((seqs, length, inner), BF),
        grad_hidden=pltpu.VMEM((seqs, length, inner), BF),
        grad_context=pltpu.VMEM((length, lanes), BF),
        up_grad=pltpu.VMEM(up_weight.shape, F32),
        down_grad=pltpu.VMEM(down_weight.shape, F32),
        outgoing=pltpu.VMEM((seqs, 2, rows, width), BF),
        keep=pltpu.VMEM((seqs, 2, rows, width), F32),
        near=pltpu.VMEM((seqs, 2, rows, width), BF),
        cross=part,
        landed=part,
        gather_send=pltpu.SemaphoreType.DMA((4, seqs, 3)),
        gather_recv=pltpu.SemaphoreType.DMA((4, seqs, 3)),
        scatter_send=pltpu.SemaphoreType.DMA((4, seqs, 3)),
        scatter_recv=pltpu.SemaphoreType.DMA((4, seqs, 3)),
        out_sem=pltpu.SemaphoreType.DMA((5, seqs)),
        load_sem=pltpu.SemaphoreType.DMA((len(inputs),)),
    )
    scratch.update(
        {name: pltpu.VMEM(item.shape, item.dtype) for name, item in inputs.items() if name != "lengths"}
    )
    given = [name if name == "lengths" else name + "_from" for name in inputs]
    if ringed:
        spots, small = count // 2, heads_width // count
        scratch.update(
            feed_opening=pltpu.VMEM((2, 2, 1, half, width), BF),
            heads_out=pltpu.VMEM((heads_parts, spots, 1, small, width), BF),
            heads_half=pltpu.VMEM((heads_parts, spots, 1, small, width), BF),
            feed_landed=pltpu.VMEM((2, 2, count - 1, 1, half, width), BF),
            heads_quarter=pltpu.VMEM((heads_parts, spots - 1, 1, small, width), BF),
            feed_shared=pltpu.VMEM((2, count, 2, 1, half, width), BF),
            heads_shared=pltpu.VMEM((heads_parts, 2, spots, 1, small, width), BF),
            pair_send=pltpu.SemaphoreType.DMA((heads_parts, 2 * spots)),
            pair_recv=pltpu.SemaphoreType.DMA((heads_parts, 2 * spots)),
            ring_send=pltpu.SemaphoreType.DMA((2,)),
            ring_recv=pltpu.SemaphoreType.DMA((2, 2, 2, count - 1)),
            small_out=pltpu.VMEM((levels, 8, width), F32),
            small_in=pltpu.VMEM((levels, 8, width), F32),
            small_send=pltpu.SemaphoreType.DMA((levels,)),
            small_recv=pltpu.SemaphoreType.DMA((levels,)),
        )
    outs = pl.pallas_call(
        functools.partial(layer, count if ringed else 0, [*given, *outputs, *scratch]),
        out_shape=list(outputs.values()),
        in_specs=[pl.BlockSpec(memory_space=pltpu.SMEM)] + [ANY_SPEC] * (len(inputs) - 1),
        out_specs=[VMEM_SPEC if name == "sums" else ANY_SPEC for name in outputs],
        scratch_shapes=list(scratch.values()),
        compiler_params=pltpu.CompilerParams(
            collective_id=0, has_side_effects=True, vmem_limit_bytes=VMEM_BYTES
        ),
        name="layer",
    )(*inputs.values())
    layer_output, input_grad, sums = outs[:3]
    if not ringed:
        up_grad, down_grad, heads_grad = lax.psum(tuple(outs[3:]), "dp")
        sums = lax.psum(sums, "dp")
        sums = jnp.concatenate([lax.psum(sums[:6], "tensor"), sums[6:]])
        mixed = heads_grad[heads_width:].reshape(-1, 3, HEAD_DIM, width)
        parts = [mixed[:, index].reshape(heads_width, width) for index in range(3)]
        parts.append(heads_grad[:heads_width])
        return (
            layer_output, input_grad, parts[0].T, sums[7, :heads_width], parts[1].T, parts[2].T,
            sums[7, 2 * lanes : 2 * lanes + heads_width], parts[3], sums[5], sums[3], sums[4],
            up_grad, sums[6], down_grad, sums[2], sums[0], sums[1],
        )
    row = shape((width,), F32)
    side_row = shape((heads_width,), F32)
    block = shape((heads_width, width), F32)
    square = shape((width, width), F32)
    results = dict(
        layer_output=shape(frames.shape, BF),
        input_grad=shape(frames.shape, F32),
        query=block,
        query_bias=side_row,
        key=block,
        value=block,
        value_bias=side_row,
        out=block,
        out_bias=row,
        first_gain=row,
        first_shift=row,
        up=square,
        up_bias=row,
        down=square,
        down_bias=row,
        second_gain=row,
        second_shift=row,
    )
    given = ["layer_in", "input_in", "sums", "feed_in", "heads_in"]
    buffers = dict(
        narrow=pltpu.VMEM((2, count, 2, half, width), BF),
        heads=pltpu.VMEM(outs[4].shape, BF),
        wide=pltpu.VMEM((3, width, width), F32),
        plain_sem=pltpu.SemaphoreType.DMA((3,)),
        load_sem=pltpu.SemaphoreType.DMA((2,)),
        store_sem=pltpu.SemaphoreType.DMA((8,)),
        layer_stage=pltpu.VMEM(frames.shape, BF),
        input_stage=pltpu.VMEM(frames.shape, F32),
    )
    final = pl.pallas_call(
        functools.partial(widen, 2 * lanes, [*given, *results, *buffers]),
        out_shape=list(results.values()),
        in_specs=[ANY_SPEC] * 2 + [VMEM_SPEC] + [ANY_SPEC] * 2,
        out_specs=[VMEM_SPEC if len(item.shape) == 1 else ANY_SPEC for item in results.values()],
        scratch_shapes=list(buffers.values()),
        compiler_params=pltpu.CompilerParams(vmem_limit_bytes=VMEM_BYTES),
        name="widen",
    )(layer_output, input_grad, sums, *outs[3:])
    final = dict(zip(results, final))
    for name in ("query", "key", "value"):
        final[name] = final[name].T
    return tuple(final.values())


def solution(mesh):
    return jax.shard_map(
        shards,
        mesh=mesh,
        in_specs=(
            P("dp", "tensor", None),
            P("dp", "tensor", None),
            P("dp"),
            P(None, "tensor"),
            P("tensor"),
            P(None, "tensor"),
            P(None, "tensor"),
            P("tensor"),
            P("tensor", None),
            P(),
            P(),
            P(),
            P(None, "tensor"),
            P("tensor"),
            P("tensor", None),
            P(),
            P(),
            P(),
        ),
        out_specs=(
            P("dp", "tensor", None),
            P("dp", "tensor", None),
            P(None, "tensor"),
            P("tensor"),
            P(None, "tensor"),
            P(None, "tensor"),
            P("tensor"),
            P("tensor", None),
            P(),
            P(),
            P(),
            P(None, "tensor"),
            P("tensor"),
            P("tensor", None),
            P(),
            P(),
            P(),
        ),
        check_vma=False,
    )
```

```python
import functools
import types

import jax
import jax.numpy as jnp
from jax import lax
from jax.experimental import pallas as pl
from jax.experimental.pallas import tpu as pltpu
from jax.sharding import PartitionSpec as P

MESH = pl.DeviceIdType.MESH
HEAD_DIM = 64
EPSILON = 1e-05
ROOT_HALF = 0.7071067811865476
INVERSE_ROOT_TAU = 0.3989422804014327
MASKED = -1e30
VMEM_BYTES = 62 << 20
POLLS = (1, 2, 0, 1, 1, 1, 1, 1)
TAIL = (
    (1, 1), (2, 1), (0, 3), (1, 2), (3, 1), (2, 2), (3, 2), (1, 3), (2, 3), (3, 3),
)
BF = jnp.bfloat16
F32 = jnp.float32


def up_to(size, unit):
    return (size + unit - 1) // unit * unit


def dot(left, right):
    return jnp.dot(left, right, preferred_element_type=F32)


def dot_nt(left, right):
    return lax.dot_general(left, right, (((1,), (1,)), ((), ())), preferred_element_type=F32)


def dot_tn(left, right):
    return lax.dot_general(left, right, (((0,), (0,)), ((), ())), preferred_element_type=F32)


def pad_rows(rows, size):
    extra = size - rows.shape[0]
    if extra == 0:
        return rows
    return jnp.concatenate([rows, jnp.zeros((extra, rows.shape[1]), rows.dtype)], axis=0)


class Group:
    def __init__(self):
        self.dp = lax.axis_index("dp")
        self.own = lax.axis_index("tensor")
        self.y = self.own // 2
        self.core = self.own % 2
        self.mate = self.y * 2 + (1 - self.core)
        self.far = (1 - self.y) * 2 + self.core

    def greet(self, dp_peers):
        barrier = pltpu.get_barrier_semaphore()
        peers = [(self.dp, self.mate), (self.dp, self.far)] + [(peer, self.own) for peer in dp_peers]
        for peer in peers:
            pl.semaphore_signal(barrier, inc=1, device_id=peer, device_id_type=MESH)
        return lambda: pl.semaphore_wait(barrier, len(peers))

    def share(self, turn):
        late = turn // 2
        other = ((turn + 1) // 2) % 2
        ybit = (1 - self.y) * (1 - late) + self.y * late
        core = self.core * (1 - other) + (1 - self.core) * other
        return ybit * 2 + core

    def copy(self, source, target, send, recv, peer):
        return pltpu.make_async_remote_copy(
            src_ref=source,
            dst_ref=target,
            send_sem=send,
            recv_sem=recv,
            device_id=(self.dp, peer),
            device_id_type=MESH,
        )


class Gather:
    def __init__(self, group, full, send, recv, real):
        self.group, self.full, self.send, self.recv = group, full, send, recv
        self.real = pl.ds(0, real)

    def _copy(self, seq, kind):
        group = self.group
        share = group.far if kind == 2 else group.own
        slot = self.full.at[seq, share, self.real] if kind == 0 else self.full.at[seq, share]
        peer = group.far if kind == 0 else group.mate
        return group.copy(slot, slot, self.send.at[seq, kind], self.recv.at[seq, kind], peer)

    def start(self, seq):
        self._copy(seq, 0).start()
        self._copy(seq, 1).start()

    def wait(self, seq, turn):
        @pl.when(turn == 0)
        def _():
            self._copy(seq, 0).wait_recv()
            self._copy(seq, 2).start()

        @pl.when(turn == 1)
        def _():
            self._copy(seq, 2).wait_recv()

        @pl.when(turn == 2)
        def _():
            self._copy(seq, 1).wait_recv()

    def close(self, seq):
        for kind in range(3):
            self._copy(seq, kind).wait_send()


class Scatter:
    def __init__(self, group, buffers, send, recv, real):
        self.group = group
        self.real = pl.ds(0, real)
        self.outgoing, self.keep, self.near, self.cross, self.landed = buffers
        self.send, self.recv = send, recv

    def _near(self, seq, index):
        return self.group.copy(
            self.outgoing.at[seq, index],
            self.near.at[seq, index],
            self.send.at[seq, index],
            self.recv.at[seq, index],
            self.group.mate,
        )

    def _cross(self, seq):
        return self.group.copy(
            self.cross.at[seq, self.real],
            self.landed.at[seq, self.real],
            self.send.at[seq, 2],
            self.recv.at[seq, 2],
            self.group.far,
        )

    def put(self, seq, turn, terms):
        @pl.when((turn == 0) | (turn == 3))
        def _():
            self.keep[seq, turn // 3] = terms

        @pl.when((turn == 1) | (turn == 2))
        def _():
            self.outgoing[seq, turn - 1] = terms.astype(BF)
            self._near(seq, turn - 1).start()

        @pl.when(turn == 2)
        def _():
            self._near(seq, 0).wait_recv()
            total = self.keep[seq, 0] + self.near[seq, 0].astype(F32)
            self.cross[seq] = total.astype(BF)
            self._cross(seq).start()

    def take(self, seq):
        self._near(seq, 1).wait_recv()
        self._cross(seq).wait_recv()
        for index in range(2):
            self._near(seq, index).wait_send()
        self._cross(seq).wait_send()
        return (
            self.keep[seq, 1]
            + self.near[seq, 1].astype(F32)
            + self.landed[seq].astype(F32)
        )


def norm(rows):
    centred = rows - jnp.mean(rows, axis=-1, keepdims=True)
    inverse = lax.rsqrt(jnp.mean(centred * centred, axis=-1, keepdims=True) + EPSILON)
    return centred * inverse, inverse


def norm_back(grad, normed, inverse, gain):
    scaled = grad * gain
    return inverse * (
        scaled
        - jnp.mean(scaled, axis=-1, keepdims=True)
        - normed * jnp.mean(scaled * normed, axis=-1, keepdims=True)
    )


def sum_rows(rows):
    return jnp.sum(rows, axis=0, keepdims=True)


def lane_index(rows, lanes):
    return lax.broadcasted_iota(jnp.int32, (rows, lanes), 1)


class Ring:
    def __init__(self, group, count, owns, opening, landed, shared, sends, recvs, first):
        self.group, self.count, self.steps = group, count, count - 1
        self.owns, self.opening, self.landed, self.shared = owns, opening, landed, shared
        self.add_send, self.share_send = sends
        self.add_recv, self.share_recv = recvs
        self.half = owns[0].shape[0] // (2 * count)
        self.first, self.rows = first, landed.shape[3]
        self.place, self.right, self.left = ring_peers(group.dp, count)

    def _own(self, which, way, step):
        shift = self.count - 1 - step if way == 0 else 1 + step
        chunk = (self.place + shift) % self.count
        start = pl.multiple_of((2 * chunk + way) * self.half + self.first, 16)
        return self.owns[which][pl.ds(start, self.rows)]

    def _copy(self, source, target, send, recv, way):
        return pltpu.make_async_remote_copy(
            src_ref=source,
            dst_ref=target,
            send_sem=send,
            recv_sem=recv,
            device_id=(self.right if way == 0 else self.left, self.group.own),
            device_id_type=MESH,
        )

    def _add(self, way, step, source=None):
        target = self.landed.at[way, step]
        return self._copy(
            target if source is None else source, target, self.add_send, self.add_recv.at[way, step], way
        )

    def _share(self, way, step):
        shift = self.count - step if way == 0 else step
        slot = self.shared.at[(self.place + shift) % self.count, way]
        return self._copy(slot, slot, self.share_send, self.share_recv.at[way, step], way)

    def open(self):
        for way in range(2):
            for which in range(len(self.owns)):
                self.opening[way, which] = self._own(which, way, 0).astype(BF)
            self._add(way, 0, self.opening.at[way]).start()

    def advance(self, step):
        last = self.steps - 1
        for way in range(2):
            if step < self.steps:
                self._add(way, step).wait_recv()
                target = self.landed.at[way, step] if step < last else self.shared.at[self.place, way]
                for which in range(len(self.owns)):
                    total = self.landed[way, step, which].astype(F32) + self._own(which, way, step + 1)
                    target[which] = total.astype(BF)
                if step < last:
                    self._add(way, step + 1, target).start()
                else:
                    self._share(way, 0).start()
            else:
                turn = step - self.steps
                self._share(way, turn).wait_recv()
                if turn < last:
                    self._share(way, turn + 1).start()

    def wait_sends(self, landed):
        for send in (self.add_send, self.share_send):
            self._copy(landed, landed, send, self.add_recv.at[0, 0], 0).wait_send()


class Pairwise:
    def __init__(self, group, count, terms, outgoing, half, quarter, shared, send, recv):
        self.group, self.spots = group, count // 2
        self.terms, self.outgoing, self.half, self.quarter = terms, outgoing, half, quarter
        self.shared, self.send, self.recv = shared, send, recv
        self.arrays = half.shape[1]
        self.spot, self.side = group.dp // 2, group.dp % 2

    def _copy(self, source, target, index, spot, side):
        return pltpu.make_async_remote_copy(
            src_ref=source,
            dst_ref=target,
            send_sem=self.send.at[index],
            recv_sem=self.recv.at[index],
            device_id=(spot * 2 + side, self.group.own),
            device_id_type=MESH,
        )

    def _out(self):
        return self._copy(self.outgoing, self.half, 0, self.spot, 1 - self.side)

    def _add(self, offset):
        spot = (self.spot + offset) % self.spots
        return self._copy(
            self.half.at[spot], self.quarter.at[offset - 1], offset, spot, self.side
        )

    def _share(self, offset):
        spot = (self.spot + offset) % self.spots
        slot = self.shared.at[self.side, self.spot]
        return self._copy(slot, slot, self.spots - 1 + offset, spot, self.side)

    def _back(self):
        slot = self.shared.at[self.side]
        return self._copy(slot, slot, 2 * self.spots - 1, self.spot, 1 - self.side)

    def act(self, phase):
        others = range(1, self.spots)
        if phase == 0:
            for spot in range(self.spots):
                for which in range(self.arrays):
                    self.outgoing[spot, which] = self.terms(which, 1 - self.side, spot).astype(BF)
            self._out().start()
        elif phase == 1:
            self._out().wait_recv()
            for offset in others:
                spot = (self.spot + offset) % self.spots
                for which in range(self.arrays):
                    total = self.half[spot, which].astype(F32) + self.terms(which, self.side, spot)
                    self.half[spot, which] = total.astype(BF)
                self._add(offset).start()
        elif phase == 2:
            for offset in others:
                self._add(offset).wait_recv()
            for which in range(self.arrays):
                total = self.half[self.spot, which].astype(F32) + self.terms(
                    which, self.side, self.spot
                )
                for offset in others:
                    total = total + self.quarter[offset - 1, which].astype(F32)
                self.shared[self.side, self.spot, which] = total.astype(BF)
            for offset in others:
                self._share(offset).start()
        elif phase == 3:
            for offset in others:
                self._share(offset).wait_recv()
            self._back().start()
        else:
            self._back().wait_recv()
            self._out().wait_send()
            self._back().wait_send()
            for offset in others:
                self._add(offset).wait_send()
                self._share(offset).wait_send()


def ring_peers(index, count):
    odd = index % 2
    place = (1 - odd) * (index // 2) + odd * (count - 1 - index // 2)

    def at(spot):
        late = spot // (count // 2)
        return (1 - late) * 2 * spot + late * (2 * (count - 1 - spot) + 1)

    return place, at((place + 1) % count), at((place + count - 1) % count)


def halving_peers(index, count):
    peers = []
    bit = 1
    while bit < count:
        peers.append(index + bit * (1 - 2 * ((index // bit) % 2)))
        bit *= 2
    return peers


class Totals:
    def __init__(self, group, peers, outgoing, arriving, send, recv, shared):
        self.group, self.shared = group, shared
        self.outgoing, self.arriving, self.send, self.recv = outgoing, arriving, send, recv
        own = group.own
        self.peers = [(group.dp, group.mate), (group.dp, group.far)] + [(peer, own) for peer in peers]

    def _copy(self, level):
        return pltpu.make_async_remote_copy(
            src_ref=self.outgoing.at[level],
            dst_ref=self.arriving.at[level],
            send_sem=self.send.at[level],
            recv_sem=self.recv.at[level],
            device_id=self.peers[level],
            device_id_type=MESH,
        )

    def begin(self, level, rows):
        self.outgoing[level] = rows
        self._copy(level).start()

    def end(self, level):
        self._copy(level).wait()
        other = self.arriving[level]
        if level < 2:
            place = lax.broadcasted_iota(jnp.int32, other.shape, 0)
            other = jnp.where(place < self.shared, other, 0.0)
        return self.outgoing[level] + other


def layer(count, names, *refs):
    r = types.SimpleNamespace(**dict(zip(names, refs)))
    loads = {
        name[:-5]: pltpu.make_async_copy(ref, getattr(r, name[:-5]), r.load_sem.at[index])
        for index, (name, ref) in enumerate(zip(names, refs))
        if name.endswith("_from")
    }

    def loaded(*wanted):
        for name in wanted or list(loads):
            loads.pop(name).wait()

    seqs, share_rows, width = r.frames.shape
    rows = r.full_frames.shape[2]
    length = 4 * rows
    heads_width = r.query_weight.shape[0]
    lanes = r.wide_weight.shape[0] // 3
    heads = heads_width // HEAD_DIM
    group = Group()
    pairs = []
    ring_sides = []
    if count:
        pairs = halving_peers(group.dp, count)
        ring_sides = list(ring_peers(group.dp, count)[1:])
        ring_sides += [
            (group.dp + 2 * offset) % count for offset in range(1, count // 2)
        ]
    tail = pl.ds(share_rows, rows - share_rows)
    if rows > share_rows:
        for full in (r.full_frames, r.first_full, r.grad_mixed, r.grad_full):
            full[:, :, tail] = jnp.zeros_like(full[:, :, tail])
        r.landed[:, tail] = jnp.zeros_like(r.landed[:, tail])
    met = group.greet(ring_sides + pairs)

    for load in loads.values():
        load.start()
    buffers = (r.outgoing, r.keep, r.near, r.cross, r.landed)
    gathers = [
        Gather(group, full, r.gather_send.at[index], r.gather_recv.at[index], share_rows)
        for index, full in enumerate((r.full_frames, r.first_full, r.grad_mixed, r.grad_full))
    ]
    scatters = [
        Scatter(group, buffers, r.scatter_send.at[index], r.scatter_recv.at[index], share_rows)
        for index in range(4)
    ]
    grad_total = r.hidden.at[0]
    heads_grad = r.hidden.at[1, pl.ds(0, 4 * heads_width)]

    def each(stage):
        def body(seq, carry):
            stage(seq)
            return carry

        lax.fori_loop(0, seqs, body, 0)

    def turns(step):
        def body(turn, carry):
            step(turn)
            return carry

        lax.fori_loop(0, 4, body, 0)

    def at_share(share):
        return pl.ds(pl.multiple_of(share * rows, 16), rows)

    def place_frames(seq):
        r.full_frames[seq, group.own] = pad_rows(r.frames[seq].astype(F32), rows).astype(BF)

    loaded("frames")
    each(place_frames)
    met()
    each(gathers[0].start)
    loaded("query_weight", "key_weight", "value_weight", "query_bias", "value_bias", "out_weight")
    r.wide_weight[...] = jnp.zeros_like(r.wide_weight)
    for index, weight in enumerate((r.query_weight, r.key_weight, r.value_weight)):
        r.wide_weight[index * lanes : index * lanes + heads_width] = weight[...]
    r.wide_out[...] = jnp.zeros_like(r.wide_out)
    r.wide_out[:heads_width] = r.out_weight[...]
    r.projection_bias[...] = jnp.where(
        lane_index(1, 3 * lanes) == heads_width, HEAD_DIM**0.5, 0.0
    )
    r.projection_bias[:, :heads_width] = r.query_bias[...].reshape(1, heads_width)
    r.projection_bias[:, 2 * lanes : 2 * lanes + heads_width] = r.value_bias[...].reshape(1, heads_width)
    r.rows_sum[...] = jnp.zeros_like(r.rows_sum)

    def attention(seq):
        def project(step):
            turn = (1 - step // 2) * (3 - step) + (step // 2) * (step - 2)
            gathers[0].wait(seq, turn)
            share = group.share(turn)
            result = dot_nt(r.full_frames[seq, share], r.wide_weight[...]) + r.projection_bias[...]
            place = lax.broadcasted_iota(jnp.int32, (rows, lanes), 0)
            dead = (place >= share_rows) | (place + share * share_rows >= r.lengths[seq])
            flag = jnp.where(dead & (lane_index(rows, lanes) == heads_width), MASKED, 0.0)
            r.projected[seq, at_share(share), 0:lanes] = (
                result[:, :lanes].astype(BF) * HEAD_DIM ** (-0.5)
            ).astype(BF)
            r.projected[seq, at_share(share), lanes : 2 * lanes] = (
                result[:, lanes : 2 * lanes] + flag
            ).astype(BF)
            r.projected[seq, at_share(share), 2 * lanes : 3 * lanes] = result[:, 2 * lanes :].astype(BF)

        turns(project)

        def attend(block, carry):
            chip = (1 - group.y) * (1 - block) + group.y * block
            span = pl.ds(pl.multiple_of(chip * 2 * rows, 16), 2 * rows)
            queries = r.projected[seq, span, 0:lanes]
            lane = lane_index(2 * rows, lanes)
            mixed = jnp.zeros((2 * rows, lanes), F32)
            for head in range(heads):
                inside = lane // HEAD_DIM == head
                picked = jnp.where(inside | (lane == heads_width), queries, jnp.zeros_like(queries))
                scores = dot_nt(picked, r.projected[seq, :, lanes : 2 * lanes])
                top = jnp.max(scores, axis=-1, keepdims=True)
                exponent = jnp.exp(scores - top)
                weight = jnp.sum(exponent, axis=-1, keepdims=True)
                r.log_total[seq, chip, head : head + 1] = jnp.transpose(top + jnp.log(weight))
                part = dot(exponent.astype(BF), r.projected[seq, :, 2 * lanes : 3 * lanes])
                mixed = jnp.where(inside, part * (1.0 / weight), mixed)
            r.context[seq, span] = mixed.astype(BF)
            for half in range(2):
                turn = 2 * block + half
                mixed = r.context[seq, at_share(group.share(turn))]
                scatters[0].put(seq, turn, dot(mixed, r.wide_out[...]))
            return carry

        lax.fori_loop(0, 2, attend, 0)

    each(attention)

    def first_norm(seq):
        attended = scatters[0].take(seq)
        normed, inverse = norm(r.full_frames[seq, group.own].astype(F32) + attended + out_bias)
        r.first_normed[seq] = normed
        r.first_inverse[seq] = inverse
        r.first_full[seq, group.own] = (normed * first_gain + first_shift).astype(BF)
        gathers[1].start(seq)

    loaded()
    out_bias, first_gain, first_shift, down_bias, second_gain, second_shift, up_bias = (
        row[...].reshape(1, row.shape[0])
        for row in (
            r.out_bias, r.first_gain, r.first_shift, r.down_bias, r.second_gain, r.second_shift, r.up_bias,
        )
    )
    each(first_norm)

    def feed(seq):
        def step(turn):
            gathers[1].wait(seq, turn)
            share = group.share(turn)
            inner = dot(r.first_full[seq, share], r.up_weight[...]) + up_bias
            r.hidden[seq, at_share(share)] = inner
            active = (0.5 * inner * (1.0 + lax.erf(inner * ROOT_HALF))).astype(BF)
            r.activated[seq, at_share(share)] = active
            scatters[1].put(seq, turn, dot(active, r.down_weight[...]))

        turns(step)

    each(feed)

    def second_norm(seq):
        mixed = scatters[1].take(seq)
        first = r.first_normed[seq] * first_gain + first_shift
        normed, inverse = norm(first + mixed + down_bias)
        place = lax.broadcasted_iota(jnp.int32, (rows, width), 0)
        live = (place < share_rows) & (place + group.own * share_rows < r.lengths[seq])
        grad = jnp.where(live, pad_rows(r.cotangent[seq], rows), 0.0)
        back = norm_back(grad, normed, inverse, second_gain)
        r.grad_mixed[seq, group.own] = back.astype(BF)
        gathers[2].start(seq)
        r.grad_rows[seq] = back
        r.frames[seq] = (normed * second_gain + second_shift)[:share_rows].astype(BF)
        r.rows_sum[0:1] += sum_rows(grad * normed)
        r.rows_sum[1:2] += sum_rows(grad)
        r.rows_sum[2:3] += sum_rows(back)

    each(second_norm)

    def feed_back(seq, waited):
        def step(turn):
            if not waited:
                gathers[2].wait(seq, turn)
            share = group.share(turn)
            grad_active = dot_nt(r.grad_mixed[seq, share], r.down_weight[...])
            inner = r.hidden[seq, at_share(share)]
            slope = (
                0.5 * (1.0 + lax.erf(inner * ROOT_HALF))
                + inner * jnp.exp(-0.5 * inner * inner) * INVERSE_ROOT_TAU
            )
            grad = (grad_active * slope).astype(BF)
            r.grad_hidden[seq, at_share(share)] = grad
            r.rows_sum[6:7] += sum_rows(grad.astype(F32))
            scatters[2].put(seq, turn, dot_nt(grad, r.up_weight[...]))

        turns(step)


    def down_weights(seq):
        down = dot_tn(r.activated[seq], r.grad_mixed[seq].reshape(length, width))
        r.down_grad[...] = down if seq == 0 else r.down_grad[...] + down

    def up_weights(seq):
        up = dot_tn(r.first_full[seq].reshape(length, width), r.grad_hidden[seq])
        r.up_grad[...] = up if seq == 0 else r.up_grad[...] + up

    def first_back(seq):
        grad = r.grad_rows[seq] + scatters[2].take(seq)
        normed = r.first_normed[seq]
        back = norm_back(grad, normed, r.first_inverse[seq], first_gain)
        r.grad_full[seq, group.own] = back.astype(BF)
        gathers[3].start(seq)
        r.grad_rows[seq] = back
        r.rows_sum[3:4] += sum_rows(grad * normed)
        r.rows_sum[4:5] += sum_rows(grad)
        r.rows_sum[5:6] += sum_rows(back)

    queue = []

    def poll(times=1):
        for _ in range(times):
            if queue:
                queue.pop(0)()

    def act(part, phase):
        if count:
            pieces[part].act(phase)

    if count:
        rings = [
            Ring(
                group,
                count,
                (own,),
                r.feed_opening.at[part],
                r.feed_landed.at[part],
                r.feed_shared.at[part],
                (r.ring_send.at[0], r.ring_send.at[1]),
                (r.ring_recv.at[part, 0], r.ring_recv.at[part, 1]),
                0,
            )
            for part, own in enumerate((r.up_grad, r.down_grad))
        ]

        def heads_terms(first, size, which, side, spot):
            start = first + (side * (count // 2) + spot) * size
            return heads_grad[pl.ds(pl.multiple_of(start, 8), size)]

        pieces = [
            Pairwise(
                group,
                count,
                functools.partial(heads_terms, part * heads_width, r.heads_half.shape[3]),
                r.heads_out.at[part],
                r.heads_half.at[part],
                r.heads_quarter.at[part],
                r.heads_shared.at[part],
                r.pair_send.at[part],
                r.pair_recv.at[part],
            )
            for part in range(1 + heads)
        ]

    def join(part):
        if count:
            rings[part].open()
            waiting = list(queue)
            queue.clear()
            for step in range(2 * (count - 1)):
                queue.extend(waiting[step : step + 1])
                queue.append(functools.partial(rings[part].advance, step))

    for seq in range(seqs):
        if seq == seqs - 1:
            for turn in range(3):
                gathers[2].wait(seq, turn)
            down_weights(seq)
            join(1)
            feed_back(seq, True)
        else:
            feed_back(seq, False)
            down_weights(seq)
    poll(POLLS[7])
    for seq in range(seqs):
        up_weights(seq)
    join(0)
    for seq in range(seqs):
        poll(POLLS[0])
        first_back(seq)
    poll(POLLS[0])
    if count:
        totals = Totals(
            group, pairs, r.small_out, r.small_in, r.small_send, r.small_recv, 6
        )
        totals.begin(0, r.rows_sum[...])
    def output_copy(seq):
        return pltpu.make_async_copy(r.frames.at[seq], r.layer_output.at[seq], r.out_sem.at[3, seq])

    def input_copy(seq):
        return pltpu.make_async_copy(r.cotangent.at[seq], r.input_grad.at[seq], r.out_sem.at[4, seq])

    def store_input(seq):
        r.cotangent[seq] = (scatters[3].take(seq) + r.grad_rows[seq])[:share_rows]
        input_copy(seq).start()

    for seq in range(seqs):
        output_copy(seq).start()

        def step(turn):
            gathers[3].wait(seq, turn)
            share = group.share(turn)
            r.grad_context[at_share(share)] = dot_nt(r.grad_full[seq, share], r.wide_out[...]).astype(BF)

        turns(step)
        part = dot_tn(r.context[seq], r.grad_full[seq].reshape(length, width))[:heads_width]
        if seq == 0:
            heads_grad[:heads_width] = part
        else:
            heads_grad[:heads_width] += part
        if seq == seqs - 1:
            act(0, 0)
        poll(POLLS[1])
        grad_total[...] = jnp.zeros_like(grad_total)
        keys = r.projected[seq, :, lanes : 2 * lanes]
        lane = lane_index(length, lanes)
        key_columns = jnp.transpose(keys.astype(F32) * HEAD_DIM ** (-0.5)).astype(BF)
        for head in range(heads):
            inside = lane // HEAD_DIM == head
            queries = r.projected[seq, :, 0:lanes]
            picked = jnp.where(inside | (lane == heads_width), queries, jnp.zeros_like(queries))
            row = jnp.concatenate(
                [r.log_total[seq, chip, head : head + 1] for chip in range(2)], axis=1
            )
            weights = jnp.exp(dot_nt(keys, picked) - row)
            grads = r.grad_context[...]
            part = dot(weights.astype(BF), grads)
            span = slice(2 * lanes, 3 * lanes)
            grad_total[:, span] = jnp.where(inside, part, grad_total[:, span])
            poll(POLLS[2])
            slopes = weights * dot_nt(
                r.projected[seq, :, 2 * lanes : 3 * lanes],
                jnp.where(inside, grads, jnp.zeros_like(grads)),
            )
            slopes = (slopes - weights * jnp.sum(slopes, axis=0, keepdims=True)).astype(BF)
            part = dot(slopes, queries)
            span = slice(lanes, 2 * lanes)
            grad_total[:, span] = jnp.where(inside, part, grad_total[:, span])
            span = slice(head * HEAD_DIM, (head + 1) * HEAD_DIM)
            grad_total[:, span] = jnp.transpose(dot(key_columns[span], slopes))
            block = slice((1 + head) * heads_width, (2 + head) * heads_width)
            columns = jnp.concatenate(
                [
                    grad_total[:, index * lanes + head * HEAD_DIM : index * lanes + (head + 1) * HEAD_DIM]
                    for index in range(3)
                ],
                axis=1,
            ).astype(BF)
            part = dot_tn(columns, r.full_frames[seq].reshape(length, width))
            if seq == 0:
                heads_grad[block] = part
            else:
                heads_grad[block] += part
            if seq == seqs - 1:
                act(1 + head, 0)
                if head:
                    act(0, head)
            poll(POLLS[3])

        def finish(turn):
            share = group.share(turn)
            grads = grad_total[at_share(share)].astype(BF)
            r.rows_sum[7:8] += sum_rows(grads.astype(F32))
            scatters[3].put(seq, turn, dot(grads, r.wide_weight[...]))

        turns(finish)
        poll(POLLS[4])
        poll(POLLS[5])
        if seq == 0:
            if count:
                totals.begin(1, totals.end(0))
        else:
            store_input(seq - 1)

    if count:
        place = lax.broadcasted_iota(jnp.int32, r.rows_sum.shape, 0)
        totals.begin(2, jnp.where(place == 7, r.rows_sum[...], totals.end(1)))
        copies = [pltpu.make_async_copy(r.feed_shared, r.feed_sum, r.out_sem.at[0, 0])] + [
            pltpu.make_async_copy(
                r.heads_shared.at[part], r.heads_sum.at[part], r.piece_sem.at[part]
            )
            for part in range(1 + heads)
        ]
        level = 2
        last = len(pairs) + 1
        sent = []
        for at, (part, phase) in enumerate(TAIL):
            pieces[part].act(phase)
            poll(POLLS[6])
            if not queue and not sent:
                copies[0].start()
                sent.append(1)
            if at == 1:
                store_input(seqs - 1)
            if at % 2 == 1 and level <= last:
                rows_total = totals.end(level)
                level += 1
                if level <= last:
                    totals.begin(level, rows_total)
                else:
                    r.sums[...] = rows_total
        poll(len(queue))
        if not sent:
            copies[0].start()
        for index, piece in enumerate(pieces):
            piece.act(4)
            copies[1 + index].start()
        rings[0].wait_sends(r.feed_landed)
    else:
        store_input(seqs - 1)
        r.sums[...] = r.rows_sum[...]
        copies = [
            pltpu.make_async_copy(own, out, r.out_sem.at[index, 0])
            for index, (own, out) in enumerate(
                ((r.up_grad, r.up_sum), (r.down_grad, r.down_sum), (heads_grad, r.heads_sum))
            )
        ]
        for copy in copies:
            copy.start()
    for seq in range(seqs):
        for gather in gathers:
            gather.close(seq)
        output_copy(seq).wait()
        input_copy(seq).wait()
    for copy in copies:
        copy.wait()


VMEM_SPEC = pl.BlockSpec(memory_space=pltpu.VMEM)
ANY_SPEC = pl.BlockSpec(memory_space=pl.ANY)


def widen(columns, refs, *rest):
    r = types.SimpleNamespace(**dict(zip(refs, rest)))
    heads_width = r.query_bias.shape[0]
    width = r.up.shape[1]
    plain = [
        (r.layer_in, r.layer_stage, r.layer_output),
        (r.input_in, r.input_stage, r.input_grad),
    ]
    plain_loads = [
        pltpu.make_async_copy(source, stage, r.plain_sem.at[index])
        for index, (source, stage, _) in enumerate(plain)
    ]
    loads = [
        pltpu.make_async_copy(r.feed_in.at[index, :, :, 0], r.narrow.at[index], r.load_sem.at[index])
        for index in range(2)
    ]
    heads_load = pltpu.make_async_copy(r.heads_in, r.heads, r.plain_sem.at[2])
    for copy in plain_loads + loads + [heads_load]:
        copy.start()
    stores = []
    for load, (_, stage, target) in zip(plain_loads, plain):
        load.wait()
        store = pltpu.make_async_copy(stage, target, r.store_sem.at[len(stores)])
        store.start()
        stores.append(store)
    for index, load in enumerate(loads):
        load.wait()
        r.wide[index] = r.narrow[index].astype(F32).reshape(width, width)
        store = pltpu.make_async_copy(r.wide.at[index], (r.up, r.down)[index], r.store_sem.at[len(stores)])
        store.start()
        stores.append(store)
    heads_load.wait()
    heads = heads_width // HEAD_DIM
    for piece in range(1 + heads):
        rows = r.heads[piece].astype(F32).reshape(heads_width, width)
        for kind in range(3):
            place = 3 * heads + kind if piece == 0 else kind * heads + piece - 1
            r.wide[2, place * HEAD_DIM : (place + 1) * HEAD_DIM] = rows[
                kind * HEAD_DIM : (kind + 1) * HEAD_DIM
            ]
    parts = [
        (r.wide.at[2, pl.ds(part * heads_width, heads_width)], target)
        for part, target in enumerate((r.query, r.key, r.value, r.out))
    ]
    for source, target in parts:
        store = pltpu.make_async_copy(source, target, r.store_sem.at[len(stores)])
        store.start()
        stores.append(store)
    rows = (
        r.second_gain, r.second_shift, r.down_bias, r.first_gain, r.first_shift, r.out_bias, r.up_bias,
    )
    for index, row in enumerate(rows):
        row[...] = r.sums[index]
    r.query_bias[...] = r.sums[7, 0:heads_width]
    r.value_bias[...] = r.sums[7, columns : columns + heads_width]
    for copy in stores:
        copy.wait()


def shards(
    frames,
    cotangent,
    lengths,
    query_weight,
    query_bias,
    key_weight,
    value_weight,
    value_bias,
    out_weight,
    out_bias,
    first_gain,
    first_shift,
    up_weight,
    up_bias,
    down_weight,
    down_bias,
    second_gain,
    second_shift,
):
    seqs, share_rows, width = frames.shape
    rows = up_to(share_rows, 16)
    length = 4 * rows
    heads_width = query_weight.shape[1]
    inner = up_weight.shape[1]
    lanes = up_to(heads_width + 1, 128)
    shape = jax.ShapeDtypeStruct
    count = lax.axis_size("dp")
    ringed = count & (count - 1) == 0 and width % (32 * count) == 0 and count >= 4
    ringed = ringed and heads_width == 3 * HEAD_DIM and heads_width % (8 * count) == 0
    half = width // (2 * count)
    heads_parts = 1 + heads_width // HEAD_DIM
    levels = 2 + count.bit_length() - 1
    full = pltpu.VMEM((seqs, 4, rows, width), BF)
    part = pltpu.VMEM((seqs, rows, width), BF)
    stream = pltpu.VMEM((seqs, rows, width), F32)
    inputs = dict(
        lengths=lengths,
        frames=frames,
        cotangent=cotangent,
        query_weight=query_weight.T,
        query_bias=query_bias,
        key_weight=key_weight.T,
        value_weight=value_weight.T,
        value_bias=value_bias,
        out_weight=out_weight,
        out_bias=out_bias,
        first_gain=first_gain,
        first_shift=first_shift,
        up_weight=up_weight,
        up_bias=up_bias,
        down_weight=down_weight,
        down_bias=down_bias,
        second_gain=second_gain,
        second_shift=second_shift,
    )
    outputs = dict(
        layer_output=shape(frames.shape, BF),
        input_grad=shape(frames.shape, F32),
        sums=shape((8, width), F32),
    )
    if ringed:
        outputs.update(
            feed_sum=shape((2, count, 2, 1, half, width), BF),
            heads_sum=shape((heads_parts, 2, count // 2, 1, heads_width // count, width), BF),
        )
    else:
        outputs.update(
            {name: shape((width, width), F32) for name in ("up_sum", "down_sum", "heads_sum")}
        )
    scratch = dict(
        wide_weight=pltpu.VMEM((3 * lanes, width), BF),
        wide_out=pltpu.VMEM((lanes, width), BF),
        projection_bias=pltpu.VMEM((1, 3 * lanes), F32),
        rows_sum=pltpu.VMEM((8, width), F32),
        full_frames=full,
        first_full=full,
        grad_mixed=full,
        grad_full=full,
        projected=pltpu.VMEM((seqs, length, 3 * lanes), BF),
        context=pltpu.VMEM((seqs, length, lanes), BF),
        log_total=pltpu.VMEM((seqs, 2, 8, 2 * rows), F32),
        first_normed=stream,
        first_inverse=pltpu.VMEM((seqs, rows, 1), F32),
        grad_rows=stream,
        hidden=pltpu.VMEM((seqs, length, inner), F32),
        activated=pltpu.VMEM((seqs, length, inner), BF),
        grad_hidden=pltpu.VMEM((seqs, length, inner), BF),
        grad_context=pltpu.VMEM((length, lanes), BF),
        up_grad=pltpu.VMEM(up_weight.shape, F32),
        down_grad=pltpu.VMEM(down_weight.shape, F32),
        outgoing=pltpu.VMEM((seqs, 2, rows, width), BF),
        keep=pltpu.VMEM((seqs, 2, rows, width), F32),
        near=pltpu.VMEM((seqs, 2, rows, width), BF),
        cross=part,
        landed=part,
        gather_send=pltpu.SemaphoreType.DMA((4, seqs, 3)),
        gather_recv=pltpu.SemaphoreType.DMA((4, seqs, 3)),
        scatter_send=pltpu.SemaphoreType.DMA((4, seqs, 3)),
        scatter_recv=pltpu.SemaphoreType.DMA((4, seqs, 3)),
        out_sem=pltpu.SemaphoreType.DMA((5, seqs)),
        load_sem=pltpu.SemaphoreType.DMA((len(inputs),)),
    )
    scratch.update(
        {name: pltpu.VMEM(item.shape, item.dtype) for name, item in inputs.items() if name != "lengths"}
    )
    given = [name if name == "lengths" else name + "_from" for name in inputs]
    if ringed:
        spots, small = count // 2, heads_width // count
        scratch.update(
            feed_opening=pltpu.VMEM((2, 2, 1, half, width), BF),
            heads_out=pltpu.VMEM((heads_parts, spots, 1, small, width), BF),
            heads_half=pltpu.VMEM((heads_parts, spots, 1, small, width), BF),
            feed_landed=pltpu.VMEM((2, 2, count - 1, 1, half, width), BF),
            heads_quarter=pltpu.VMEM((heads_parts, spots - 1, 1, small, width), BF),
            feed_shared=pltpu.VMEM((2, count, 2, 1, half, width), BF),
            heads_shared=pltpu.VMEM((heads_parts, 2, spots, 1, small, width), BF),
            pair_send=pltpu.SemaphoreType.DMA((heads_parts, 2 * spots)),
            piece_sem=pltpu.SemaphoreType.DMA((heads_parts,)),
            pair_recv=pltpu.SemaphoreType.DMA((heads_parts, 2 * spots)),
            ring_send=pltpu.SemaphoreType.DMA((2,)),
            ring_recv=pltpu.SemaphoreType.DMA((2, 2, 2, count - 1)),
            small_out=pltpu.VMEM((levels, 8, width), F32),
            small_in=pltpu.VMEM((levels, 8, width), F32),
            small_send=pltpu.SemaphoreType.DMA((levels,)),
            small_recv=pltpu.SemaphoreType.DMA((levels,)),
        )
    outs = pl.pallas_call(
        functools.partial(layer, count if ringed else 0, [*given, *outputs, *scratch]),
        out_shape=list(outputs.values()),
        in_specs=[pl.BlockSpec(memory_space=pltpu.SMEM)] + [ANY_SPEC] * (len(inputs) - 1),
        out_specs=[VMEM_SPEC if name == "sums" else ANY_SPEC for name in outputs],
        scratch_shapes=list(scratch.values()),
        compiler_params=pltpu.CompilerParams(
            collective_id=0, has_side_effects=True, vmem_limit_bytes=VMEM_BYTES
        ),
        name="layer",
    )(*inputs.values())
    layer_output, input_grad, sums = outs[:3]
    if not ringed:
        up_grad, down_grad, heads_grad = lax.psum(tuple(outs[3:]), "dp")
        sums = lax.psum(sums, "dp")
        sums = jnp.concatenate([lax.psum(sums[:6], "tensor"), sums[6:]])
        mixed = heads_grad[heads_width:].reshape(-1, 3, HEAD_DIM, width)
        parts = [mixed[:, index].reshape(heads_width, width) for index in range(3)]
        parts.append(heads_grad[:heads_width])
        return (
            layer_output, input_grad, parts[0].T, sums[7, :heads_width], parts[1].T, parts[2].T,
            sums[7, 2 * lanes : 2 * lanes + heads_width], parts[3], sums[5], sums[3], sums[4],
            up_grad, sums[6], down_grad, sums[2], sums[0], sums[1],
        )
    row = shape((width,), F32)
    side_row = shape((heads_width,), F32)
    block = shape((heads_width, width), F32)
    square = shape((width, width), F32)
    results = dict(
        layer_output=shape(frames.shape, BF),
        input_grad=shape(frames.shape, F32),
        query=block,
        query_bias=side_row,
        key=block,
        value=block,
        value_bias=side_row,
        out=block,
        out_bias=row,
        first_gain=row,
        first_shift=row,
        up=square,
        up_bias=row,
        down=square,
        down_bias=row,
        second_gain=row,
        second_shift=row,
    )
    given = ["layer_in", "input_in", "sums", "feed_in", "heads_in"]
    buffers = dict(
        narrow=pltpu.VMEM((2, count, 2, half, width), BF),
        heads=pltpu.VMEM(outs[4].shape, BF),
        wide=pltpu.VMEM((3, width, width), F32),
        plain_sem=pltpu.SemaphoreType.DMA((3,)),
        load_sem=pltpu.SemaphoreType.DMA((2,)),
        store_sem=pltpu.SemaphoreType.DMA((8,)),
        layer_stage=pltpu.VMEM(frames.shape, BF),
        input_stage=pltpu.VMEM(frames.shape, F32),
    )
    final = pl.pallas_call(
        functools.partial(widen, 2 * lanes, [*given, *results, *buffers]),
        out_shape=list(results.values()),
        in_specs=[ANY_SPEC] * 2 + [VMEM_SPEC] + [ANY_SPEC] * 2,
        out_specs=[VMEM_SPEC if len(item.shape) == 1 else ANY_SPEC for item in results.values()],
        scratch_shapes=list(buffers.values()),
        compiler_params=pltpu.CompilerParams(vmem_limit_bytes=VMEM_BYTES),
        name="widen",
    )(layer_output, input_grad, sums, *outs[3:])
    final = dict(zip(results, final))
    for name in ("query", "key", "value"):
        final[name] = final[name].T
    return tuple(final.values())


def solution(mesh):
    return jax.shard_map(
        shards,
        mesh=mesh,
        in_specs=(
            P("dp", "tensor", None),
            P("dp", "tensor", None),
            P("dp"),
            P(None, "tensor"),
            P("tensor"),
            P(None, "tensor"),
            P(None, "tensor"),
            P("tensor"),
            P("tensor", None),
            P(),
            P(),
            P(),
            P(None, "tensor"),
            P("tensor"),
            P("tensor", None),
            P(),
            P(),
            P(),
        ),
        out_specs=(
            P("dp", "tensor", None),
            P("dp", "tensor", None),
            P(None, "tensor"),
            P("tensor"),
            P(None, "tensor"),
            P(None, "tensor"),
            P("tensor"),
            P("tensor", None),
            P(),
            P(),
            P(),
            P(None, "tensor"),
            P("tensor"),
            P("tensor", None),
            P(),
            P(),
            P(),
        ),
        check_vma=False,
    )
```
